32 devices in a mesh: groups: 2 (over x), seq: 16 (over z, y, core).
Axes of the slice: x: 2, y: 2, z: 4, core: 2. Of those that a mesh axis runs over, the one named last changes fastest.
Arguments:
- queries: bfloat16 [12288, 2240], P(('groups', 'seq')), parts along dimension 0, may hold values from -6 to 6
- key_rows: bfloat16 [12288, 2240], P(('groups', 'seq')), parts along dimension 0, may hold values from -6 to 6
- value_rows: bfloat16 [12288, 2240], P(('groups', 'seq')), parts along dimension 0, may hold values from -6 to 6
- frame_len: int32 [32, 2], P(('groups', 'seq')), parts along dimension 0, may hold values from 1 to 240, 384 in all within a row
- log_decay: float32 [32, 2, 20], P(('groups', 'seq')), parts along dimension 0, may hold values from -6 to 0
- timestep: int32 [32], P(('groups', 'seq')), parts along dimension 0, may hold values from 0 to 49
- conv_kernel: float32 [4, 2240], replicated, may hold values from -3 to 3
- norm_gain: float32 [2240], replicated, may hold values from 0.1 to 1.9
- mod_table: float32 [50, 2240], replicated, may hold values from -3 to 3
- out_grad: bfloat16 [12288, 2240], P(('groups', 'seq')), parts along dimension 0, may hold values from -6 to 6
Outputs:
- grad_queries: bfloat16 [12288, 2240], P(('groups', 'seq')), parts along dimension 0
- grad_keys: bfloat16 [12288, 2240], P(('groups', 'seq')), parts along dimension 0
- grad_values: bfloat16 [12288, 2240], P(('groups', 'seq')), parts along dimension 0
- grad_kernel: float32 [8, 2240], P('groups'), parts along dimension 0
- grad_gain: float32 [4480], P('groups'), parts along dimension 0
- grad_table: float32 [100, 2240], P('groups'), parts along dimension 0
The draws below stay inside these ranges and needn't reach their ends.
There are 2 independent parts, one for each index of `groups`. The reference program is written for one: setup_inputs(seed, part) draws one part's arguments, and reference() takes and returns one part's arrays. A program takes and returns all parts, laid end to end along the dimension named above; an argument that names none is the same for every part. Nothing has to cross between parts.
Inputs may be any that keep to these rules, and one draw needn't show every extreme that they name: `frame_len`: the 2 frames of each block hold 384 tokens together, and in every block the longest frame has at most 240 tokens.
All inputs are finite; a program needn't handle non-finite values.
Results may differ from the reference program's by a relative error of at most 0.0058.
Values may be sent and summed in bfloat16 or wider, within the bound.
A program may use at most 384 MiB of HBM per device.

```python
import math
import jax
import jax.numpy as jnp
import numpy as np
from jax import lax

H = 20
HD = 112
C = 2240
TOK_DEV = 384
FPD = 2
FMAX = 240
KC = 4
NT = 50
BLOCKS = 16
TOKENS = 6144


def draw_log_decay(key, part):
    random_child_keys = jax.random.split(key, 10)
    sequence_token_length = BLOCKS * FPD
    fast_count = H // 2
    cut_count = max(1, H // 10)
    head_rank = jax.random.permutation(random_child_keys[0], H)
    fast_heads = head_rank < fast_count
    early_heads = (head_rank >= fast_count) & (head_rank < fast_count + cut_count)
    late_heads = (head_rank >= fast_count + cut_count) & (head_rank < fast_count + 2 * cut_count)
    fast_rate = jnp.exp(jax.random.uniform(random_child_keys[1], (H,), minval=jnp.log(0.22), maxval=jnp.log(0.32)))
    slow_rate = jnp.exp(jax.random.uniform(random_child_keys[2], (H,), minval=jnp.log(0.1), maxval=jnp.log(0.5))) / sequence_token_length
    forgetting_rate = jnp.where(fast_heads, fast_rate, slow_rate)
    random_jitter = jax.random.uniform(random_child_keys[3], (BLOCKS, FPD, H), minval=0.8, maxval=1.6)
    spike_begin = jax.random.randint(random_child_keys[4], (2,), 0, sequence_token_length)
    spike_depth = jnp.log(jax.random.uniform(random_child_keys[5], (2,), minval=0.5, maxval=0.8))
    frame_offset = jnp.arange(sequence_token_length, dtype=jnp.int32).reshape(BLOCKS, FPD)
    spike_groups = jnp.sum(jnp.where(frame_offset[:, :, None] == spike_begin[None, None, :], spike_depth[None, None, :], 0.0), axis=2)
    early_block = BLOCKS // 16 + jax.random.randint(random_child_keys[6], (), 0, max(1, BLOCKS // 16))
    late_block = BLOCKS - 2 - jax.random.randint(random_child_keys[7], (), 0, 2)
    early_depth = jnp.log(jax.random.uniform(random_child_keys[8], (H,), minval=0.03, maxval=0.095))
    late_depth = jnp.log(jax.random.uniform(random_child_keys[9], (H,), minval=0.006, maxval=0.0095))
    early_drop = jnp.where(early_heads, early_depth, 0.0)
    late_drop = jnp.where(late_heads, late_depth, 0.0)
    early_here = (frame_offset == early_block * FPD)[:, :, None]
    late_here = (frame_offset == late_block * FPD)[:, :, None]
    split_groups = jnp.where(early_here, early_drop[None, None, :], 0.0) + jnp.where(late_here, late_drop[None, None, :], 0.0)
    computed_output = -forgetting_rate[None, None, :] * random_jitter + spike_groups[:, :, None] + split_groups
    return jnp.maximum(computed_output, -6.0).astype(jnp.float32)


def plant(array, stream_key, smallest, largest):
    place = [jax.random.randint(jax.random.fold_in(stream_key, axis), (), 0, length) for axis, length in enumerate(array.shape)]
    longest = array.shape.index(max(array.shape))
    neighbour = place[:longest] + [(place[longest] + 1) % array.shape[longest]] + place[longest + 1:]
    return array.at[tuple(place)].set(smallest).at[tuple(neighbour)].set(largest)


def level_of(own_key, shape, cuts, low, high):
    def one(dim, shards_of):
        steps = jax.random.uniform(jax.random.fold_in(jax.random.fold_in(own_key, 6), dim), (shards_of,), jnp.float32, low / len(cuts), high / len(cuts))
        return jnp.repeat(jnp.exp(steps), shape[dim] // shards_of).reshape((-1,) + (1,) * (len(shape) - dim - 1))

    level = one(*cuts[0])
    for cut in cuts[1:]:
        level = level * one(*cut)
    return level


def split_up(amount, total, most, slope):
    portions = [(1 << 20) // math.isqrt(grade ** slope) + 1 for grade in range(2, amount + 1)]
    spare, given = total - most - (amount - 1), [1] * (amount - 1)
    while spare > 0:
        free = [i for i in range(amount - 1) if given[i] < most]
        mass, budget = sum([portions[i] for i in free]), spare
        for i in free:
            more = min(most - given[i], max(1, budget * portions[i] // mass), spare)
            given[i] = given[i] + more
            spare = spare - more
    return np.array([most] + given)


def ragged(own_key, number_of, total, limit, lean):
    if number_of == 2:
        one = jax.random.randint(own_key, (), max(1, total - limit), min(limit, total - 1) + 1)
        return jnp.stack([one, total - one])
    sizes = jnp.asarray(split_up(number_of, total, limit, lean), jnp.int32)
    couples = (number_of - 1) // 2
    source_of, receiver = sizes[1:1 + 2 * couples:2], sizes[2:2 + 2 * couples:2]
    margin = jnp.minimum(source_of - 1, limit - receiver)
    passed = jax.random.randint(jax.random.fold_in(own_key, 1), (couples,), 0, 1 << 20) % (margin + 1)
    sizes = sizes.at[1:1 + 2 * couples:2].set(source_of - passed).at[2:2 + 2 * couples:2].set(receiver + passed)
    return sizes[jax.random.permutation(jax.random.fold_in(own_key, 2), number_of)]


def gaussian(key, shape, scale, bound, cuts=(), held_as=jnp.bfloat16):
    drawn = jax.random.normal(key, shape, jnp.float32) * scale
    if len(cuts) > 0:
        drawn = level_of(key, shape, cuts, -0.22, 0.18) * drawn
    return jnp.clip(drawn, min=-bound, max=bound).astype(held_as)


def setup_inputs(seed: int = 0, part: int = 0) -> dict:
    streams_of = jax.random.split(jax.random.key(seed), 11)
    own_keys = jax.random.split(jax.random.fold_in(streams_of[10], part), 11)
    queries = gaussian(own_keys[0], (TOKENS, C), 1.0, 6.0, ((0, 16),))
    key_rows = gaussian(own_keys[1], (TOKENS, C), 1.0, 6.0, ((0, 16),))
    value_rows = gaussian(own_keys[2], (TOKENS, C), 1.0, 6.0, ((0, 16),))
    frame_len = jax.vmap(lambda own: ragged(own, FPD, TOK_DEV, FMAX, 1))(jax.random.split(own_keys[3], BLOCKS)).reshape((BLOCKS, FPD)).astype(jnp.int32)
    log_decay = draw_log_decay(jax.random.fold_in(jax.random.fold_in(streams_of[10], part), 71), part)
    timestep = plant(jax.random.randint(own_keys[5], (BLOCKS,), 0, NT), jax.random.fold_in(own_keys[5], 1), 0, NT - 1).astype(jnp.int32)
    conv_kernel = gaussian(streams_of[6], (KC, C), 0.5, 3.0, (), jnp.float32)
    norm_gain = jnp.clip(1.0 + 0.18 * jax.random.normal(streams_of[7], (C,), jnp.float32), 0.1, 1.9)
    mod_table = gaussian(streams_of[8], (NT, C), 0.5, 3.0, (), jnp.float32)
    out_grad = gaussian(own_keys[9], (TOKENS, C), 1.0, 6.0, ((0, 16),))
    return {"queries": queries, "key_rows": key_rows, "value_rows": value_rows, "frame_len": frame_len, "log_decay": log_decay, "timestep": timestep, "conv_kernel": conv_kernel, "norm_gain": norm_gain, "mod_table": mod_table, "out_grad": out_grad}


EPSILON = 1e-06

def frame_layout(lengths, decays, count):
    bounds = jnp.cumsum(lengths).astype(jnp.int32)
    position = jnp.arange(count, dtype=jnp.int32)
    frame_id = lax.optimization_barrier(jnp.sum((position[:, None] >= bounds[None, :]).astype(jnp.int32), axis=1))
    frame_cum = jnp.cumsum(decays, axis=0)
    frame_numbers = jnp.arange(lengths.shape[0], dtype=jnp.int32)
    selector = (frame_id[:, None] == frame_numbers[None, :]).astype(decays.dtype)
    token_decay = lax.optimization_barrier(jnp.sum(selector[:, :, None] * frame_cum[None, :, :], axis=1))
    return (frame_id, token_decay, frame_cum[-1])

def decay_weights(frame_id, token_decay):
    allowed = (frame_id[:, None] >= frame_id[None, :])[None, :, :]
    head_major = token_decay.T
    spread = head_major[:, :, None] - head_major[:, None, :]
    return jnp.where(allowed, jnp.exp(jnp.where(allowed, spread, 0.0)), 0.0)

def causal_conv(padded, kernel, count):
    tap_count = kernel.shape[0]
    computed_output = jnp.zeros((count, kernel.shape[1]), jnp.float32)
    for offset in range(tap_count):
        computed_output = computed_output + kernel[offset] * padded[tap_count - 1 - offset:tap_count - 1 - offset + count]
    return computed_output

def conv_back(padded_grad, kernel, count):
    computed_output = jnp.zeros((count, kernel.shape[1]), jnp.float32)
    for offset in range(kernel.shape[0]):
        computed_output = computed_output + kernel[offset] * padded_grad[offset:offset + count]
    return computed_output

def reference(queries, key_rows, value_rows, frame_len, log_decay, timestep, conv_kernel, norm_gain, mod_table, out_grad):
    score_scale = HD ** (-0.5)
    exact = lax.Precision.HIGHEST
    padded = jnp.concatenate([jnp.zeros((KC - 1, C), jnp.float32), value_rows.astype(jnp.float32)], axis=0)
    conv_values = causal_conv(padded, conv_kernel, TOKENS).astype(jnp.bfloat16)
    query_blocks = queries.reshape(BLOCKS, TOK_DEV, H, HD)
    key_blocks = key_rows.reshape(BLOCKS, TOK_DEV, H, HD)
    value_blocks = conv_values.reshape(BLOCKS, TOK_DEV, H, HD)
    grad_blocks = out_grad.reshape(BLOCKS, TOK_DEV, H, HD)
    mod_rows = mod_table[timestep]

    def forward_step(state, pieces):
        key_block, value_block, lengths, decays = pieces
        frame_id, token_decay, block_decay = frame_layout(lengths, decays, TOK_DEV)
        into_end = jnp.exp(block_decay[None, :] - token_decay)
        scaled_keys = key_block.astype(jnp.float32) * into_end[:, :, None]
        local_state = jnp.einsum('thd,the->hde', scaled_keys, value_block.astype(jnp.float32), precision=exact)
        return (jnp.exp(block_decay)[:, None, None] * state + local_state, state)
    zero_state = jnp.zeros((H, HD, HD), jnp.float32)
    final_state, states_in = lax.scan(forward_step, zero_state, (key_blocks, value_blocks, frame_len, log_decay))

    def first_pass(pieces):
        query_block, key_block, value_block, lengths, decays, state_in, grad_block, mod_row = pieces
        frame_id, token_decay, block_decay = frame_layout(lengths, decays, TOK_DEV)
        weights_mask = decay_weights(frame_id, token_decay)
        from_start = jnp.exp(token_decay)
        query_float = query_block.astype(jnp.float32)
        key_float = key_block.astype(jnp.float32)
        value_float = value_block.astype(jnp.float32)
        scores = jnp.einsum('thd,shd->hts', query_float, key_float)
        attn_weights = (scores * weights_mask * score_scale).astype(jnp.bfloat16)
        numerator = jnp.einsum('hts,shd->thd', attn_weights.astype(jnp.float32), value_float)
        scaled_queries = query_float * (score_scale * from_start)[:, :, None]
        numerator = numerator + jnp.einsum('thd,hde->the', scaled_queries, state_in, precision=exact)
        inv_rms = lax.rsqrt(lax.optimization_barrier(jnp.mean(numerator * numerator, axis=2, keepdims=True)) + EPSILON)
        normed = numerator * inv_rms
        upstream = grad_block.astype(jnp.float32)
        normed_grad = upstream * (norm_gain * (1.0 + mod_row)).reshape(H, HD)
        numer_grad = inv_rms * (normed_grad - normed * lax.optimization_barrier(jnp.mean(normed_grad * normed, axis=2, keepdims=True)))
        grad_rounded = numer_grad.astype(jnp.bfloat16)
        rounded_float = grad_rounded.astype(jnp.float32)
        score_grad = jnp.einsum('thd,shd->hts', rounded_float, value_float)
        score_grad = (score_grad * weights_mask * score_scale).astype(jnp.bfloat16).astype(jnp.float32)
        adjoint_local = jnp.einsum('thd,the->hde', scaled_queries, numer_grad, precision=exact)
        query_grad = jnp.einsum('hts,shd->thd', score_grad, key_float)
        query_grad = query_grad + (score_scale * from_start)[:, :, None] * jnp.einsum('the,hde->thd', numer_grad, state_in, precision=exact)
        key_local = jnp.einsum('hts,thd->shd', score_grad, query_float)
        value_local = jnp.einsum('hts,thd->shd', attn_weights.astype(jnp.float32), rounded_float)
        block_terms = lax.optimization_barrier(jnp.sum((upstream * normed).reshape(TOK_DEV, C), axis=0))
        return (query_grad.astype(jnp.bfloat16), key_local, value_local, adjoint_local, block_terms, jnp.exp(block_decay))
    first = lax.map(first_pass, (query_blocks, key_blocks, value_blocks, frame_len, log_decay, states_in, grad_blocks, mod_rows))
    query_grads, key_locals, value_locals, adjoint_locals, block_terms, block_factors = first

    def backward_step(running, pieces):
        factor, local_part = pieces
        return (factor[:, None, None] * running + local_part, running)
    last_adjoint, adjoints = lax.scan(backward_step, zero_state, (block_factors, adjoint_locals), reverse=True)

    def second_pass(pieces):
        key_block, value_block, lengths, decays, adjoint, key_local, value_local = pieces
        frame_id, token_decay, block_decay = frame_layout(lengths, decays, TOK_DEV)
        into_end = jnp.exp(block_decay[None, :] - token_decay)
        scaled_keys = key_block.astype(jnp.float32) * into_end[:, :, None]
        key_grad = key_local + into_end[:, :, None] * jnp.einsum('the,hde->thd', value_block.astype(jnp.float32), adjoint, precision=exact)
        value_grad = value_local + jnp.einsum('thd,hde->the', scaled_keys, adjoint, precision=exact)
        return (key_grad.astype(jnp.bfloat16), value_grad)
    key_grads, value_grads = lax.map(second_pass, (key_blocks, value_blocks, frame_len, log_decay, adjoints, key_locals, value_locals))
    conv_grad = value_grads.reshape(TOKENS, C)
    padded_grad = jnp.concatenate([conv_grad, jnp.zeros((KC - 1, C), jnp.float32)], axis=0)
    grad_values = conv_back(padded_grad, conv_kernel, TOKENS).astype(jnp.bfloat16)
    kernel_rows = [lax.optimization_barrier(jnp.sum(conv_grad * padded[KC - 1 - offset:KC - 1 - offset + TOKENS], axis=0)) for offset in range(KC)]
    grad_kernel = jnp.stack(kernel_rows, axis=0) / BLOCKS
    grad_gain = lax.optimization_barrier(jnp.sum(block_terms * (1.0 + mod_rows), axis=0)) / BLOCKS
    selector = (timestep[:, None] == jnp.arange(NT, dtype=jnp.int32)[None, :]).astype(jnp.float32)
    grad_table = jnp.dot(selector.T, block_terms * norm_gain, precision=exact) / BLOCKS
    return (query_grads.reshape(TOKENS, C), key_grads.reshape(TOKENS, C), grad_values, grad_kernel, grad_gain, grad_table)
```

```python
import functools

import jax
import jax.numpy as jnp
from jax import lax
from jax.experimental import pallas as pl
from jax.experimental.pallas import tpu as pltpu
from jax.sharding import PartitionSpec as P

EPSILON = 1e-06
MESH = pl.DeviceIdType.MESH
F32, BF16 = jnp.float32, jnp.bfloat16


def mm(a, b, ca, cb):
    return lax.dot_general(a, b, (((ca,), (cb,)), ((), ())), preferred_element_type=F32)


def fused_kernel(
    n, heads, dim, count, taps, levels, early_attn,
    frame_len, log_decay, timestep, query_hbm, key_hbm, value_hbm, up_hbm, mod_hbm, conv_kernel, norm_gain,
    grad_query, grad_key, grad_value, kernel_sum, gain_sum, table_sum,
    query, key, value, up, mod, conv, attn, part, key_part, grad, state, local, late_pairs,
    from_core, to_chip, from_chip, to_plane, from_plane, back_chip, got_chip, back_core, chip_sum, plane_sum, chip_in,
    factors, e1_tab, rs_tab, ie_tab, we_tab, sc0_tab, sc1_tab, columns, before,
    halo_out, halo_in, edge_out, edge_in, edge_fix, opening, ending, tap_cols, term_cols, term_row, terms_all, terms_rows,
    tap_rows, tap_in, tap_own, tap_all,
    load_sem, halo_sem, edge_sem, f_send, f_recv, scan_send, scan_recv, term_send, term_recv,
    t1_send, t1_recv, t2_send, t2_recv,
):
    groups = heads // 4
    planes = n // 4
    channels = heads * dim
    padded = columns.shape[0]
    chunks = padded // 128
    span = taps - 1
    scale = dim ** (-0.5)
    me = lax.axis_index("seq")
    video = lax.axis_index("groups")
    core, chip, plane = me % 2, (me // 2) % 2, me // 4
    spot = me % 4
    core_peer = me + 1 - 2 * core
    chip_peer = me + 2 - 4 * chip

    def dev(peer):
        return (video, peer)

    def remote(src, dst, send, recv, peer):
        return pltpu.make_async_remote_copy(
            src_ref=src, dst_ref=dst, send_sem=send, recv_sem=recv, device_id=dev(peer), device_id_type=MESH)

    def others(fn):
        def go(k, c):
            fn(lax.rem(me + k, n))
            return c

        lax.fori_loop(1, n, go, 0)

    barrier = pltpu.get_barrier_semaphore()
    others(lambda peer: pl.semaphore_signal(barrier, inc=1, device_id=dev(peer), device_id_type=MESH))
    loads = [
        pltpu.make_async_copy(src, dst, load_sem.at[i])
        for i, (src, dst) in enumerate(
            ((value_hbm, value), (key_hbm, key), (query_hbm, query), (mod_hbm, mod), (up_hbm, up)))
    ]
    for load in loads:
        load.start()

    first = frame_len[0, 0]
    rows = e1_tab.shape[0]
    row_index = lax.broadcasted_iota(jnp.int32, (rows, count), 0)
    late = lax.broadcasted_iota(jnp.int32, (1, count), 1) >= first
    late_rows = lax.broadcasted_iota(jnp.int32, (rows, count), 1) >= first
    cum0 = jnp.zeros((rows, count), F32)
    cum1 = jnp.zeros((rows, count), F32)
    for h in range(heads):
        a = log_decay[0, h]
        b = a + log_decay[1, h]
        cum0 = jnp.where(row_index == h, a, cum0)
        cum1 = jnp.where(row_index == h, b, cum1)
    e1 = jnp.exp(cum1 - cum0)
    from0, from1 = scale * jnp.exp(cum0), scale * jnp.exp(cum1)
    e1_tab[...] = e1
    sc0_tab[...] = from0
    sc1_tab[...] = from1
    rs_tab[...] = jnp.where(late_rows, from1, from0)
    ie_tab[...] = jnp.where(late_rows, 1.0, e1)
    we_tab[...] = scale * jnp.where(late_rows, e1, 1.0)
    factors[spot] = jnp.exp(cum1)[:, :128]
    tap_cols[...] = jnp.zeros(tap_cols.shape, F32)
    term_cols[...] = jnp.zeros(term_cols.shape, F32)

    sel_row = lax.broadcasted_iota(jnp.int32, (16, 128), 0)
    sel_lane = lax.broadcasted_iota(jnp.int32, (16, 128), 1)
    sel_last = ((sel_lane == sel_row + 128 - span) & (sel_row < span)).astype(F32).astype(BF16)
    sel_first = ((sel_lane == sel_row) & (sel_row < span)).astype(F32).astype(BF16)

    loads[0].wait()
    halo_out[...] = mm(sel_last, value[:, count - 128 :], 1, 1).astype(BF16)

    @pl.when(me == 0)
    def _():
        halo_in[...] = jnp.zeros(halo_in.shape, BF16)

    @pl.when(me == n - 1)
    def _():
        edge_in[...] = jnp.zeros(edge_in.shape, BF16)

    @pl.when(plane == 0)
    def _():
        from_plane[0] = jnp.zeros(from_plane.shape[1:], BF16)

    @pl.when(plane == planes - 1)
    def _():
        from_plane[1] = jnp.zeros(from_plane.shape[1:], BF16)

    pl.semaphore_wait(barrier, n - 1)

    halo_copy = remote(halo_out, halo_in, halo_sem.at[0], halo_sem.at[1], lax.rem(me + 1, n))
    edge_copy = remote(edge_out, edge_in, edge_sem.at[0], edge_sem.at[1], lax.rem(me + n - 1, n))

    @pl.when(me < n - 1)
    def _():
        halo_copy.start()

    def factor_copy(k, slot):
        peer = me - spot + lax.rem(spot + k, 4)
        return remote(factors.at[spot], factors.at[slot], f_send.at[k], f_recv.at[slot], peer)

    for k in range(1, 4):
        factor_copy(k, spot).start()

    loads[3].wait()
    level = timestep[0]
    mod_row = mod[pl.ds(level, 1), :]
    gain_row = norm_gain[...] * (1.0 + mod_row)
    table = jnp.concatenate([conv_kernel[...], gain_row, jnp.zeros((8 - taps - 1, channels), F32)], axis=0)
    table = jnp.concatenate([table, jnp.zeros((8, padded - channels), F32)], axis=1)
    for k in range(chunks):
        columns[k * 128 : (k + 1) * 128, :] = table[:, k * 128 : (k + 1) * 128].T

    loads[1].wait()
    loads[2].wait()

    def lanes(h):
        return pl.ds(pl.multiple_of(h * dim, 16), dim)

    def weigh(product, h):
        rows_of = lax.broadcasted_iota(jnp.int32, (count, count), 0) >= first
        early = we_tab[pl.ds(h, 1), :]
        behind = jnp.where(late, scale, 0.0)
        return (product * jnp.where(rows_of, behind, early)).astype(BF16)

    def attn_work(h):
        c = lanes(h)
        attn[h] = weigh(mm(key[c, :], query[c, :], 0, 0), h)

    def pair(p, fn):
        fn(p * 2, 0)
        fn(p * 2 + 1, 1)

    def pairs(start, stop, fn):
        def go(p, c):
            pair(p, fn)
            return c

        lax.fori_loop(start, stop, go, 0)

    pairs(0, early_attn, lambda h, j: attn_work(h))

    @pl.when(me > 0)
    def _():
        halo_copy.wait_recv()

    for k in range(1, 4):
        factor_copy(k, lax.rem(spot + k, 4)).wait_recv()
    before[0:channels, :] = mm(halo_in[...], sel_last, 0, 0).astype(BF16)

    def conv_work(g, i, h, j):
        c = lanes(h)
        x = value[c, :].astype(F32)
        joined = jnp.concatenate([before[c, :].astype(F32), x], axis=1)
        cols = columns[c, :]
        total = cols[:, 0:1] * x
        for t in range(1, taps):
            total = total + cols[:, t : t + 1] * pltpu.roll(joined, t, 1)[:, 128:]
        v = total.astype(BF16)
        conv[c, :] = v
        both = jnp.concatenate([jnp.where(late, 0.0, total), jnp.where(late, total, 0.0)], axis=0).astype(BF16)
        outer = mm(both, key[c, :], 1, 1)
        local[0, g, j, i] = (e1_tab[pl.ds(h, 1), :][:, :dim] * outer[:dim] + outer[dim:]).astype(BF16)

    def part_work(h):
        c = lanes(h)
        part[c, :] = mm(conv[c, :], attn[h], 1, 0)

    def norm_work(g, i, h, j):
        c = lanes(h)
        q = query[c, :]
        numerator = part[c, :] + rs_tab[pl.ds(h, 1), :] * mm(state[0, g, j, i], q, 1, 0)
        inv_rms = lax.rsqrt(jnp.mean(numerator * numerator, axis=0, keepdims=True) + EPSILON)
        normed = numerator * inv_rms
        upstream = up[c, :].astype(F32)
        term_cols[c, 0:1] = jnp.sum(upstream * normed, axis=1, keepdims=True)
        normed_grad = upstream * columns[c, :][:, taps : taps + 1]
        g_full = inv_rms * (normed_grad - normed * jnp.mean(normed_grad * normed, axis=0, keepdims=True))
        grad[c, :] = g_full.astype(BF16)
        both = jnp.concatenate([jnp.where(late, 0.0, g_full), jnp.where(late, g_full, 0.0)], axis=0).astype(BF16)
        outer = mm(both, q, 1, 1)
        local[1, g, j, i] = (
            sc0_tab[pl.ds(h, 1), :][:, :dim] * outer[:dim] + sc1_tab[pl.ds(h, 1), :][:, :dim] * outer[dim:]
        ).astype(BF16)

    def back_work(g, i, h, j):
        c = lanes(h)
        q, k, gr = query[c, :], key[c, :], grad[c, :]
        score = weigh(mm(conv[c, :], gr, 0, 0), h)
        grad_query[c, :] = (
            mm(k, score, 1, 0) + rs_tab[pl.ds(h, 1), :] * mm(state[0, g, j, i], gr, 0, 0)
        ).astype(BF16)
        key_part[c, :] = mm(q, score, 1, 1)
        part[c, :] = mm(gr, attn[h], 1, 1)

    lane_row = lax.broadcasted_iota(jnp.int32, (1, 128), 1)

    def value_work(g, i, h, j):
        c = lanes(h)
        own = part[c, :] + ie_tab[pl.ds(h, 1), :] * mm(state[1, g, j, i], key[c, :], 1, 0)
        opening[c, :] = own[:, :128].astype(BF16)
        x = value[c, :].astype(F32)
        prior = before[c, :].astype(F32)
        cols = columns[c, :]
        token = lax.broadcasted_iota(jnp.int32, (1, count), 1)
        total = cols[:, 0:1] * own
        sums = [jnp.sum(own * x, axis=1, keepdims=True)]
        for t in range(1, taps):
            ahead = jnp.where(token < count - t, pltpu.roll(own, count - t, 1), 0.0)
            total = total + cols[:, t : t + 1] * ahead
            edge = own[:, :128] * jnp.where(lane_row < t, pltpu.roll(prior, t, 1), 0.0)
            product = ahead * x
            product = edge + sum(product[:, k * 128 : (k + 1) * 128] for k in range(count // 128))
            sums.append(jnp.sum(product, axis=1, keepdims=True))
        grad_value[c, :] = total.astype(BF16)
        ending[c, :] = total[:, count - 128 :]
        tap_cols[c, 0:taps] = jnp.concatenate(sums, axis=1)

    def key_work(g, i, h, j):
        c = lanes(h)
        grad_key[c, :] = (
            key_part[c, :] + ie_tab[pl.ds(h, 1), :] * mm(state[1, g, j, i], conv[c, :], 0, 0)
        ).astype(BF16)

    def group_work(g, fn):
        def go(i, c):
            for j in range(2):
                fn(g, i, 4 * g + 2 * i + j, j)
            return c

        lax.fori_loop(0, 2, go, 0)

    def factor(slot, h):
        return factors[slot, pl.ds(h, 1), :][:, :dim]

    def scan_steps(rev):
        at = plane if rev == 0 else planes - 1 - plane
        core_first = core == rev
        chip_first = chip == rev
        ahead_plane = me + 4 if rev == 0 else me - 4
        onward = jnp.clip(ahead_plane, 0, n - 1)
        peer_slot = spot + 1 - 2 * core
        send = lambda k, g: scan_send.at[rev, k, g]
        recv = lambda k, g: scan_recv.at[rev, k, g]

        def core_copy(g, part_of):
            return remote(local.at[rev, g, part_of], from_core.at[rev, g], send(0, g), recv(0, g), core_peer)

        def chip_copy(g):
            return remote(to_chip.at[rev, g], from_chip.at[rev, g], send(1, g), recv(1, g), chip_peer)

        def plane_copy(g):
            return remote(to_plane.at[rev, g], from_plane.at[rev, g], send(2, g), recv(2, g), onward)

        def chip_back(g):
            return remote(back_chip.at[rev, g], got_chip.at[rev, g], send(3, g), recv(3, g), chip_peer)

        def core_back(g, part_of):
            return remote(back_core.at[rev, g], state.at[rev, g, part_of], send(4, g), recv(4, g), core_peer)

        def h0(g):
            core_copy(g, 1 - core).start()

        def h1(g):
            core_copy(g, core).wait_recv()
            for mine in (False, True):
                y = chip if mine else 1 - chip
                h = 4 * g + 2 * y + core
                a = jnp.where(core_first, factor(peer_slot, h), 1.0)
                b = jnp.where(core_first, 1.0, factor(spot, h))
                both = a * local[rev, g, core, y].astype(F32) + b * from_core[rev, g, y].astype(F32)
                if mine:
                    chip_sum[rev, g] = both
                else:
                    to_chip[rev, g] = both.astype(BF16)
                    chip_copy(g).start()

        def chip_factors(h):
            mine = factor(spot, h) * factor(peer_slot, h)
            other_chip = 2 * (1 - chip)
            return mine, factor(other_chip, h) * factor(other_chip + 1, h)

        def h2(g):
            chip_copy(g).wait_recv()
            h = 4 * g + spot
            mine, other = chip_factors(h)
            a = jnp.where(chip_first, other, 1.0)
            b = jnp.where(chip_first, 1.0, mine)
            plane_sum[rev, g] = a * chip_sum[rev, g] + b * from_chip[rev, g].astype(F32)

        def h3(g):
            @pl.when(at > 0)
            def _():
                plane_copy(g).wait_recv()

            h = 4 * g + spot
            mine, other = chip_factors(h)
            inward = from_plane[rev, g].astype(F32)

            @pl.when(at < planes - 1)
            def _():
                to_plane[rev, g] = (mine * other * inward + plane_sum[rev, g]).astype(BF16)
                plane_copy(g).start()

            one_if = lambda p: jnp.where(p, 1.0, 0.0)
            lead = jnp.where(chip_first, mine, other)
            first_sum = jnp.where(chip_first, chip_sum[rev, g], from_chip[rev, g].astype(F32))
            second = lead * inward + first_sum
            back_chip[rev, g] = jnp.where(chip_first, second, inward).astype(BF16)
            chip_back(g).start()
            chip_in[rev, g] = jnp.where(chip_first, inward, second)

        def h4(g):
            chip_back(g).wait_recv()
            first_slot = 2 * chip + rev
            for mine in (False, True):
                y = chip if mine else 1 - chip
                h = 4 * g + 2 * y + core
                entering = chip_in[rev, g] if mine else got_chip[rev, g].astype(F32)
                lead = jnp.where(core_first, local[rev, g, core, y].astype(F32), from_core[rev, g, y].astype(F32))
                second = factor(first_slot, h) * entering + lead
                state[rev, g, core, y] = jnp.where(core_first, entering, second).astype(BF16)
                back_core[rev, g, y] = jnp.where(core_first, second, entering).astype(BF16)
            core_back(g, core).start()

        def h5(g):
            core_back(g, 1 - core).wait_recv()

        def finish(g):
            core_copy(g, 1 - core).wait_send()
            chip_copy(g).wait_send()

            @pl.when(at < planes - 1)
            def _():
                plane_copy(g).wait_send()

            chip_back(g).wait_send()
            core_back(g, core).wait_send()

        return at, (h0, h1, h2, h3, h4, h5), finish

    fore_at, fore, fore_finish = scan_steps(0)
    back_at, back, back_finish = scan_steps(1)

    half = heads // 2
    norm_base = groups + 5 + 3 * (planes - 1)
    norm_base = max(norm_base, groups + half)
    back_base = norm_base + groups
    value_base = max(back_base + half, back_base + 2 * (planes - 1) + 4)
    ticks = value_base + groups

    def tick(i, carry):
        def at_tick(start, fn, stop=groups):
            g = i - start

            @pl.when((g >= 0) & (g < stop))
            def _():
                fn(g)

        at_tick(2, fore[1])
        at_tick(5, fore[2])
        at_tick(5 + 3 * fore_at, fore[3])
        at_tick(8 + 3 * fore_at, fore[4])
        at_tick(10 + 3 * fore_at, fore[5])
        at_tick(norm_base + 2, back[1])
        at_tick(back_base, back[2])
        at_tick(back_base + 2 * back_at, back[3])
        at_tick(back_base + 2 + 2 * back_at, back[4])
        at_tick(back_base + 3 + 2 * back_at, back[5])

        def stage_conv(g):
            group_work(g, conv_work)
            fore[0](g)

        def stage_part(p):
            @pl.when(p >= early_attn)
            def _():
                pair(p, lambda h, j: attn_work(h))

            pair(p, lambda h, j: part_work(h))

        def stage_norm(g):
            group_work(g, norm_work)
            back[0](g)

        def stage_back(p):
            pair(p, lambda h, j: back_work(p // 2, p % 2, h, j))

        def stage_value(g):
            group_work(g, value_work)

        at_tick(0, stage_conv)
        at_tick(groups, stage_part, half)

        @pl.when(i == norm_base)
        def _():
            loads[4].wait()

        at_tick(norm_base, stage_norm)

        @pl.when(i == back_base)
        def _():
            send_terms()

        at_tick(back_base, stage_back, half)
        at_tick(value_base, stage_value)
        return carry

    def term_copy(peer, slot):
        return remote(term_row, terms_all.at[slot], term_send.at[peer], term_recv.at[slot], peer)

    def send_terms():
        for k in range(chunks):
            piece = term_cols[k * 128 : (k + 1) * 128, :].T[0:1, :]
            if k == chunks - 1:
                piece = jnp.where(lane_row == channels - k * 128, level.astype(F32), piece)
            term_row[:, k * 128 : (k + 1) * 128] = piece
        terms_all[me] = term_row[...]
        others(lambda peer: term_copy(peer, me).start())

    lax.fori_loop(0, ticks, tick, 0)

    edge_out[...] = mm(sel_first, opening[...], 1, 1).astype(BF16)

    @pl.when(me > 0)
    def _():
        edge_copy.start()

    def t1_copy(peer, slot):
        return remote(tap_rows.at[peer], tap_in.at[slot], t1_send.at[peer], t1_recv.at[slot], peer)

    def t2_copy(peer, slot):
        return remote(tap_own, tap_all.at[slot], t2_send.at[peer], t2_recv.at[slot], peer)

    shares = tap_rows.shape[1]
    if shares * n > chunks:
        tap_rows[...] = jnp.zeros(tap_rows.shape, F32)
    for k in range(chunks):
        tap_rows[k % n, k // n] = tap_cols[k * 128 : (k + 1) * 128, :].T
    tap_in[me] = tap_rows[me]
    others(lambda peer: t1_copy(peer, me).start())

    def key_groups(start, stop):
        def go(g, c):
            group_work(g, key_work)
            return c

        lax.fori_loop(start, stop, go, 0)

    key_groups(0, groups // 2 + 1)
    others(lambda peer: t1_copy(peer, peer).wait_recv())
    tap_own[...] = jnp.sum(tap_in[...], axis=0) * (1.0 / n)
    tap_all[me] = tap_own[...]
    others(lambda peer: t2_copy(peer, me).start())
    key_groups(groups // 2 + 1, groups)

    others(lambda peer: term_copy(peer, peer).wait_recv())

    def gather_row(b, c):
        terms_rows[pl.ds(b, 1), :] = terms_all[b]
        return c

    lax.fori_loop(0, n, gather_row, 0)
    wanted = terms_rows[:, channels : channels + 1]
    level_lane = lax.broadcasted_iota(jnp.int32, (n, 64), 1).astype(F32)
    chosen = jnp.where(level_lane == wanted, 1.0, 0.0)
    sums = lax.dot_general(
        chosen, terms_rows[:, :channels], (((0,), (0,)), ((), ())), precision=lax.Precision.HIGHEST,
        preferred_element_type=F32)[:levels]
    gain_sum[...] = jnp.sum(sums * (1.0 + mod[...]), axis=0, keepdims=True) * (1.0 / n)
    table_sum[...] = sums * norm_gain[...] * (1.0 / n)

    @pl.when(me < n - 1)
    def _():
        edge_copy.wait_recv()

    fix_row = lax.broadcasted_iota(jnp.int32, (16, span * 128), 0)
    fix_lane = lax.broadcasted_iota(jnp.int32, (16, span * 128), 1)
    ahead_by = fix_lane // 128 + 1
    sel_fix = ((fix_lane % 128 == 128 - ahead_by + fix_row) & (fix_row < ahead_by)).astype(F32).astype(BF16)
    edge_fix[...] = mm(edge_in[...], sel_fix, 0, 0)

    def fix_work(h, j):
        c = lanes(h)
        cols = columns[c, :]
        tile = ending[c, :]
        for t in range(1, taps):
            tile = tile + cols[:, t : t + 1] * edge_fix[c, (t - 1) * 128 : t * 128]
        grad_value[c, count - 128 :] = tile.astype(BF16)

    pairs(0, half, fix_work)

    others(lambda peer: t2_copy(peer, peer).wait_recv())
    for k in range(chunks):
        width = min(128, channels - k * 128)
        kernel_sum[:, k * 128 : k * 128 + width] = tap_all[k % n, k // n][:taps, :width]

    @pl.when(me < n - 1)
    def _():
        halo_copy.wait_send()

    @pl.when(me > 0)
    def _():
        edge_copy.wait_send()

    for k in range(1, 4):
        factor_copy(k, spot).wait_send()

    def finish_scan(g, c):
        fore_finish(g)
        back_finish(g)
        return c

    lax.fori_loop(0, groups, finish_scan, 0)

    def finish_peer(peer):
        term_copy(peer, me).wait_send()
        t1_copy(peer, me).wait_send()
        t2_copy(peer, me).wait_send()

    others(finish_peer)


def write_kernel(parts, *refs):
    sem = refs[-1]
    copies = [pltpu.make_async_copy(refs[i], refs[parts + i], sem.at[i]) for i in range(parts)]
    for copy in copies:
        copy.start()
    for copy in copies:
        copy.wait()


def body(
    queries,
    key_rows,
    value_rows,
    frame_len,
    log_decay,
    timestep,
    conv_kernel,
    norm_gain,
    mod_table,
    out_grad,
):
    shape = jax.ShapeDtypeStruct
    count, channels = queries.shape
    heads = log_decay.shape[2]
    dim = channels // heads
    taps = conv_kernel.shape[0]
    levels = mod_table.shape[0]
    n = lax.axis_size("seq")
    groups = heads // 4
    padded = -(-channels // 128) * 128
    chunks = padded // 128
    shares = -(-chunks // n)
    head_rows = -(-heads // 8) * 8

    vmem = pl.BlockSpec(memory_space=pltpu.VMEM)
    smem = pl.BlockSpec(memory_space=pltpu.SMEM)
    hbm = pl.BlockSpec(memory_space=pl.ANY)
    whole = (channels, count)
    tile = (dim, dim)
    per = lambda *lead, dtype=BF16: pltpu.VMEM(tuple(lead) + tile, dtype)
    table = pltpu.VMEM((head_rows, count), F32)
    dma = lambda *dims: pltpu.SemaphoreType.DMA(dims)
    outs = (
        shape(whole, BF16), shape(whole, BF16), shape(whole, BF16),
        shape((taps, channels), F32), shape((1, channels), F32), shape((levels, channels), F32))
    results = pl.pallas_call(
        functools.partial(fused_kernel, n, heads, dim, count, taps, levels, 4),
        out_shape=outs,
        in_specs=[smem] * 3 + [hbm] * 5 + [vmem] * 2,
        out_specs=(vmem,) * len(outs),
        scratch_shapes=[
            pltpu.VMEM(whole, BF16), pltpu.VMEM(whole, BF16), pltpu.VMEM(whole, BF16), pltpu.VMEM(whole, BF16),
            pltpu.VMEM((levels, channels), F32),
            pltpu.VMEM(whole, BF16),
            pltpu.VMEM((heads, count, count), BF16),
            pltpu.VMEM(whole, F32), pltpu.VMEM(whole, F32),
            pltpu.VMEM(whole, BF16),
            per(2, groups, 2, 2), per(2, groups, 2, 2), pltpu.VMEM((8, 128), F32),
            per(2, groups, 2), per(2, groups), per(2, groups), per(2, groups), per(2, groups),
            per(2, groups), per(2, groups), per(2, groups, 2),
            per(2, groups, dtype=F32), per(2, groups, dtype=F32), per(2, groups, dtype=F32),
            pltpu.VMEM((4, head_rows, 128), F32),
            table, table, table, table, table, table,
            pltpu.VMEM((padded, 8), F32), pltpu.VMEM((padded, 128), BF16),
            pltpu.VMEM((16, channels), BF16), pltpu.VMEM((16, channels), BF16),
            pltpu.VMEM((16, channels), BF16), pltpu.VMEM((16, channels), BF16),
            pltpu.VMEM((channels, (taps - 1) * 128), F32),
            pltpu.VMEM((channels, 128), BF16), pltpu.VMEM((channels, 128), F32),
            pltpu.VMEM((padded, 8), F32), pltpu.VMEM((padded, 8), F32),
            pltpu.VMEM((1, padded), F32), pltpu.VMEM((n, 1, padded), F32), pltpu.VMEM((n, padded), F32),
            pltpu.VMEM((n, shares, 8, 128), F32), pltpu.VMEM((n, shares, 8, 128), F32),
            pltpu.VMEM((shares, 8, 128), F32), pltpu.VMEM((n, shares, 8, 128), F32),
            dma(5), dma(2), dma(2), dma(4), dma(4), dma(2, 5, groups), dma(2, 5, groups), dma(n), dma(n),
            dma(n), dma(n), dma(n), dma(n),
        ],
        compiler_params=pltpu.CompilerParams(
            collective_id=0, has_side_effects=True, vmem_limit_bytes=52 << 20),
        name="fused",
    )(
        frame_len, log_decay[0], timestep, queries.T, key_rows.T, value_rows.T, out_grad.T, mod_table,
        conv_kernel, norm_gain[None, :])
    grad_query, grad_key, grad_value, kernel_sum, gain_sum, table_sum = pl.pallas_call(
        functools.partial(write_kernel, len(outs)),
        out_shape=outs,
        in_specs=[hbm] * len(outs),
        out_specs=(hbm,) * len(outs),
        scratch_shapes=[dma(len(outs))],
        name="write",
    )(*results)
    return (grad_query.T, grad_key.T, grad_value.T, kernel_sum, gain_sum[0], table_sum)


def solution(mesh):
    in_specs = (
        P(("groups", "seq"), None),
        P(("groups", "seq"), None),
        P(("groups", "seq"), None),
        P(("groups", "seq"), None),
        P(("groups", "seq"), None, None),
        P(("groups", "seq")),
        P(),
        P(),
        P(),
        P(("groups", "seq"), None),
    )
    out_specs = (
        P(("groups", "seq"), None),
        P(("groups", "seq"), None),
        P(("groups", "seq"), None),
        P("groups", None),
        P("groups"),
        P("groups", None),
    )
    return jax.shard_map(body, mesh=mesh, in_specs=in_specs, out_specs=out_specs, check_vma=False)
```

```python
import functools

import jax
import jax.numpy as jnp
from jax import lax
from jax.experimental import pallas as pl
from jax.experimental.pallas import tpu as pltpu
from jax.sharding import PartitionSpec as P

EPSILON = 1e-06
MESH = pl.DeviceIdType.MESH
F32, BF16 = jnp.float32, jnp.bfloat16


def mm(a, b, ca, cb):
    return lax.dot_general(a, b, (((ca,), (cb,)), ((), ())), preferred_element_type=F32)


def fused_kernel(
    n, heads, dim, count, taps, levels, early_attn,
    frame_hbm, decay_hbm, level_hbm, query_hbm, key_hbm, value_hbm, up_hbm, mod_hbm, taps_hbm, gain_hbm,
    grad_query, grad_key, grad_value, kernel_sum, gain_sum, table_sum,
    frame_len, log_decay, timestep, conv_kernel, norm_gain, query, key, value, up, mod, conv, attn, part, key_part, grad, state, local, late_mask,
    from_core, to_chip, from_chip, to_plane, from_plane, back_chip, got_chip, back_core, chip_sum, plane_sum, chip_in,
    factors, e1_tab, rs_tab, ie_tab, we_tab, sc0_tab, sc1_tab, stack, columns, before,
    halo_out, halo_in, edge_out, edge_in, opening, ending, folds, term_row, terms_all, terms_rows,
    tap_rows, tap_in, tap_own, tap_all,
    load_sem, halo_sem, edge_sem, f_send, f_recv, scan_send, scan_recv, term_send, term_recv,
    t1_send, t1_recv, t2_send, t2_recv,
):
    groups = heads // 4
    planes = n // 4
    channels = heads * dim
    padded = stack.shape[1]
    chunks = padded // 128
    span = taps - 1
    scale = dim ** (-0.5)
    me = lax.axis_index("seq")
    video = lax.axis_index("groups")
    core, chip, plane = me % 2, (me // 2) % 2, me // 4
    spot = me % 4
    core_peer = me + 1 - 2 * core
    chip_peer = me + 2 - 4 * chip

    def dev(peer):
        return (video, peer)

    def remote(src, dst, send, recv, peer):
        return pltpu.make_async_remote_copy(
            src_ref=src, dst_ref=dst, send_sem=send, recv_sem=recv, device_id=dev(peer), device_id_type=MESH)

    def others(fn):
        def go(k, c):
            fn(lax.rem(me + k, n))
            return c

        lax.fori_loop(1, n, go, 0)

    barrier = pltpu.get_barrier_semaphore()
    others(lambda peer: pl.semaphore_signal(barrier, inc=1, device_id=dev(peer), device_id_type=MESH))
    loads = [
        pltpu.make_async_copy(src, dst, load_sem.at[i])
        for i, (src, dst) in enumerate(
            ((frame_hbm, frame_len), (decay_hbm, log_decay), (level_hbm, timestep), (value_hbm, value), (key_hbm, key),
             (query_hbm, query), (taps_hbm, conv_kernel), (gain_hbm, norm_gain), (mod_hbm, mod), (up_hbm, up)))
    ]
    for load in loads:
        load.start()
    load_value, load_key, load_query, load_taps, load_gain, load_mod, load_up = loads[3:]
    for load in loads[:3]:
        load.wait()

    first = frame_len[0, 0]
    rows = e1_tab.shape[0]
    row_index = lax.broadcasted_iota(jnp.int32, (rows, count), 0)
    late = lax.broadcasted_iota(jnp.int32, (1, count), 1) >= first
    late_rows = lax.broadcasted_iota(jnp.int32, (rows, count), 1) >= first
    cum0 = jnp.zeros((rows, count), F32)
    cum1 = jnp.zeros((rows, count), F32)
    for h in range(heads):
        a = log_decay[0, 0, h]
        b = a + log_decay[0, 1, h]
        cum0 = jnp.where(row_index == h, a, cum0)
        cum1 = jnp.where(row_index == h, b, cum1)
    e1 = jnp.exp(cum1 - cum0)
    from0, from1 = scale * jnp.exp(cum0), scale * jnp.exp(cum1)
    e1_tab[...] = e1
    sc0_tab[...] = from0
    sc1_tab[...] = from1
    rs_tab[...] = jnp.where(late_rows, from1, from0)
    ie_tab[...] = jnp.where(late_rows, 1.0, e1)
    we_tab[...] = scale * jnp.where(late_rows, e1, 1.0)
    factors[spot] = jnp.exp(cum1)[:, :128]
    late_mask[...] = jnp.where(lax.broadcasted_iota(jnp.int32, (dim, count), 1) >= first, 1.0, 0.0).astype(BF16)

    sel_row = lax.broadcasted_iota(jnp.int32, (16, 128), 0)
    sel_lane = lax.broadcasted_iota(jnp.int32, (16, 128), 1)
    sel_last = ((sel_lane == sel_row + 128 - span) & (sel_row < span)).astype(F32).astype(BF16)
    sel_first = ((sel_lane == sel_row) & (sel_row < span)).astype(F32).astype(BF16)

    load_value.wait()
    halo_out[...] = mm(sel_last, value[:, count - 128 :], 1, 1).astype(BF16)

    @pl.when(me == 0)
    def _():
        halo_in[...] = jnp.zeros(halo_in.shape, BF16)

    @pl.when(me == n - 1)
    def _():
        edge_in[...] = jnp.zeros(edge_in.shape, BF16)

    @pl.when(plane == 0)
    def _():
        from_plane[0] = jnp.zeros(from_plane.shape[1:], BF16)

    @pl.when(plane == planes - 1)
    def _():
        from_plane[1] = jnp.zeros(from_plane.shape[1:], BF16)

    pl.semaphore_wait(barrier, n - 1)

    halo_copy = remote(halo_out, halo_in, halo_sem.at[0], halo_sem.at[1], lax.rem(me + 1, n))
    edge_copy = remote(edge_out, edge_in, edge_sem.at[0], edge_sem.at[1], lax.rem(me + n - 1, n))

    @pl.when(me < n - 1)
    def _():
        halo_copy.start()

    def factor_copy(k, slot):
        peer = me - spot + lax.rem(spot + k, 4)
        return remote(factors.at[spot], factors.at[slot], f_send.at[k], f_recv.at[slot], peer)

    for k in range(1, 4):
        factor_copy(k, spot).start()

    for load in (load_mod, load_taps, load_gain):
        load.wait()
    level = timestep[0]
    gain = norm_gain[...][None, :]
    gain_row = gain * (1.0 + mod[pl.ds(level, 1), :])
    table = jnp.concatenate([conv_kernel[...], gain_row, jnp.zeros((8 - taps - 1, channels), F32)], axis=0)
    upper = table.astype(BF16).astype(F32)
    middle = (table - upper).astype(BF16).astype(F32)
    stack[:, 0:channels] = jnp.concatenate(
        [upper, middle, table - upper - middle, jnp.zeros((8, channels), F32)], axis=0).astype(BF16)
    stack[:, channels:] = jnp.zeros((32, padded - channels), BF16)
    row_of = lax.broadcasted_iota(jnp.int32, (32, (taps + 1) * 128), 0)
    tap_of = lax.broadcasted_iota(jnp.int32, (32, (taps + 1) * 128), 1) // 128
    spread = ((row_of % 8 == tap_of) & (row_of < 24)).astype(F32).astype(BF16)

    def spread_columns(k, c):
        at = pl.ds(pl.multiple_of(k * 128, 128), 128)
        columns[at, :] = mm(stack[:, at], spread, 0, 0)
        return c

    lax.fori_loop(0, chunks, spread_columns, 0)

    def column(strip, t):
        tile = columns[strip, t * 128 : (t + 1) * 128]
        return jnp.concatenate([tile] * (count // 128), axis=1)

    load_key.wait()
    load_query.wait()

    def lanes(h):
        return pl.ds(pl.multiple_of(h * dim, 16), dim)

    def weigh(product, h):
        rows_of = lax.broadcasted_iota(jnp.int32, (count, count), 0) >= first
        early = we_tab[pl.ds(h, 1), :]
        behind = jnp.where(late, scale, 0.0)
        return (product * jnp.where(rows_of, behind, early)).astype(BF16)

    def attn_work(h):
        c = lanes(h)
        attn[h] = weigh(mm(key[c, :], query[c, :], 0, 0), h)

    def pair(p, fn):
        fn(p * 2, 0)
        fn(p * 2 + 1, 1)

    def pairs(start, stop, fn):
        def go(p, c):
            pair(p, fn)
            return c

        lax.fori_loop(start, stop, go, 0)

    pairs(0, early_attn, lambda h, j: attn_work(h))

    @pl.when(me > 0)
    def _():
        halo_copy.wait_recv()

    for k in range(1, 4):
        factor_copy(k, lax.rem(spot + k, 4)).wait_recv()
    before[...] = mm(halo_in[...], sel_last, 0, 0).astype(BF16)

    step = 16

    def strips(h):
        for r in range(0, dim, step):
            yield r, pl.ds(pl.multiple_of(h * dim + r, 16), step)

    def split_late(rows):
        second = rows * late_mask[...]
        return jnp.concatenate([rows - second, second], axis=0)

    def conv_work(g, i, h, j):
        c = lanes(h)
        for _, strip in strips(h):
            x = value[strip, :]
            joined = jnp.concatenate([before[strip, :], x], axis=1)
            total = column(strip, 0) * x.astype(F32)
            for t in range(1, taps):
                total = total + column(strip, t) * pltpu.roll(joined, t, 1)[:, 128:].astype(F32)
            conv[strip, :] = total.astype(BF16)
        outer = mm(split_late(conv[c, :]), key[c, :], 1, 1)
        local[0, g, j, i] = (e1_tab[pl.ds(h, 1), :][:, :dim] * outer[:dim] + outer[dim:]).astype(BF16)

    def part_work(h):
        c = lanes(h)
        part[c, :] = mm(conv[c, :], attn[h], 1, 0)

    def fold(t, strip, rows):
        total = sum(rows[:, k * 128 : (k + 1) * 128] for k in range(count // 128))
        upper = total.astype(BF16)
        folds[t, strip, 0:128] = upper
        folds[t, strip, 128:256] = (total - upper.astype(F32)).astype(BF16)

    def fold_sums(row, t):
        ones = (lax.broadcasted_iota(jnp.int32, (8, 256), 0) == row).astype(F32).astype(BF16)
        return mm(ones, folds[t], 1, 1)

    def norm_work(g, i, h, j):
        c = lanes(h)
        q = query[c, :]
        inter = mm(state[0, g, j, i], q, 1, 0)
        row_scale = rs_tab[pl.ds(h, 1), :]
        square = jnp.zeros((step, count), F32)
        cross = jnp.zeros((step, count), F32)
        for r, strip in strips(h):
            numerator = part[strip, :] + row_scale * inter[r : r + step]
            part[strip, :] = numerator
            square = square + numerator * numerator
            cross = cross + numerator * (up[strip, :].astype(F32) * column(strip, taps))
        square = jnp.sum(square, axis=0, keepdims=True) * (1.0 / dim)
        cross = jnp.sum(cross, axis=0, keepdims=True) * (1.0 / dim)
        inv_rms = lax.rsqrt(square + EPSILON)
        pull = inv_rms * (inv_rms * (inv_rms * cross))
        for _, strip in strips(h):
            numerator = part[strip, :]
            upstream = up[strip, :].astype(F32)
            terms = upstream * (numerator * inv_rms)
            fold(0, strip, terms)
            normed_grad = upstream * column(strip, taps)
            grad[strip, :] = (inv_rms * normed_grad - pull * numerator).astype(BF16)
        outer = mm(split_late(grad[c, :]), q, 1, 1)
        local[1, g, j, i] = (
            sc0_tab[pl.ds(h, 1), :][:, :dim] * outer[:dim] + sc1_tab[pl.ds(h, 1), :][:, :dim] * outer[dim:]
        ).astype(BF16)

    def back_work(g, i, h, j):
        c = lanes(h)
        q, k, gr = query[c, :], key[c, :], grad[c, :]
        score = weigh(mm(conv[c, :], gr, 0, 0), h)
        grad_query[c, :] = (
            mm(k, score, 1, 0) + rs_tab[pl.ds(h, 1), :] * mm(state[0, g, j, i], gr, 0, 0)
        ).astype(BF16)
        key_part[c, :] = mm(q, score, 1, 1)
        part[c, :] = mm(gr, attn[h], 1, 1)


    token = lax.broadcasted_iota(jnp.int32, (1, 128), 1)

    def value_work(g, i, h, j):
        c = lanes(h)
        inter = mm(state[1, g, j, i], key[c, :], 1, 0)
        into_end = ie_tab[pl.ds(h, 1), :]
        for r, strip in strips(h):
            own = part[strip, :] + into_end * inter[r : r + step]
            rounded = own.astype(BF16)
            opening[strip, :] = rounded[:, :128]
            x = value[strip, :].astype(F32)
            prior = before[strip, :]
            total = column(strip, 0) * own
            fold(0, strip, own * x)
            for t in range(1, taps):
                ahead = pltpu.roll(rounded, count - t, 1).astype(F32)
                ahead = jnp.concatenate(
                    [ahead[:, : count - 128], jnp.where(token < 128 - t, ahead[:, count - 128 :], 0.0)], axis=1)
                total = total + column(strip, t) * ahead
                edge = own[:, :128] * jnp.where(token < t, pltpu.roll(prior, t, 1).astype(F32), 0.0)
                product = ahead * x
                fold(t, strip, jnp.concatenate([product[:, :128] + edge, product[:, 128:]], axis=1))
            grad_value[strip, :] = total.astype(BF16)
            ending[strip, :] = total[:, count - 128 :]

    def key_work(g, i, h, j):
        c = lanes(h)
        grad_key[c, :] = (
            key_part[c, :] + ie_tab[pl.ds(h, 1), :] * mm(state[1, g, j, i], conv[c, :], 0, 0)
        ).astype(BF16)

    def group_work(g, fn):
        def go(i, c):
            for j in range(2):
                fn(g, i, 4 * g + 2 * i + j, j)
            return c

        lax.fori_loop(0, 2, go, 0)

    def factor(slot, h):
        return factors[slot, pl.ds(h, 1), :][:, :dim]

    def scan_steps(rev):
        at = plane if rev == 0 else planes - 1 - plane
        core_first = core == rev
        chip_first = chip == rev
        ahead_plane = me + 4 if rev == 0 else me - 4
        onward = jnp.clip(ahead_plane, 0, n - 1)
        peer_slot = spot + 1 - 2 * core
        send = lambda k, g: scan_send.at[rev, k, g]
        recv = lambda k, g: scan_recv.at[rev, k, g]

        def core_copy(g, part_of):
            return remote(local.at[rev, g, part_of], from_core.at[rev, g], send(0, g), recv(0, g), core_peer)

        def chip_copy(g):
            return remote(to_chip.at[rev, g], from_chip.at[rev, g], send(1, g), recv(1, g), chip_peer)

        def plane_copy(g):
            return remote(to_plane.at[rev, g], from_plane.at[rev, g], send(2, g), recv(2, g), onward)

        def chip_back(g):
            return remote(back_chip.at[rev, g], got_chip.at[rev, g], send(3, g), recv(3, g), chip_peer)

        def core_back(g, part_of):
            return remote(back_core.at[rev, g], state.at[rev, g, part_of], send(4, g), recv(4, g), core_peer)

        def h0(g):
            core_copy(g, 1 - core).start()

        def h1(g):
            core_copy(g, core).wait_recv()
            for mine in (False, True):
                y = chip if mine else 1 - chip
                h = 4 * g + 2 * y + core
                a = jnp.where(core_first, factor(peer_slot, h), 1.0)
                b = jnp.where(core_first, 1.0, factor(spot, h))
                both = a * local[rev, g, core, y].astype(F32) + b * from_core[rev, g, y].astype(F32)
                if mine:
                    chip_sum[rev, g] = both
                else:
                    to_chip[rev, g] = both.astype(BF16)
                    chip_copy(g).start()

        def chip_factors(h):
            mine = factor(spot, h) * factor(peer_slot, h)
            other_chip = 2 * (1 - chip)
            return mine, factor(other_chip, h) * factor(other_chip + 1, h)

        def h2(g):
            chip_copy(g).wait_recv()
            h = 4 * g + spot
            mine, other = chip_factors(h)
            a = jnp.where(chip_first, other, 1.0)
            b = jnp.where(chip_first, 1.0, mine)
            plane_sum[rev, g] = a * chip_sum[rev, g] + b * from_chip[rev, g].astype(F32)

        def h3(g):
            @pl.when(at > 0)
            def _():
                plane_copy(g).wait_recv()

            h = 4 * g + spot
            mine, other = chip_factors(h)
            inward = from_plane[rev, g].astype(F32)

            @pl.when(at < planes - 1)
            def _():
                to_plane[rev, g] = (mine * other * inward + plane_sum[rev, g]).astype(BF16)
                plane_copy(g).start()

            one_if = lambda p: jnp.where(p, 1.0, 0.0)
            lead = jnp.where(chip_first, mine, other)
            first_sum = jnp.where(chip_first, chip_sum[rev, g], from_chip[rev, g].astype(F32))
            second = lead * inward + first_sum
            back_chip[rev, g] = jnp.where(chip_first, second, inward).astype(BF16)
            chip_back(g).start()
            chip_in[rev, g] = jnp.where(chip_first, inward, second)

        def h4(g):
            chip_back(g).wait_recv()
            first_slot = 2 * chip + rev
            for mine in (False, True):
                y = chip if mine else 1 - chip
                h = 4 * g + 2 * y + core
                entering = chip_in[rev, g] if mine else got_chip[rev, g].astype(F32)
                lead = jnp.where(core_first, local[rev, g, core, y].astype(F32), from_core[rev, g, y].astype(F32))
                second = factor(first_slot, h) * entering + lead
                state[rev, g, core, y] = jnp.where(core_first, entering, second).astype(BF16)
                back_core[rev, g, y] = jnp.where(core_first, second, entering).astype(BF16)
            core_back(g, core).start()

        def h5(g):
            core_back(g, 1 - core).wait_recv()

        def finish(g):
            core_copy(g, 1 - core).wait_send()
            chip_copy(g).wait_send()

            @pl.when(at < planes - 1)
            def _():
                plane_copy(g).wait_send()

            chip_back(g).wait_send()
            core_back(g, core).wait_send()

        return at, (h0, h1, h2, h3, h4, h5), finish

    fore_at, fore, fore_finish = scan_steps(0)
    back_at, back, back_finish = scan_steps(1)

    half = heads // 2
    norm_base = groups + 5 + 3 * (planes - 1)
    norm_base = max(norm_base, groups + half)
    back_base = norm_base + groups
    value_base = max(back_base + half, back_base + 2 * (planes - 1) + 4)
    ticks = value_base + groups

    def tick(i, carry):
        def at_tick(start, fn, stop=groups):
            g = i - start

            @pl.when((g >= 0) & (g < stop))
            def _():
                fn(g)

        at_tick(2, fore[1])
        at_tick(5, fore[2])
        at_tick(5 + 3 * fore_at, fore[3])
        at_tick(8 + 3 * fore_at, fore[4])
        at_tick(10 + 3 * fore_at, fore[5])
        at_tick(norm_base + 2, back[1])
        at_tick(back_base, back[2])
        at_tick(back_base + 2 * back_at, back[3])
        at_tick(back_base + 2 + 2 * back_at, back[4])
        at_tick(back_base + 3 + 2 * back_at, back[5])

        def stage_conv(g):
            group_work(g, conv_work)
            fore[0](g)

        def stage_part(p):
            @pl.when(p >= early_attn)
            def _():
                pair(p, lambda h, j: attn_work(h))

            pair(p, lambda h, j: part_work(h))

        def stage_norm(g):
            group_work(g, norm_work)
            back[0](g)

        def stage_back(p):
            pair(p, lambda h, j: back_work(p // 2, p % 2, h, j))

        def stage_value(g):
            group_work(g, value_work)

        at_tick(0, stage_conv)
        at_tick(groups, stage_part, half)

        @pl.when(i == norm_base)
        def _():
            load_up.wait()

        at_tick(norm_base, stage_norm)

        @pl.when(i == back_base)
        def _():
            send_terms()

        at_tick(back_base, stage_back, half)
        at_tick(value_base, stage_value)
        return carry

    def term_copy(peer, slot):
        return remote(term_row, terms_all.at[slot], term_send.at[peer], term_recv.at[slot], peer)

    def send_terms():
        row = fold_sums(0, 0)[0:1, :]
        last = (chunks - 1) * 128
        term_row[:, :last] = row[:, :last]
        term_row[:, last:] = jnp.concatenate(
            [row[:, last:], jnp.full((1, padded - channels), level.astype(F32))], axis=1)
        terms_all[me] = term_row[...]
        others(lambda peer: term_copy(peer, me).start())

    lax.fori_loop(0, ticks, tick, 0)

    edge_out[...] = mm(sel_first, opening[...], 1, 1).astype(BF16)

    @pl.when(me > 0)
    def _():
        edge_copy.start()

    def t1_copy(peer, slot):
        return remote(tap_rows.at[peer], tap_in.at[slot], t1_send.at[peer], t1_recv.at[slot], peer)

    def t2_copy(peer, slot):
        return remote(tap_own, tap_all.at[slot], t2_send.at[peer], t2_recv.at[slot], peer)

    shares = tap_rows.shape[1]
    tap_rows[...] = jnp.zeros(tap_rows.shape, F32)
    tap_sums = sum(fold_sums(t, t) for t in range(taps))
    for k in range(chunks):
        width = min(128, channels - k * 128)
        tap_rows[k % n, k // n, :, :width] = tap_sums[:, k * 128 : k * 128 + width]
    tap_in[me] = tap_rows[me]
    others(lambda peer: t1_copy(peer, me).start())

    def key_groups(start, stop):
        def go(g, c):
            group_work(g, key_work)
            return c

        lax.fori_loop(start, stop, go, 0)

    key_groups(0, groups // 2 + 1)
    others(lambda peer: t1_copy(peer, peer).wait_recv())
    tap_own[...] = jnp.sum(tap_in[...], axis=0) * (1.0 / n)
    tap_all[me] = tap_own[...]
    others(lambda peer: t2_copy(peer, me).start())
    key_groups(groups // 2 + 1, groups)

    others(lambda peer: term_copy(peer, peer).wait_recv())

    def gather_row(b, c):
        terms_rows[pl.ds(b, 1), :] = terms_all[b]
        return c

    lax.fori_loop(0, n, gather_row, 0)
    wanted = terms_rows[:, channels : channels + 1]
    level_lane = lax.broadcasted_iota(jnp.int32, (n, 64), 1).astype(F32)
    chosen = jnp.where(level_lane == wanted, 1.0, 0.0)
    sums = lax.dot_general(
        chosen, terms_rows[:, :channels], (((0,), (0,)), ((), ())), precision=lax.Precision.HIGHEST,
        preferred_element_type=F32)[:levels]
    gain_sum[...] = (jnp.sum(sums * (1.0 + mod[...]), axis=0, keepdims=True) * (1.0 / n))[0]
    table_sum[...] = sums * gain * (1.0 / n)

    @pl.when(me < n - 1)
    def _():
        edge_copy.wait_recv()

    fix_row = lax.broadcasted_iota(jnp.int32, (16, span * 128), 0)
    fix_lane = lax.broadcasted_iota(jnp.int32, (16, span * 128), 1)
    ahead_by = fix_lane // 128 + 1
    sel_fix = ((fix_lane % 128 == 128 - ahead_by + fix_row) & (fix_row < ahead_by)).astype(F32).astype(BF16)
    key_part[:, 0 : span * 128] = mm(edge_in[...], sel_fix, 0, 0)

    def fix_work(h, j):
        c = lanes(h)
        tile = ending[c, :]
        for t in range(1, taps):
            tile = tile + columns[c, t * 128 : (t + 1) * 128] * key_part[c, (t - 1) * 128 : t * 128]
        grad_value[c, count - 128 :] = tile.astype(BF16)

    pairs(0, half, fix_work)

    others(lambda peer: t2_copy(peer, peer).wait_recv())
    for k in range(chunks):
        width = min(128, channels - k * 128)
        kernel_sum[:, k * 128 : k * 128 + width] = tap_all[k % n, k // n][:taps, :width]

    @pl.when(me < n - 1)
    def _():
        halo_copy.wait_send()

    @pl.when(me > 0)
    def _():
        edge_copy.wait_send()

    for k in range(1, 4):
        factor_copy(k, spot).wait_send()

    def finish_scan(g, c):
        fore_finish(g)
        back_finish(g)
        return c

    lax.fori_loop(0, groups, finish_scan, 0)

    def finish_peer(peer):
        term_copy(peer, me).wait_send()
        t1_copy(peer, me).wait_send()
        t2_copy(peer, me).wait_send()

    others(finish_peer)


def write_kernel(parts, *refs):
    sem = refs[-1]
    copies = [pltpu.make_async_copy(refs[i], refs[parts + i], sem.at[i]) for i in range(parts)]
    for copy in copies:
        copy.start()
    for copy in copies:
        copy.wait()


def body(
    queries,
    key_rows,
    value_rows,
    frame_len,
    log_decay,
    timestep,
    conv_kernel,
    norm_gain,
    mod_table,
    out_grad,
):
    shape = jax.ShapeDtypeStruct
    count, channels = queries.shape
    heads = log_decay.shape[2]
    dim = channels // heads
    taps = conv_kernel.shape[0]
    levels = mod_table.shape[0]
    n = lax.axis_size("seq")
    groups = heads // 4
    padded = -(-channels // 128) * 128
    chunks = padded // 128
    shares = -(-chunks // n)
    head_rows = -(-heads // 8) * 8

    vmem = pl.BlockSpec(memory_space=pltpu.VMEM)
    hbm = pl.BlockSpec(memory_space=pltpu.HBM)
    whole = (channels, count)
    tile = (dim, dim)
    per = lambda *lead, dtype=BF16: pltpu.VMEM(tuple(lead) + tile, dtype)
    table = pltpu.VMEM((head_rows, count), F32)
    dma = lambda *dims: pltpu.SemaphoreType.DMA(dims)
    outs = (
        shape(whole, BF16), shape(whole, BF16), shape(whole, BF16),
        shape((taps, channels), F32), shape((channels,), F32), shape((levels, channels), F32))
    results = pl.pallas_call(
        functools.partial(fused_kernel, n, heads, dim, count, taps, levels, 4),
        out_shape=outs,
        in_specs=[hbm] * 10,
        out_specs=(vmem,) * len(outs),
        scratch_shapes=[
            pltpu.SMEM(frame_len.shape, jnp.int32), pltpu.SMEM(log_decay.shape, F32), pltpu.SMEM((1,), jnp.int32),
            pltpu.VMEM(conv_kernel.shape, F32), pltpu.VMEM((channels,), F32),
            pltpu.VMEM(whole, BF16), pltpu.VMEM(whole, BF16), pltpu.VMEM(whole, BF16), pltpu.VMEM(whole, BF16),
            pltpu.VMEM((levels, channels), F32),
            pltpu.VMEM(whole, BF16),
            pltpu.VMEM((heads, count, count), BF16),
            pltpu.VMEM(whole, F32), pltpu.VMEM(whole, F32),
            pltpu.VMEM(whole, BF16),
            per(2, groups, 2, 2), per(2, groups, 2, 2), pltpu.VMEM((dim, count), BF16),
            per(2, groups, 2), per(2, groups), per(2, groups), per(2, groups), per(2, groups),
            per(2, groups), per(2, groups), per(2, groups, 2),
            per(2, groups, dtype=F32), per(2, groups, dtype=F32), per(2, groups, dtype=F32),
            pltpu.VMEM((4, head_rows, 128), F32),
            table, table, table, table, table, table,
            pltpu.VMEM((32, padded), BF16), pltpu.VMEM((padded, (taps + 1) * 128), F32),
            pltpu.VMEM((channels, 128), BF16),
            pltpu.VMEM((16, channels), BF16), pltpu.VMEM((16, channels), BF16),
            pltpu.VMEM((16, channels), BF16), pltpu.VMEM((16, channels), BF16),
            pltpu.VMEM((channels, 128), BF16), pltpu.VMEM((channels, 128), F32),
            pltpu.VMEM((taps, channels, 256), BF16),
            pltpu.VMEM((1, padded), F32), pltpu.VMEM((n, 1, padded), F32), pltpu.VMEM((n, padded), F32),
            pltpu.VMEM((n, shares, 8, 128), F32), pltpu.VMEM((n, shares, 8, 128), F32),
            pltpu.VMEM((shares, 8, 128), F32), pltpu.VMEM((n, shares, 8, 128), F32),
            dma(10), dma(2), dma(2), dma(4), dma(4), dma(2, 5, groups), dma(2, 5, groups), dma(n), dma(n),
            dma(n), dma(n), dma(n), dma(n),
        ],
        compiler_params=pltpu.CompilerParams(
            collective_id=0, has_side_effects=True, vmem_limit_bytes=(46 << 20) + (n << 16)),
        name="fused",
    )(
        frame_len, log_decay, timestep, queries.T, key_rows.T, value_rows.T, out_grad.T, mod_table,
        conv_kernel, norm_gain)
    grad_query, grad_key, grad_value, kernel_sum, gain_sum, table_sum = pl.pallas_call(
        functools.partial(write_kernel, len(outs)),
        out_shape=outs,
        in_specs=[vmem] * len(outs),
        out_specs=(hbm,) * len(outs),
        scratch_shapes=[dma(len(outs))],
        compiler_params=pltpu.CompilerParams(vmem_limit_bytes=1 << 20),
        name="write",
    )(*results)
    return (grad_query.T, grad_key.T, grad_value.T, kernel_sum, gain_sum, table_sum)


def solution(mesh):
    in_specs = (
        P(("groups", "seq"), None),
        P(("groups", "seq"), None),
        P(("groups", "seq"), None),
        P(("groups", "seq"), None),
        P(("groups", "seq"), None, None),
        P(("groups", "seq")),
        P(),
        P(),
        P(),
        P(("groups", "seq"), None),
    )
    out_specs = (
        P(("groups", "seq"), None),
        P(("groups", "seq"), None),
        P(("groups", "seq"), None),
        P("groups", None),
        P("groups"),
        P("groups", None),
    )
    return jax.shard_map(body, mesh=mesh, in_specs=in_specs, out_specs=out_specs, check_vma=False)
```

```python
import functools

import jax
import jax.numpy as jnp
from jax import lax
from jax.experimental import pallas as pl
from jax.experimental.pallas import tpu as pltpu
from jax.sharding import PartitionSpec as P

EPSILON = 1e-06
MESH = pl.DeviceIdType.MESH
F32, BF16 = jnp.float32, jnp.bfloat16


def mm(a, b, ca, cb):
    return lax.dot_general(a, b, (((ca,), (cb,)), ((), ())), preferred_element_type=F32)


def fused_kernel(
    n, heads, dim, count, taps, levels, early_attn, early_back,
    frame_hbm, decay_hbm, level_hbm, query_hbm, key_hbm, value_hbm, up_hbm, mod_hbm, taps_hbm, gain_hbm,
    grad_query, grad_key, grad_value, kernel_sum, gain_sum, table_sum,
    frame_len, log_decay, timestep, conv_kernel, norm_gain, query, key, value, up, mod, conv, attn, part, key_part, grad, state, local, late_mask,
    gathered, scattered, to_pair, from_pair, to_next, from_next, plane_sum, pair_sum, entering,
    factors, e1_tab, rs_tab, ie_tab, we_tab, sc0_tab, sc1_tab, stack, columns, before,
    halo_out, halo_in, edge_out, edge_in, opening, ending, folds, term_row, terms_all, terms_rows,
    tap_rows, tap_in, tap_own, tap_all,
    load_sem, halo_sem, edge_sem, f_send, f_recv, gather_send, gather_recv, scatter_send, scatter_recv,
    pair_send, pair_recv, next_send, next_recv, term_send, term_recv,
    t1_send, t1_recv, t2_send, t2_recv,
):
    groups = heads // 4
    planes = n // 4
    channels = heads * dim
    padded = stack.shape[1]
    chunks = padded // 128
    span = taps - 1
    scale = dim ** (-0.5)
    me = lax.axis_index("seq")
    video = lax.axis_index("groups")
    plane = me // 4
    spot, octet = me % 4, me % 8
    half_octet = octet - spot

    def dev(peer):
        return (video, peer)

    def remote(src, dst, send, recv, peer):
        return pltpu.make_async_remote_copy(
            src_ref=src, dst_ref=dst, send_sem=send, recv_sem=recv, device_id=dev(peer), device_id_type=MESH)

    def others(fn):
        def go(k, c):
            fn(lax.rem(me + k, n))
            return c

        lax.fori_loop(1, n, go, 0)

    barrier = pltpu.get_barrier_semaphore()
    others(lambda peer: pl.semaphore_signal(barrier, inc=1, device_id=dev(peer), device_id_type=MESH))
    loads = [
        pltpu.make_async_copy(src, dst, load_sem.at[i])
        for i, (src, dst) in enumerate(
            ((frame_hbm, frame_len), (decay_hbm, log_decay), (level_hbm, timestep), (value_hbm, value), (key_hbm, key),
             (query_hbm, query), (taps_hbm, conv_kernel), (gain_hbm, norm_gain), (mod_hbm, mod), (up_hbm, up)))
    ]
    for load in loads:
        load.start()
    load_value, load_key, load_query, load_taps, load_gain, load_mod, load_up = loads[3:]
    for load in loads[:3]:
        load.wait()

    first = frame_len[0, 0]
    rows = e1_tab.shape[0]
    row_index = lax.broadcasted_iota(jnp.int32, (rows, count), 0)
    late = lax.broadcasted_iota(jnp.int32, (1, count), 1) >= first
    late_rows = lax.broadcasted_iota(jnp.int32, (rows, count), 1) >= first
    cum0 = jnp.zeros((rows, count), F32)
    cum1 = jnp.zeros((rows, count), F32)
    for h in range(heads):
        a = log_decay[0, 0, h]
        b = a + log_decay[0, 1, h]
        cum0 = jnp.where(row_index == h, a, cum0)
        cum1 = jnp.where(row_index == h, b, cum1)
    e1 = jnp.exp(cum1 - cum0)
    from0, from1 = scale * jnp.exp(cum0), scale * jnp.exp(cum1)
    e1_tab[...] = e1
    sc0_tab[...] = from0
    sc1_tab[...] = from1
    rs_tab[...] = jnp.where(late_rows, from1, from0)
    ie_tab[...] = jnp.where(late_rows, 1.0, e1)
    we_tab[...] = scale * jnp.where(late_rows, e1, 1.0)
    factors[octet] = jnp.exp(cum1)[:, :128]
    late_mask[...] = jnp.where(lax.broadcasted_iota(jnp.int32, (dim, count), 1) >= first, 1.0, 0.0).astype(BF16)

    sel_row = lax.broadcasted_iota(jnp.int32, (16, 128), 0)
    sel_lane = lax.broadcasted_iota(jnp.int32, (16, 128), 1)
    sel_last = ((sel_lane == sel_row + 128 - span) & (sel_row < span)).astype(F32).astype(BF16)
    sel_first = ((sel_lane == sel_row) & (sel_row < span)).astype(F32).astype(BF16)

    load_value.wait()
    halo_out[...] = mm(sel_last, value[:, count - 128 :], 1, 1).astype(BF16)

    @pl.when(me == 0)
    def _():
        halo_in[...] = jnp.zeros(halo_in.shape, BF16)

    @pl.when(me == n - 1)
    def _():
        edge_in[...] = jnp.zeros(edge_in.shape, BF16)

    @pl.when(plane < 2)
    def _():
        from_next[0] = jnp.zeros(from_next.shape[1:], BF16)

    @pl.when(plane >= planes - 2)
    def _():
        from_next[1] = jnp.zeros(from_next.shape[1:], BF16)

    pl.semaphore_wait(barrier, n - 1)

    halo_copy = remote(halo_out, halo_in, halo_sem.at[0], halo_sem.at[1], lax.rem(me + 1, n))
    edge_copy = remote(edge_out, edge_in, edge_sem.at[0], edge_sem.at[1], lax.rem(me + n - 1, n))

    @pl.when(me < n - 1)
    def _():
        halo_copy.start()

    def factor_copy(k, slot):
        peer = me - octet + lax.rem(octet + k, 8)
        return remote(factors.at[octet], factors.at[slot], f_send.at[k], f_recv.at[slot], peer)

    for k in range(1, 8):
        factor_copy(k, octet).start()

    for load in (load_mod, load_taps, load_gain):
        load.wait()
    level = timestep[0]
    gain = norm_gain[...][None, :]
    gain_row = gain * (1.0 + mod[pl.ds(level, 1), :])
    table = jnp.concatenate([conv_kernel[...], gain_row, jnp.zeros((8 - taps - 1, channels), F32)], axis=0)
    upper = table.astype(BF16).astype(F32)
    middle = (table - upper).astype(BF16).astype(F32)
    stack[:, 0:channels] = jnp.concatenate(
        [upper, middle, table - upper - middle, jnp.zeros((8, channels), F32)], axis=0).astype(BF16)
    stack[:, channels:] = jnp.zeros((32, padded - channels), BF16)
    row_of = lax.broadcasted_iota(jnp.int32, (32, (taps + 1) * 128), 0)
    tap_of = lax.broadcasted_iota(jnp.int32, (32, (taps + 1) * 128), 1) // 128
    spread = ((row_of % 8 == tap_of) & (row_of < 24)).astype(F32).astype(BF16)

    def spread_columns(k, c):
        at = pl.ds(pl.multiple_of(k * 128, 128), 128)
        columns[at, :] = mm(stack[:, at], spread, 0, 0)
        return c

    lax.fori_loop(0, chunks, spread_columns, 0)

    def column(strip, t):
        tile = columns[strip, t * 128 : (t + 1) * 128]
        return jnp.concatenate([tile] * (count // 128), axis=1)

    load_key.wait()
    load_query.wait()

    def lanes(h):
        return pl.ds(pl.multiple_of(h * dim, 16), dim)

    def weigh(product, h):
        rows_of = lax.broadcasted_iota(jnp.int32, (count, count), 0) >= first
        early = we_tab[pl.ds(h, 1), :]
        behind = jnp.where(late, scale, 0.0)
        return (product * jnp.where(rows_of, behind, early)).astype(BF16)

    def attn_work(h):
        c = lanes(h)
        attn[h] = weigh(mm(key[c, :], query[c, :], 0, 0), h)

    def pair(p, fn):
        fn(p * 2, 0)
        fn(p * 2 + 1, 1)

    def pairs(start, stop, fn):
        def go(p, c):
            pair(p, fn)
            return c

        lax.fori_loop(start, stop, go, 0)

    pairs(0, early_attn, lambda h, j: attn_work(h))

    @pl.when(me > 0)
    def _():
        halo_copy.wait_recv()

    for k in range(1, 8):
        factor_copy(k, lax.rem(octet + k, 8)).wait_recv()
    before[...] = mm(halo_in[...], sel_last, 0, 0).astype(BF16)

    step = dim

    def strips(h):
        for r in range(0, dim, step):
            yield r, pl.ds(pl.multiple_of(h * dim + r, 16), step)

    def split_late(rows):
        second = rows * late_mask[...]
        return jnp.concatenate([rows - second, second], axis=0)

    def conv_work(g, i, h, j):
        c = lanes(h)
        for _, strip in strips(h):
            x = value[strip, :]
            joined = jnp.concatenate([before[strip, :], x], axis=1)
            total = column(strip, 0) * x.astype(F32)
            for t in range(1, taps):
                total = total + column(strip, t) * pltpu.roll(joined, t, 1)[:, 128:].astype(F32)
            conv[strip, :] = total.astype(BF16)
        outer = mm(split_late(conv[c, :]), key[c, :], 1, 1)
        local[0, g, 2 * i + j] = (e1_tab[pl.ds(h, 1), :][:, :dim] * outer[:dim] + outer[dim:]).astype(BF16)

    def part_work(h):
        c = lanes(h)
        part[c, :] = mm(conv[c, :], attn[h], 1, 0)

    def fold(t, strip, rows):
        total = sum(rows[:, k * 128 : (k + 1) * 128] for k in range(count // 128))
        upper = total.astype(BF16)
        folds[t, strip, 0:128] = upper
        folds[t, strip, 128:256] = (total - upper.astype(F32)).astype(BF16)

    def fold_sums(row, t):
        ones = (lax.broadcasted_iota(jnp.int32, (8, 256), 0) == row).astype(F32).astype(BF16)
        return mm(ones, folds[t], 1, 1)

    def norm_work(g, i, h, j):
        c = lanes(h)
        q = query[c, :]
        inter = mm(state[0, g, 2 * i + j], q, 1, 0)
        row_scale = rs_tab[pl.ds(h, 1), :]
        square = jnp.zeros((step, count), F32)
        cross = jnp.zeros((step, count), F32)
        for r, strip in strips(h):
            numerator = part[strip, :] + row_scale * inter[r : r + step]
            part[strip, :] = numerator
            square = square + numerator * numerator
            cross = cross + numerator * (up[strip, :].astype(F32) * column(strip, taps))
        square = jnp.sum(square, axis=0, keepdims=True) * (1.0 / dim)
        cross = jnp.sum(cross, axis=0, keepdims=True) * (1.0 / dim)
        inv_rms = lax.rsqrt(square + EPSILON)
        pull = inv_rms * (inv_rms * (inv_rms * cross))
        for _, strip in strips(h):
            numerator = part[strip, :]
            upstream = up[strip, :].astype(F32)
            terms = upstream * (numerator * inv_rms)
            fold(0, strip, terms)
            normed_grad = upstream * column(strip, taps)
            grad[strip, :] = (inv_rms * normed_grad - pull * numerator).astype(BF16)
        outer = mm(split_late(grad[c, :]), q, 1, 1)
        local[1, g, 2 * i + j] = (
            sc0_tab[pl.ds(h, 1), :][:, :dim] * outer[:dim] + sc1_tab[pl.ds(h, 1), :][:, :dim] * outer[dim:]
        ).astype(BF16)

    def back_work(g, i, h, j):
        c = lanes(h)
        q, k, gr = query[c, :], key[c, :], grad[c, :]
        score = weigh(mm(conv[c, :], gr, 0, 0), h)
        grad_query[c, :] = (
            mm(k, score, 1, 0) + rs_tab[pl.ds(h, 1), :] * mm(state[0, g, 2 * i + j], gr, 0, 0)
        ).astype(BF16)
        key_part[c, :] = mm(q, score, 1, 1)


    def carry_work(g, i, h, j):
        c = lanes(h)
        part[c, :] = mm(grad[c, :], attn[h], 1, 1)

    token = lax.broadcasted_iota(jnp.int32, (1, 128), 1)

    def value_work(g, i, h, j):
        c = lanes(h)
        inter = mm(state[1, g, 2 * i + j], key[c, :], 1, 0)
        into_end = ie_tab[pl.ds(h, 1), :]
        for r, strip in strips(h):
            own = part[strip, :] + into_end * inter[r : r + step]
            rounded = own.astype(BF16)
            opening[strip, :] = rounded[:, :128]
            x = value[strip, :].astype(F32)
            prior = before[strip, :]
            total = column(strip, 0) * own
            fold(0, strip, own * x)
            for t in range(1, taps):
                ahead = pltpu.roll(rounded, count - t, 1).astype(F32)
                ahead = jnp.concatenate(
                    [ahead[:, : count - 128], jnp.where(token < 128 - t, ahead[:, count - 128 :], 0.0)], axis=1)
                total = total + column(strip, t) * ahead
                edge = own[:, :128] * jnp.where(token < t, pltpu.roll(prior, t, 1).astype(F32), 0.0)
                product = ahead * x
                fold(t, strip, jnp.concatenate([product[:, :128] + edge, product[:, 128:]], axis=1))
            grad_value[strip, :] = total.astype(BF16)
            ending[strip, :] = total[:, count - 128 :]

    def key_work(g, i, h, j):
        c = lanes(h)
        grad_key[c, :] = (
            key_part[c, :] + ie_tab[pl.ds(h, 1), :] * mm(state[1, g, 2 * i + j], conv[c, :], 0, 0)
        ).astype(BF16)

    def group_work(g, fn):
        def go(i, c):
            for j in range(2):
                fn(g, i, 4 * g + 2 * i + j, j)
            return c

        lax.fori_loop(0, 2, go, 0)

    def factor(slot, h):
        return factors[slot, pl.ds(h, 1), :][:, :dim]

    def scan_steps(rev):
        at = plane if rev == 0 else planes - 1 - plane
        odd = at % 2
        order = range(4) if rev == 0 else range(3, -1, -1)
        stride = 4 if rev == 0 else -4
        peer_of = lambda k: me - spot + lax.rem(spot + k, 4)
        slot_of = lambda k: lax.rem(spot + k, 4)

        def gather_copy(g, k, slot):
            return remote(
                local.at[rev, g, slot_of(k)], gathered.at[rev, g, slot],
                gather_send.at[rev, g, k], gather_recv.at[rev, g, slot], peer_of(k))

        def scatter_copy(g, k, slot):
            return remote(
                scattered.at[rev, g, slot_of(k)], state.at[rev, g, slot],
                scatter_send.at[rev, g, k], scatter_recv.at[rev, g, slot], peer_of(k))

        def reach(hops):
            return jnp.clip(me + hops * stride, 0, n - 1)

        def pair_copy(g):
            return remote(
                to_pair.at[rev, g], from_pair.at[rev, g], pair_send.at[rev, g], pair_recv.at[rev, g], reach(1))

        def next_copy(g, hops):
            return remote(
                to_next.at[rev, g], from_next.at[rev, g], next_send.at[rev, g, hops - 1], next_recv.at[rev, g],
                reach(hops))

        def plane_factor(first, h):
            return (factor(first, h) * factor(first + 1, h)) * (factor(first + 2, h) * factor(first + 3, h))

        def onward(g, value):
            to_next[rev, g] = value.astype(BF16)
            for hops in (1, 2):
                @pl.when(at + hops < planes)
                def _():
                    next_copy(g, hops).start()

        def h0(g):
            for k in (2, 3, 1):
                gather_copy(g, k, spot).start()

        def h1(g):
            gathered[rev, g, spot] = local[rev, g, spot]
            for k in range(1, 4):
                gather_copy(g, k, slot_of(k)).wait_recv()
            h = 4 * g + spot
            total = None
            for p in order:
                x = gathered[rev, g, p].astype(F32)
                total = x if total is None else factor(half_octet + p, h) * total + x
            plane_sum[rev, g] = total

            @pl.when(odd == 0)
            def _():
                to_pair[rev, g] = total.astype(BF16)
                pair_copy(g).start()

        def h2(g):
            @pl.when(odd == 1)
            def _():
                pair_copy(g).wait_recv()
                h = 4 * g + spot
                total = plane_factor(half_octet, h) * from_pair[rev, g].astype(F32) + plane_sum[rev, g]
                pair_sum[rev, g] = total

                @pl.when(at == 1)
                def _():
                    onward(g, total)

        def h3(g):
            @pl.when(at >= 2)
            def _():
                next_copy(g, 1).wait_recv()

            h = 4 * g + spot

            @pl.when(odd == 1)
            def _():
                mine, prior = plane_factor(half_octet, h), plane_factor(4 - half_octet, h)
                start = from_next[rev, g].astype(F32)

                @pl.when(at >= 3)
                def _():
                    onward(g, mine * prior * start + pair_sum[rev, g])

                entering[rev, g] = prior * start + from_pair[rev, g].astype(F32)

            @pl.when(odd == 0)
            def _():
                entering[rev, g] = from_next[rev, g].astype(F32)

            total = entering[rev, g]
            for i, p in enumerate(order):
                scattered[rev, g, p] = total.astype(BF16)
                if i < 3:
                    total = factor(half_octet + p, h) * total + gathered[rev, g, p].astype(F32)
            for k in (2, 3, 1):
                scatter_copy(g, k, spot).start()
            state[rev, g, spot] = scattered[rev, g, spot]

        def h5(g):
            for k in range(1, 4):
                scatter_copy(g, k, slot_of(k)).wait_recv()

        def finish(g):
            for k in range(1, 4):
                gather_copy(g, k, spot).wait_send()
                scatter_copy(g, k, spot).wait_send()

            @pl.when(odd == 0)
            def _():
                pair_copy(g).wait_send()

            @pl.when(odd == 1)
            def _():
                for hops in (1, 2):
                    @pl.when(at + hops < planes)
                    def _():
                        next_copy(g, hops).wait_send()

        wait = jnp.where(odd == 1, 2 + 3 * (at // 2), jnp.where(at == 0, 0, 3 * (at // 2) + 1))
        return 3 + wait, (h0, h1, h2, h3, h5), finish

    fore_at, fore, fore_finish = scan_steps(0)
    back_at, back, back_finish = scan_steps(1)

    half = heads // 2
    depth = 5 + 3 * (planes // 2 - 1)
    norm_base = max(depth + 5, 2 * groups)
    carry_base = norm_base + groups
    back_base = carry_base + groups
    value_base = max(back_base + early_back, norm_base + depth + 5)
    ticks = value_base + groups

    def stage_back(p):
        pair(p, lambda h, j: back_work(p // 2, p % 2, h, j))

    def tick(i, carry):
        def at_tick(start, fn, stop=groups):
            g = i - start

            @pl.when((g >= 0) & (g < stop))
            def _():
                fn(g)

        at_tick(3, fore[1])
        at_tick(5, fore[2])
        at_tick(fore_at, fore[3])
        at_tick(norm_base, fore[4])
        at_tick(norm_base + 3, back[1])
        at_tick(norm_base + 5, back[2])
        at_tick(norm_base + back_at, back[3])
        at_tick(value_base, back[4])

        def stage_conv(g):
            group_work(g, conv_work)
            fore[0](g)

        def stage_part(g):
            for p in (2 * g, 2 * g + 1):
                @pl.when(p >= early_attn)
                def _():
                    pair(p, lambda h, j: attn_work(h))

                pair(p, lambda h, j: part_work(h))

        def stage_norm(g):
            group_work(g, norm_work)
            back[0](g)

        def stage_value(g):
            group_work(g, value_work)

        at_tick(0, stage_conv)
        at_tick(groups, stage_part)

        @pl.when(i == norm_base)
        def _():
            load_up.wait()

        at_tick(norm_base, stage_norm)

        @pl.when(i == carry_base)
        def _():
            send_terms()

        at_tick(carry_base, lambda g: group_work(g, carry_work))
        at_tick(back_base, stage_back, early_back)
        at_tick(value_base, stage_value)
        return carry

    def term_copy(peer, slot):
        return remote(term_row, terms_all.at[slot], term_send.at[peer], term_recv.at[slot], peer)

    def send_terms():
        row = fold_sums(0, 0)[0:1, :]
        last = (chunks - 1) * 128
        term_row[:, :last] = row[:, :last]
        term_row[:, last:] = jnp.concatenate(
            [row[:, last:], jnp.full((1, padded - channels), level.astype(F32))], axis=1)
        terms_all[me] = term_row[...]
        others(lambda peer: term_copy(peer, me).start())

    lax.fori_loop(0, ticks, tick, 0)

    edge_out[...] = mm(sel_first, opening[...], 1, 1).astype(BF16)

    @pl.when(me > 0)
    def _():
        edge_copy.start()

    def t1_copy(peer, slot):
        return remote(tap_rows.at[peer], tap_in.at[slot], t1_send.at[peer], t1_recv.at[slot], peer)

    def t2_copy(peer, slot):
        return remote(tap_own, tap_all.at[slot], t2_send.at[peer], t2_recv.at[slot], peer)

    shares = tap_rows.shape[1]
    tap_rows[...] = jnp.zeros(tap_rows.shape, F32)
    tap_sums = sum(fold_sums(t, t) for t in range(taps))
    for k in range(chunks):
        width = min(128, channels - k * 128)
        tap_rows[k % n, k // n, :, :width] = tap_sums[:, k * 128 : k * 128 + width]
    tap_in[me] = tap_rows[me]
    others(lambda peer: t1_copy(peer, me).start())

    def key_groups(start, stop):
        def go(g, c):
            group_work(g, key_work)
            return c

        lax.fori_loop(start, stop, go, 0)

    def late_back(p, c):
        stage_back(p)
        return c

    lax.fori_loop(early_back, half, late_back, 0)
    others(lambda peer: t1_copy(peer, peer).wait_recv())
    tap_own[...] = jnp.sum(tap_in[...], axis=0) * (1.0 / n)
    tap_all[me] = tap_own[...]
    others(lambda peer: t2_copy(peer, me).start())
    key_groups(0, groups)

    others(lambda peer: term_copy(peer, peer).wait_recv())

    def gather_row(b, c):
        terms_rows[pl.ds(b, 1), :] = terms_all[b]
        return c

    lax.fori_loop(0, n, gather_row, 0)
    wanted = terms_rows[:, channels : channels + 1]
    level_lane = lax.broadcasted_iota(jnp.int32, (n, 64), 1).astype(F32)
    chosen = jnp.where(level_lane == wanted, 1.0, 0.0)
    sums = lax.dot_general(
        chosen, terms_rows[:, :channels], (((0,), (0,)), ((), ())), precision=lax.Precision.HIGHEST,
        preferred_element_type=F32)[:levels]
    gain_sum[...] = (jnp.sum(sums * (1.0 + mod[...]), axis=0, keepdims=True) * (1.0 / n))[0]
    table_sum[...] = sums * gain * (1.0 / n)

    @pl.when(me < n - 1)
    def _():
        edge_copy.wait_recv()

    fix_row = lax.broadcasted_iota(jnp.int32, (16, span * 128), 0)
    fix_lane = lax.broadcasted_iota(jnp.int32, (16, span * 128), 1)
    ahead_by = fix_lane // 128 + 1
    sel_fix = ((fix_lane % 128 == 128 - ahead_by + fix_row) & (fix_row < ahead_by)).astype(F32).astype(BF16)
    key_part[:, 0 : span * 128] = mm(edge_in[...], sel_fix, 0, 0)

    def fix_work(h, j):
        c = lanes(h)
        tile = ending[c, :]
        for t in range(1, taps):
            tile = tile + columns[c, t * 128 : (t + 1) * 128] * key_part[c, (t - 1) * 128 : t * 128]
        grad_value[c, count - 128 :] = tile.astype(BF16)

    pairs(0, half, fix_work)

    others(lambda peer: t2_copy(peer, peer).wait_recv())
    for k in range(chunks):
        width = min(128, channels - k * 128)
        kernel_sum[:, k * 128 : k * 128 + width] = tap_all[k % n, k // n][:taps, :width]

    @pl.when(me < n - 1)
    def _():
        halo_copy.wait_send()

    @pl.when(me > 0)
    def _():
        edge_copy.wait_send()

    for k in range(1, 8):
        factor_copy(k, octet).wait_send()

    def finish_scan(g, c):
        fore_finish(g)
        back_finish(g)
        return c

    lax.fori_loop(0, groups, finish_scan, 0)

    def finish_peer(peer):
        term_copy(peer, me).wait_send()
        t1_copy(peer, me).wait_send()
        t2_copy(peer, me).wait_send()

    others(finish_peer)


def write_kernel(parts, *refs):
    sem = refs[-1]
    copies = [pltpu.make_async_copy(refs[i], refs[parts + i], sem.at[i]) for i in range(parts)]
    for copy in copies:
        copy.start()
    for copy in copies:
        copy.wait()


def body(
    queries,
    key_rows,
    value_rows,
    frame_len,
    log_decay,
    timestep,
    conv_kernel,
    norm_gain,
    mod_table,
    out_grad,
):
    shape = jax.ShapeDtypeStruct
    count, channels = queries.shape
    heads = log_decay.shape[2]
    dim = channels // heads
    taps = conv_kernel.shape[0]
    levels = mod_table.shape[0]
    n = lax.axis_size("seq")
    groups = heads // 4
    padded = -(-channels // 128) * 128
    chunks = padded // 128
    shares = -(-chunks // n)
    head_rows = -(-heads // 8) * 8

    vmem = pl.BlockSpec(memory_space=pltpu.VMEM)
    hbm = pl.BlockSpec(memory_space=pltpu.HBM)
    whole = (channels, count)
    tile = (dim, dim)
    per = lambda *lead, dtype=BF16: pltpu.VMEM(tuple(lead) + tile, dtype)
    table = pltpu.VMEM((head_rows, count), F32)
    dma = lambda *dims: pltpu.SemaphoreType.DMA(dims)
    outs = (
        shape(whole, BF16), shape(whole, BF16), shape(whole, BF16),
        shape((taps, channels), F32), shape((channels,), F32), shape((levels, channels), F32))
    results = pl.pallas_call(
        functools.partial(fused_kernel, n, heads, dim, count, taps, levels, 4, 6),
        out_shape=outs,
        in_specs=[hbm] * 10,
        out_specs=(vmem,) * len(outs),
        scratch_shapes=[
            pltpu.SMEM(frame_len.shape, jnp.int32), pltpu.SMEM(log_decay.shape, F32), pltpu.SMEM((1,), jnp.int32),
            pltpu.VMEM(conv_kernel.shape, F32), pltpu.VMEM((channels,), F32),
            pltpu.VMEM(whole, BF16), pltpu.VMEM(whole, BF16), pltpu.VMEM(whole, BF16), pltpu.VMEM(whole, BF16),
            pltpu.VMEM((levels, channels), F32),
            pltpu.VMEM(whole, BF16),
            pltpu.VMEM((heads, count, count), BF16),
            pltpu.VMEM(whole, F32), pltpu.VMEM(whole, F32),
            pltpu.VMEM(whole, BF16),
            per(2, groups, 4), per(2, groups, 4), pltpu.VMEM((dim, count), BF16),
            per(2, groups, 4), per(2, groups, 4), per(2, groups), per(2, groups), per(2, groups), per(2, groups),
            per(2, groups, dtype=F32), per(2, groups, dtype=F32), per(2, groups, dtype=F32),
            pltpu.VMEM((8, head_rows, 128), F32),
            table, table, table, table, table, table,
            pltpu.VMEM((32, padded), BF16), pltpu.VMEM((padded, (taps + 1) * 128), F32),
            pltpu.VMEM((channels, 128), BF16),
            pltpu.VMEM((16, channels), BF16), pltpu.VMEM((16, channels), BF16),
            pltpu.VMEM((16, channels), BF16), pltpu.VMEM((16, channels), BF16),
            pltpu.VMEM((channels, 128), BF16), pltpu.VMEM((channels, 128), F32),
            pltpu.VMEM((taps, channels, 256), BF16),
            pltpu.VMEM((1, padded), F32), pltpu.VMEM((n, 1, padded), F32), pltpu.VMEM((n, padded), F32),
            pltpu.VMEM((n, shares, 8, 128), F32), pltpu.VMEM((n, shares, 8, 128), F32),
            pltpu.VMEM((shares, 8, 128), F32), pltpu.VMEM((n, shares, 8, 128), F32),
            dma(10), dma(2), dma(2), dma(8), dma(8), dma(2, groups, 4), dma(2, groups, 4),
            dma(2, groups, 4), dma(2, groups, 4), dma(2, groups), dma(2, groups), dma(2, groups, 2), dma(2, groups),
            dma(n), dma(n),
            dma(n), dma(n), dma(n), dma(n),
        ],
        compiler_params=pltpu.CompilerParams(
            collective_id=0, has_side_effects=True, vmem_limit_bytes=(46 << 20) + (n << 16)),
        name="fused",
    )(
        frame_len, log_decay, timestep, queries.T, key_rows.T, value_rows.T, out_grad.T, mod_table,
        conv_kernel, norm_gain)
    grad_query, grad_key, grad_value, kernel_sum, gain_sum, table_sum = pl.pallas_call(
        functools.partial(write_kernel, len(outs)),
        out_shape=outs,
        in_specs=[vmem] * len(outs),
        out_specs=(hbm,) * len(outs),
        scratch_shapes=[dma(len(outs))],
        compiler_params=pltpu.CompilerParams(vmem_limit_bytes=1 << 20),
        name="write",
    )(*results)
    return (grad_query.T, grad_key.T, grad_value.T, kernel_sum, gain_sum, table_sum)


def solution(mesh):
    in_specs = (
        P(("groups", "seq"), None),
        P(("groups", "seq"), None),
        P(("groups", "seq"), None),
        P(("groups", "seq"), None),
        P(("groups", "seq"), None, None),
        P(("groups", "seq")),
        P(),
        P(),
        P(),
        P(("groups", "seq"), None),
    )
    out_specs = (
        P(("groups", "seq"), None),
        P(("groups", "seq"), None),
        P(("groups", "seq"), None),
        P("groups", None),
        P("groups"),
        P("groups", None),
    )
    return jax.shard_map(body, mesh=mesh, in_specs=in_specs, out_specs=out_specs, check_vma=False)
```

```python
import functools

import jax
import jax.numpy as jnp
from jax import lax
from jax.experimental import pallas as pl
from jax.experimental.pallas import tpu as pltpu
from jax.sharding import PartitionSpec as P

EPSILON = 1e-06
MESH = pl.DeviceIdType.MESH
F32, BF16 = jnp.float32, jnp.bfloat16


def mm(a, b, ca, cb):
    return lax.dot_general(a, b, (((ca,), (cb,)), ((), ())), preferred_element_type=F32)


def fused_kernel(
    n, heads, dim, count, taps, levels, early_attn,
    frame_hbm, decay_hbm, level_hbm, query_hbm, key_hbm, value_hbm, up_hbm, mod_hbm, taps_hbm, gain_hbm,
    grad_query, grad_key, grad_value, kernel_sum, gain_sum, table_sum,
    frame_len, log_decay, timestep, conv_kernel, norm_gain, query, key, value, up, mod, conv, attn, part, key_part, grad, state, local, late_mask,
    gathered, scattered, to_pair, from_pair, to_next, from_next, plane_sum, pair_sum, entering,
    factors, e1_tab, rs_tab, ie_tab, we_tab, sc0_tab, sc1_tab, stack, columns, before,
    halo_out, halo_in, edge_out, edge_in, opening, ending, folds, term_row, terms_all, terms_rows,
    tap_rows, tap_in, tap_own, tap_all,
    load_sem, halo_sem, edge_sem, f_send, f_recv, gather_send, gather_recv, scatter_send, scatter_recv,
    pair_send, pair_recv, next_send, next_recv, term_send, term_recv,
    t1_send, t1_recv, t2_send, t2_recv,
):
    groups = heads // 4
    planes = n // 4
    channels = heads * dim
    padded = stack.shape[1]
    chunks = padded // 128
    span = taps - 1
    scale = dim ** (-0.5)
    me = lax.axis_index("seq")
    video = lax.axis_index("groups")
    plane = me // 4
    spot, octet = me % 4, me % 8
    half_octet = octet - spot

    def dev(peer):
        return (video, peer)

    def remote(src, dst, send, recv, peer):
        return pltpu.make_async_remote_copy(
            src_ref=src, dst_ref=dst, send_sem=send, recv_sem=recv, device_id=dev(peer), device_id_type=MESH)

    def others(fn):
        def go(k, c):
            fn(lax.rem(me + k, n))
            return c

        lax.fori_loop(1, n, go, 0)

    barrier = pltpu.get_barrier_semaphore()
    others(lambda peer: pl.semaphore_signal(barrier, inc=1, device_id=dev(peer), device_id_type=MESH))
    loads = [
        pltpu.make_async_copy(src, dst, load_sem.at[i])
        for i, (src, dst) in enumerate(
            ((frame_hbm, frame_len), (decay_hbm, log_decay), (level_hbm, timestep), (value_hbm, value), (key_hbm, key),
             (query_hbm, query), (taps_hbm, conv_kernel), (gain_hbm, norm_gain), (mod_hbm, mod), (up_hbm, up)))
    ]
    for load in loads:
        load.start()
    load_value, load_key, load_query, load_taps, load_gain, load_mod, load_up = loads[3:]
    for load in loads[:3]:
        load.wait()

    first = frame_len[0, 0]
    rows = e1_tab.shape[0]
    row_index = lax.broadcasted_iota(jnp.int32, (rows, count), 0)
    late = lax.broadcasted_iota(jnp.int32, (1, count), 1) >= first
    late_rows = lax.broadcasted_iota(jnp.int32, (rows, count), 1) >= first
    cum0 = jnp.zeros((rows, count), F32)
    cum1 = jnp.zeros((rows, count), F32)
    for h in range(heads):
        a = log_decay[0, 0, h]
        b = a + log_decay[0, 1, h]
        cum0 = jnp.where(row_index == h, a, cum0)
        cum1 = jnp.where(row_index == h, b, cum1)
    e1 = jnp.exp(cum1 - cum0)
    from0, from1 = scale * jnp.exp(cum0), scale * jnp.exp(cum1)
    e1_tab[...] = e1
    sc0_tab[...] = from0
    sc1_tab[...] = from1
    rs_tab[...] = jnp.where(late_rows, from1, from0)
    ie_tab[...] = jnp.where(late_rows, 1.0, e1)
    we_tab[...] = scale * jnp.where(late_rows, e1, 1.0)
    factors[octet] = jnp.exp(cum1)[:, :128]
    late_mask[...] = jnp.where(lax.broadcasted_iota(jnp.int32, (dim, count), 1) >= first, 1.0, 0.0).astype(BF16)

    sel_row = lax.broadcasted_iota(jnp.int32, (16, 128), 0)
    sel_lane = lax.broadcasted_iota(jnp.int32, (16, 128), 1)
    sel_last = ((sel_lane == sel_row + 128 - span) & (sel_row < span)).astype(F32).astype(BF16)
    sel_first = ((sel_lane == sel_row) & (sel_row < span)).astype(F32).astype(BF16)

    load_value.wait()
    halo_out[...] = mm(sel_last, value[:, count - 128 :], 1, 1).astype(BF16)

    @pl.when(me == 0)
    def _():
        halo_in[...] = jnp.zeros(halo_in.shape, BF16)

    @pl.when(me == n - 1)
    def _():
        edge_in[...] = jnp.zeros(edge_in.shape, BF16)

    @pl.when(plane < 2)
    def _():
        from_next[0] = jnp.zeros(from_next.shape[1:], BF16)

    @pl.when(plane >= planes - 2)
    def _():
        from_next[1] = jnp.zeros(from_next.shape[1:], BF16)

    pl.semaphore_wait(barrier, n - 1)

    halo_copy = remote(halo_out, halo_in, halo_sem.at[0], halo_sem.at[1], lax.rem(me + 1, n))
    edge_copy = remote(edge_out, edge_in, edge_sem.at[0], edge_sem.at[1], lax.rem(me + n - 1, n))

    @pl.when(me < n - 1)
    def _():
        halo_copy.start()

    def factor_copy(k, slot):
        peer = me - octet + lax.rem(octet + k, 8)
        return remote(factors.at[octet], factors.at[slot], f_send.at[k], f_recv.at[slot], peer)

    for k in range(1, 8):
        factor_copy(k, octet).start()

    for load in (load_mod, load_taps, load_gain):
        load.wait()
    level = timestep[0]
    gain = norm_gain[...][None, :]
    gain_row = gain * (1.0 + mod[pl.ds(level, 1), :])
    table = jnp.concatenate([conv_kernel[...], gain_row, jnp.zeros((8 - taps - 1, channels), F32)], axis=0)
    upper = table.astype(BF16).astype(F32)
    middle = (table - upper).astype(BF16).astype(F32)
    stack[:, 0:channels] = jnp.concatenate(
        [upper, middle, table - upper - middle, jnp.zeros((8, channels), F32)], axis=0).astype(BF16)
    stack[:, channels:] = jnp.zeros((32, padded - channels), BF16)
    row_of = lax.broadcasted_iota(jnp.int32, (32, (taps + 1) * 128), 0)
    tap_of = lax.broadcasted_iota(jnp.int32, (32, (taps + 1) * 128), 1) // 128
    spread = ((row_of % 8 == tap_of) & (row_of < 24)).astype(F32).astype(BF16)

    def spread_columns(k, c):
        at = pl.ds(pl.multiple_of(k * 128, 128), 128)
        columns[at, :] = mm(stack[:, at], spread, 0, 0)
        return c

    def spread_some(k, c):
        for j in range(6):
            spread_columns(k * 6 + j, c)
        return c

    lax.fori_loop(0, chunks // 6, spread_some, 0)
    for k in range(chunks // 6 * 6, chunks):
        spread_columns(k, 0)

    def column(strip, t):
        tile = columns[strip, t * 128 : (t + 1) * 128]
        return jnp.concatenate([tile] * (count // 128), axis=1)

    load_key.wait()
    load_query.wait()

    def lanes(h):
        return pl.ds(pl.multiple_of(h * dim, 16), dim)

    def weigh(product, h):
        rows_of = lax.broadcasted_iota(jnp.int32, (count, count), 0) >= first
        early = we_tab[pl.ds(h, 1), :]
        behind = jnp.where(late, scale, 0.0)
        return (product * jnp.where(rows_of, behind, early)).astype(BF16)

    def attn_work(h):
        c = lanes(h)
        attn[h] = weigh(mm(key[c, :], query[c, :], 0, 0), h)

    def pair(p, fn):
        fn(p * 2, 0)
        fn(p * 2 + 1, 1)

    def pairs(start, stop, fn):
        def go(p, c):
            pair(p, fn)
            return c

        lax.fori_loop(start, stop, go, 0)

    pairs(0, early_attn, lambda h, j: attn_work(h))

    @pl.when(me > 0)
    def _():
        halo_copy.wait_recv()

    for k in range(1, 8):
        factor_copy(k, lax.rem(octet + k, 8)).wait_recv()
    before[...] = mm(halo_in[...], sel_last, 0, 0).astype(BF16)

    step = dim

    def strips(h):
        for r in range(0, dim, step):
            yield r, pl.ds(pl.multiple_of(h * dim + r, 16), step)

    def split_late(rows):
        second = rows * late_mask[...]
        return jnp.concatenate([rows - second, second], axis=0)

    def conv_work(g, i, h, j):
        c = lanes(h)
        for _, strip in strips(h):
            x = value[strip, :]
            joined = jnp.concatenate([before[strip, :], x], axis=1)
            total = column(strip, 0) * x.astype(F32)
            for t in range(1, taps):
                total = total + column(strip, t) * pltpu.roll(joined, t, 1)[:, 128:].astype(F32)
            conv[strip, :] = total.astype(BF16)
        outer = mm(split_late(conv[c, :]), key[c, :], 1, 1)
        local[0, g, 2 * i + j] = (e1_tab[pl.ds(h, 1), :][:, :dim] * outer[:dim] + outer[dim:]).astype(BF16)

    def part_work(h):
        c = lanes(h)
        part[c, :] = mm(conv[c, :], attn[h], 1, 0)

    def fold(t, strip, rows):
        total = sum(rows[:, k * 128 : (k + 1) * 128] for k in range(count // 128))
        upper = total.astype(BF16)
        folds[t, strip, 0:128] = upper
        folds[t, strip, 128:256] = (total - upper.astype(F32)).astype(BF16)

    def fold_sums(row, t):
        ones = (lax.broadcasted_iota(jnp.int32, (8, 256), 0) == row).astype(F32).astype(BF16)
        return mm(ones, folds[t], 1, 1)

    def norm_work(g, i, h, j):
        c = lanes(h)
        q = query[c, :]
        inter = mm(state[0, g, 2 * i + j], q, 1, 0)
        row_scale = rs_tab[pl.ds(h, 1), :]
        square = jnp.zeros((step, count), F32)
        cross = jnp.zeros((step, count), F32)
        for r, strip in strips(h):
            numerator = part[strip, :] + row_scale * inter[r : r + step]
            part[strip, :] = numerator
            square = square + numerator * numerator
            cross = cross + numerator * (up[strip, :].astype(F32) * column(strip, taps))
        square = jnp.sum(square, axis=0, keepdims=True) * (1.0 / dim)
        cross = jnp.sum(cross, axis=0, keepdims=True) * (1.0 / dim)
        inv_rms = lax.rsqrt(square + EPSILON)
        pull = inv_rms * (inv_rms * (inv_rms * cross))
        for _, strip in strips(h):
            numerator = part[strip, :]
            upstream = up[strip, :].astype(F32)
            terms = upstream * (numerator * inv_rms)
            fold(0, strip, terms)
            normed_grad = upstream * column(strip, taps)
            grad[strip, :] = (inv_rms * normed_grad - pull * numerator).astype(BF16)
        outer = mm(split_late(grad[c, :]), q, 1, 1)
        local[1, g, 2 * i + j] = (
            sc0_tab[pl.ds(h, 1), :][:, :dim] * outer[:dim] + sc1_tab[pl.ds(h, 1), :][:, :dim] * outer[dim:]
        ).astype(BF16)

    def back_work(g, i, h, j):
        c = lanes(h)
        q, k, gr = query[c, :], key[c, :], grad[c, :]
        score = weigh(mm(conv[c, :], gr, 0, 0), h)
        grad_query[c, :] = (
            mm(k, score, 1, 0) + rs_tab[pl.ds(h, 1), :] * mm(state[0, g, 2 * i + j], gr, 0, 0)
        ).astype(BF16)
        key_part[c, :] = mm(q, score, 1, 1)


    def carry_work(g, i, h, j):
        c = lanes(h)
        part[c, :] = mm(grad[c, :], attn[h], 1, 1)

    token = lax.broadcasted_iota(jnp.int32, (1, 128), 1)

    def value_work(g, i, h, j):
        c = lanes(h)
        inter = mm(state[1, g, 2 * i + j], key[c, :], 1, 0)
        into_end = ie_tab[pl.ds(h, 1), :]
        for r, strip in strips(h):
            own = part[strip, :] + into_end * inter[r : r + step]
            rounded = own.astype(BF16)
            opening[strip, :] = rounded[:, :128]
            x = value[strip, :].astype(F32)
            prior = before[strip, :]
            total = column(strip, 0) * own
            fold(0, strip, own * x)
            for t in range(1, taps):
                ahead = pltpu.roll(rounded, count - t, 1).astype(F32)
                ahead = jnp.concatenate(
                    [ahead[:, : count - 128], jnp.where(token < 128 - t, ahead[:, count - 128 :], 0.0)], axis=1)
                total = total + column(strip, t) * ahead
                edge = own[:, :128] * jnp.where(token < t, pltpu.roll(prior, t, 1).astype(F32), 0.0)
                product = ahead * x
                fold(t, strip, jnp.concatenate([product[:, :128] + edge, product[:, 128:]], axis=1))
            grad_value[strip, :] = total.astype(BF16)
            ending[strip, :] = total[:, count - 128 :]

    def key_work(g, i, h, j):
        c = lanes(h)
        grad_key[c, :] = (
            key_part[c, :] + ie_tab[pl.ds(h, 1), :] * mm(state[1, g, 2 * i + j], conv[c, :], 0, 0)
        ).astype(BF16)

    def group_work(g, fn):
        for i in range(2):
            for j in range(2):
                fn(g, i, 4 * g + 2 * i + j, j)

    def factor(slot, h):
        return factors[slot, pl.ds(h, 1), :][:, :dim]

    def scan_steps(rev):
        at = plane if rev == 0 else planes - 1 - plane
        odd = at % 2
        order = range(4) if rev == 0 else range(3, -1, -1)
        stride = 4 if rev == 0 else -4
        peer_of = lambda k: me - spot + lax.rem(spot + k, 4)
        slot_of = lambda k: lax.rem(spot + k, 4)

        def gather_copy(g, k, slot):
            return remote(
                local.at[rev, g, slot_of(k)], gathered.at[rev, g, slot],
                gather_send.at[rev, g, k], gather_recv.at[rev, g, slot], peer_of(k))

        def scatter_copy(g, k, slot):
            return remote(
                scattered.at[rev, g, slot_of(k)], state.at[rev, g, slot],
                scatter_send.at[rev, g, k], scatter_recv.at[rev, g, slot], peer_of(k))

        def reach(hops):
            return jnp.clip(me + hops * stride, 0, n - 1)

        def pair_copy(g):
            return remote(
                to_pair.at[rev, g], from_pair.at[rev, g], pair_send.at[rev, g], pair_recv.at[rev, g], reach(1))

        def next_copy(g, hops):
            return remote(
                to_next.at[rev, g], from_next.at[rev, g], next_send.at[rev, g, hops - 1], next_recv.at[rev, g],
                reach(hops))

        def plane_factor(first, h):
            return (factor(first, h) * factor(first + 1, h)) * (factor(first + 2, h) * factor(first + 3, h))

        def onward(g, value):
            to_next[rev, g] = value.astype(BF16)
            for hops in (1, 2):
                @pl.when(at + hops < planes)
                def _():
                    next_copy(g, hops).start()

        def h0(g):
            for k in (2, 3, 1):
                gather_copy(g, k, spot).start()

        def h1(g):
            gathered[rev, g, spot] = local[rev, g, spot]
            for k in range(1, 4):
                gather_copy(g, k, slot_of(k)).wait_recv()
            h = 4 * g + spot
            total = None
            for p in order:
                x = gathered[rev, g, p].astype(F32)
                total = x if total is None else factor(half_octet + p, h) * total + x
            plane_sum[rev, g] = total

            @pl.when(odd == 0)
            def _():
                to_pair[rev, g] = total.astype(BF16)
                pair_copy(g).start()

        def h2(g):
            @pl.when(odd == 1)
            def _():
                pair_copy(g).wait_recv()
                h = 4 * g + spot
                total = plane_factor(half_octet, h) * from_pair[rev, g].astype(F32) + plane_sum[rev, g]
                pair_sum[rev, g] = total

                @pl.when(at == 1)
                def _():
                    onward(g, total)

        def h3(g):
            @pl.when(at >= 2)
            def _():
                next_copy(g, 1).wait_recv()

            h = 4 * g + spot

            @pl.when(odd == 1)
            def _():
                mine, prior = plane_factor(half_octet, h), plane_factor(4 - half_octet, h)
                start = from_next[rev, g].astype(F32)

                @pl.when(at >= 3)
                def _():
                    onward(g, mine * prior * start + pair_sum[rev, g])

                entering[rev, g] = prior * start + from_pair[rev, g].astype(F32)

            @pl.when(odd == 0)
            def _():
                entering[rev, g] = from_next[rev, g].astype(F32)

            total = entering[rev, g]
            for i, p in enumerate(order):
                scattered[rev, g, p] = total.astype(BF16)
                if i < 3:
                    total = factor(half_octet + p, h) * total + gathered[rev, g, p].astype(F32)
            for k in (2, 3, 1):
                scatter_copy(g, k, spot).start()
            state[rev, g, spot] = scattered[rev, g, spot]

        def h5(g):
            for k in range(1, 4):
                scatter_copy(g, k, slot_of(k)).wait_recv()

        def finish(g):
            for k in range(1, 4):
                gather_copy(g, k, spot).wait_send()
                scatter_copy(g, k, spot).wait_send()

            @pl.when(odd == 0)
            def _():
                pair_copy(g).wait_send()

            @pl.when(odd == 1)
            def _():
                for hops in (1, 2):
                    @pl.when(at + hops < planes)
                    def _():
                        next_copy(g, hops).wait_send()

        wait = jnp.where(odd == 1, 2 + 3 * (at // 2), jnp.where(at == 0, 0, 3 * (at // 2) + 1))
        return 4 + wait, (h0, h1, h2, h3, h5), finish

    fore_at, fore, fore_finish = scan_steps(0)
    back_at, back, back_finish = scan_steps(1)

    half = heads // 2
    depth = 5 + 3 * (planes // 2 - 1)
    norm_base = max(depth + 6, 2 * groups)
    carry_base = norm_base + groups
    value_base = max(carry_base + groups, norm_base + depth + 5)
    ticks = value_base + groups

    def stage_back(p):
        pair(p, lambda h, j: back_work(p // 2, p % 2, h, j))

    def tick(i, carry):
        def at_tick(start, fn, stop=groups):
            g = i - start

            @pl.when((g >= 0) & (g < stop))
            def _():
                fn(g)

        at_tick(4, fore[1])
        at_tick(6, fore[2])
        at_tick(fore_at, fore[3])
        at_tick(norm_base, fore[4])
        at_tick(norm_base + 4, back[1])
        at_tick(norm_base + 6, back[2])
        at_tick(norm_base + back_at, back[3])
        at_tick(value_base, back[4])

        def stage_conv(g):
            group_work(g, conv_work)
            fore[0](g)

        def stage_part(g):
            for p in (2 * g, 2 * g + 1):
                @pl.when(p >= early_attn)
                def _():
                    pair(p, lambda h, j: attn_work(h))

                pair(p, lambda h, j: part_work(h))

        def stage_norm(g):
            group_work(g, norm_work)
            back[0](g)

        def stage_carry(g):
            group_work(g, carry_work)
            stage_back(g)

        def stage_value(g):
            group_work(g, value_work)

        at_tick(0, stage_conv)
        at_tick(groups, stage_part)

        @pl.when(i == norm_base)
        def _():
            load_up.wait()

        at_tick(norm_base, stage_norm)

        @pl.when(i == value_base)
        def _():
            send_terms()

        at_tick(carry_base, stage_carry)
        at_tick(value_base, stage_value)
        return carry

    def term_copy(peer, slot):
        return remote(term_row, terms_all.at[slot], term_send.at[peer], term_recv.at[slot], peer)

    def send_terms():
        row = fold_sums(0, 0)[0:1, :]
        last = (chunks - 1) * 128
        term_row[:, :last] = row[:, :last]
        term_row[:, last:] = jnp.concatenate(
            [row[:, last:], jnp.full((1, padded - channels), level.astype(F32))], axis=1)
        terms_all[me] = term_row[...]
        others(lambda peer: term_copy(peer, me).start())

    lax.fori_loop(0, ticks, tick, 0)

    def t1_copy(peer, slot):
        return remote(tap_rows.at[peer], tap_in.at[slot], t1_send.at[peer], t1_recv.at[slot], peer)

    def t2_copy(peer, slot):
        return remote(tap_own, tap_all.at[slot], t2_send.at[peer], t2_recv.at[slot], peer)

    shares = tap_rows.shape[1]
    tap_rows[...] = jnp.zeros(tap_rows.shape, F32)
    tap_sums = sum(fold_sums(t, t) for t in range(taps))
    for k in range(chunks):
        width = min(128, channels - k * 128)
        tap_rows[k % n, k // n, :, :width] = tap_sums[:, k * 128 : k * 128 + width]
    tap_in[me] = tap_rows[me]
    others(lambda peer: t1_copy(peer, me).start())
    edge_out[...] = mm(sel_first, opening[...], 1, 1).astype(BF16)

    @pl.when(me > 0)
    def _():
        edge_copy.start()

    def key_groups(start, stop):
        def go(g, c):
            group_work(g, key_work)
            return c

        lax.fori_loop(start, stop, go, 0)

    def late_back(p, c):
        stage_back(p)
        return c

    middle_back = (groups + half + 1) // 2
    lax.fori_loop(groups, middle_back, late_back, 0)
    others(lambda peer: t1_copy(peer, peer).wait_recv())
    tap_own[...] = jnp.sum(tap_in[...], axis=0) * (1.0 / n)
    tap_all[me] = tap_own[...]
    others(lambda peer: t2_copy(peer, me).start())
    lax.fori_loop(middle_back, half, late_back, 0)
    key_groups(0, groups)

    others(lambda peer: term_copy(peer, peer).wait_recv())

    def gather_row(b, c):
        terms_rows[pl.ds(b, 1), :] = terms_all[b]
        return c

    lax.fori_loop(0, n, gather_row, 0)
    wanted = terms_rows[:, channels : channels + 1]
    level_lane = lax.broadcasted_iota(jnp.int32, (n, 64), 1).astype(F32)
    chosen = jnp.where(level_lane == wanted, 1.0, 0.0)
    sums = lax.dot_general(
        chosen, terms_rows[:, :channels], (((0,), (0,)), ((), ())), precision=lax.Precision.HIGHEST,
        preferred_element_type=F32)[:levels]
    gain_sum[...] = (jnp.sum(sums * (1.0 + mod[...]), axis=0, keepdims=True) * (1.0 / n))[0]
    table_sum[...] = sums * gain * (1.0 / n)

    @pl.when(me < n - 1)
    def _():
        edge_copy.wait_recv()

    fix_row = lax.broadcasted_iota(jnp.int32, (16, span * 128), 0)
    fix_lane = lax.broadcasted_iota(jnp.int32, (16, span * 128), 1)
    ahead_by = fix_lane // 128 + 1
    sel_fix = ((fix_lane % 128 == 128 - ahead_by + fix_row) & (fix_row < ahead_by)).astype(F32).astype(BF16)
    key_part[:, 0 : span * 128] = mm(edge_in[...], sel_fix, 0, 0)

    def fix_work(h, j):
        c = lanes(h)
        tile = ending[c, :]
        for t in range(1, taps):
            tile = tile + columns[c, t * 128 : (t + 1) * 128] * key_part[c, (t - 1) * 128 : t * 128]
        grad_value[c, count - 128 :] = tile.astype(BF16)

    pairs(0, half, fix_work)

    others(lambda peer: t2_copy(peer, peer).wait_recv())
    for k in range(chunks):
        width = min(128, channels - k * 128)
        kernel_sum[:, k * 128 : k * 128 + width] = tap_all[k % n, k // n][:taps, :width]

    @pl.when(me < n - 1)
    def _():
        halo_copy.wait_send()

    @pl.when(me > 0)
    def _():
        edge_copy.wait_send()

    for k in range(1, 8):
        factor_copy(k, octet).wait_send()

    def finish_scan(g, c):
        fore_finish(g)
        back_finish(g)
        return c

    lax.fori_loop(0, groups, finish_scan, 0)

    def finish_peer(peer):
        term_copy(peer, me).wait_send()
        t1_copy(peer, me).wait_send()
        t2_copy(peer, me).wait_send()

    others(finish_peer)


def write_kernel(parts, *refs):
    sem = refs[-1]
    copies = [pltpu.make_async_copy(refs[i], refs[parts + i], sem.at[i]) for i in range(parts)]
    for copy in copies:
        copy.start()
    for copy in copies:
        copy.wait()


def body(
    queries,
    key_rows,
    value_rows,
    frame_len,
    log_decay,
    timestep,
    conv_kernel,
    norm_gain,
    mod_table,
    out_grad,
):
    shape = jax.ShapeDtypeStruct
    count, channels = queries.shape
    heads = log_decay.shape[2]
    dim = channels // heads
    taps = conv_kernel.shape[0]
    levels = mod_table.shape[0]
    n = lax.axis_size("seq")
    groups = heads // 4
    padded = -(-channels // 128) * 128
    chunks = padded // 128
    shares = -(-chunks // n)
    head_rows = -(-heads // 8) * 8

    vmem = pl.BlockSpec(memory_space=pltpu.VMEM)
    hbm = pl.BlockSpec(memory_space=pltpu.HBM)
    whole = (channels, count)
    tile = (dim, dim)
    per = lambda *lead, dtype=BF16: pltpu.VMEM(tuple(lead) + tile, dtype)
    table = pltpu.VMEM((head_rows, count), F32)
    dma = lambda *dims: pltpu.SemaphoreType.DMA(dims)
    outs = (
        shape(whole, BF16), shape(whole, BF16), shape(whole, BF16),
        shape((taps, channels), F32), shape((channels,), F32), shape((levels, channels), F32))
    results = pl.pallas_call(
        functools.partial(fused_kernel, n, heads, dim, count, taps, levels, 2),
        out_shape=outs,
        in_specs=[hbm] * 10,
        out_specs=(vmem,) * len(outs),
        scratch_shapes=[
            pltpu.SMEM(frame_len.shape, jnp.int32), pltpu.SMEM(log_decay.shape, F32), pltpu.SMEM((1,), jnp.int32),
            pltpu.VMEM(conv_kernel.shape, F32), pltpu.VMEM((channels,), F32),
            pltpu.VMEM(whole, BF16), pltpu.VMEM(whole, BF16), pltpu.VMEM(whole, BF16), pltpu.VMEM(whole, BF16),
            pltpu.VMEM((levels, channels), F32),
            pltpu.VMEM(whole, BF16),
            pltpu.VMEM((heads, count, count), BF16),
            pltpu.VMEM(whole, F32), pltpu.VMEM(whole, F32),
            pltpu.VMEM(whole, BF16),
            per(2, groups, 4), per(2, groups, 4), pltpu.VMEM((dim, count), BF16),
            per(2, groups, 4), per(2, groups, 4), per(2, groups), per(2, groups), per(2, groups), per(2, groups),
            per(2, groups, dtype=F32), per(2, groups, dtype=F32), per(2, groups, dtype=F32),
            pltpu.VMEM((8, head_rows, 128), F32),
            table, table, table, table, table, table,
            pltpu.VMEM((32, padded), BF16), pltpu.VMEM((padded, (taps + 1) * 128), F32),
            pltpu.VMEM((channels, 128), BF16),
            pltpu.VMEM((16, channels), BF16), pltpu.VMEM((16, channels), BF16),
            pltpu.VMEM((16, channels), BF16), pltpu.VMEM((16, channels), BF16),
            pltpu.VMEM((channels, 128), BF16), pltpu.VMEM((channels, 128), F32),
            pltpu.VMEM((taps, channels, 256), BF16),
            pltpu.VMEM((1, padded), F32), pltpu.VMEM((n, 1, padded), F32), pltpu.VMEM((n, padded), F32),
            pltpu.VMEM((n, shares, 8, 128), F32), pltpu.VMEM((n, shares, 8, 128), F32),
            pltpu.VMEM((shares, 8, 128), F32), pltpu.VMEM((n, shares, 8, 128), F32),
            dma(10), dma(2), dma(2), dma(8), dma(8), dma(2, groups, 4), dma(2, groups, 4),
            dma(2, groups, 4), dma(2, groups, 4), dma(2, groups), dma(2, groups), dma(2, groups, 2), dma(2, groups),
            dma(n), dma(n),
            dma(n), dma(n), dma(n), dma(n),
        ],
        compiler_params=pltpu.CompilerParams(
            collective_id=0, has_side_effects=True, vmem_limit_bytes=(46 << 20) + (n << 16)),
        name="fused",
    )(
        frame_len, log_decay, timestep, queries.T, key_rows.T, value_rows.T, out_grad.T, mod_table,
        conv_kernel, norm_gain)
    grad_query, grad_key, grad_value, kernel_sum, gain_sum, table_sum = pl.pallas_call(
        functools.partial(write_kernel, len(outs)),
        out_shape=outs,
        in_specs=[vmem] * len(outs),
        out_specs=(hbm,) * len(outs),
        scratch_shapes=[dma(len(outs))],
        compiler_params=pltpu.CompilerParams(vmem_limit_bytes=1 << 20),
        name="write",
    )(*results)
    return (grad_query.T, grad_key.T, grad_value.T, kernel_sum, gain_sum, table_sum)


def solution(mesh):
    in_specs = (
        P(("groups", "seq"), None),
        P(("groups", "seq"), None),
        P(("groups", "seq"), None),
        P(("groups", "seq"), None),
        P(("groups", "seq"), None, None),
        P(("groups", "seq")),
        P(),
        P(),
        P(),
        P(("groups", "seq"), None),
    )
    out_specs = (
        P(("groups", "seq"), None),
        P(("groups", "seq"), None),
        P(("groups", "seq"), None),
        P("groups", None),
        P("groups"),
        P("groups", None),
    )
    return jax.shard_map(body, mesh=mesh, in_specs=in_specs, out_specs=out_specs, check_vma=False)
```

```python
import functools

import jax
import jax.numpy as jnp
from jax import lax
from jax.experimental import pallas as pl
from jax.experimental.pallas import tpu as pltpu
from jax.sharding import PartitionSpec as P

EPSILON = 1e-06
MESH = pl.DeviceIdType.MESH
F32, BF16 = jnp.float32, jnp.bfloat16


def mm(a, b, ca, cb):
    return lax.dot_general(a, b, (((ca,), (cb,)), ((), ())), preferred_element_type=F32)


def fused_kernel(
    n, heads, dim, count, taps, levels,
    frame_hbm, decay_hbm, level_hbm, query_hbm, key_hbm, value_hbm, up_hbm, mod_hbm, taps_hbm, gain_hbm,
    query_out, key_out, value_out, kernel_out, gain_out, table_out,
    grad_query, grad_key, grad_value, kernel_sum, gain_sum, table_sum, frame_len, log_decay, timestep, conv_kernel, norm_gain, query, key, value, up, mod, conv, attn, part, key_part, grad, state, local, late_mask,
    gathered, scattered, to_pair, from_pair, to_next, from_next, plane_sum, pair_sum, entering,
    factors, e1_tab, rs_tab, ie_tab, we_tab, sc0_tab, sc1_tab, stack, columns, before,
    halo_out, halo_in, edge_out, edge_in, opening, ending, folds, term_row, terms_all, terms_rows,
    tap_rows, tap_in, tap_own, tap_all,
    load_sem, store_sem, halo_sem, edge_sem, f_send, f_recv, gather_send, gather_recv, scatter_send, scatter_recv,
    pair_send, pair_recv, next_send, next_recv, term_send, term_recv,
    t1_send, t1_recv, t2_send, t2_recv,
):
    groups = heads // 4
    planes = n // 4
    channels = heads * dim
    padded = stack.shape[1]
    chunks = padded // 128
    span = taps - 1
    scale = dim ** (-0.5)
    me = lax.axis_index("seq")
    video = lax.axis_index("groups")
    plane = me // 4
    spot, octet = me % 4, me % 8
    half_octet = octet - spot

    def dev(peer):
        return (video, peer)

    def remote(src, dst, send, recv, peer):
        return pltpu.make_async_remote_copy(
            src_ref=src, dst_ref=dst, send_sem=send, recv_sem=recv, device_id=dev(peer), device_id_type=MESH)

    def others(fn):
        def go(k, c):
            fn(lax.rem(me + k, n))
            return c

        lax.fori_loop(1, n, go, 0)

    barrier = pltpu.get_barrier_semaphore()
    others(lambda peer: pl.semaphore_signal(barrier, inc=1, device_id=dev(peer), device_id_type=MESH))
    loads = [
        pltpu.make_async_copy(src, dst, load_sem.at[i])
        for i, (src, dst) in enumerate(
            ((value_hbm, value), (frame_hbm, frame_len), (decay_hbm, log_decay), (level_hbm, timestep),
             (taps_hbm, conv_kernel), (gain_hbm, norm_gain), (mod_hbm, mod), (key_hbm, key), (query_hbm, query),
             (up_hbm, up)))
    ]
    for load in loads:
        load.start()
    load_value, load_key, load_query, load_up = loads[0], loads[7], loads[8], loads[9]
    small_loads = loads[1:7]
    outputs = [
        pltpu.make_async_copy(src, dst, store_sem.at[i])
        for i, (src, dst) in enumerate(
            ((grad_query, query_out), (grad_key, key_out), (grad_value, value_out), (kernel_sum, kernel_out),
             (gain_sum, gain_out), (table_sum, table_out)))
    ]

    sel_row = lax.broadcasted_iota(jnp.int32, (16, 128), 0)
    sel_lane = lax.broadcasted_iota(jnp.int32, (16, 128), 1)
    sel_last = ((sel_lane == sel_row + 128 - span) & (sel_row < span)).astype(F32).astype(BF16)
    sel_first = ((sel_lane == sel_row) & (sel_row < span)).astype(F32).astype(BF16)

    load_value.wait()
    halo_out[...] = mm(sel_last, value[:, count - 128 :], 1, 1).astype(BF16)

    @pl.when(me == 0)
    def _():
        halo_in[...] = jnp.zeros(halo_in.shape, BF16)

    @pl.when(me == n - 1)
    def _():
        edge_in[...] = jnp.zeros(edge_in.shape, BF16)

    @pl.when(plane < 2)
    def _():
        from_next[0] = jnp.zeros(from_next.shape[1:], BF16)

    @pl.when(plane >= planes - 2)
    def _():
        from_next[1] = jnp.zeros(from_next.shape[1:], BF16)

    pl.semaphore_wait(barrier, n - 1)

    halo_copy = remote(halo_out, halo_in, halo_sem.at[0], halo_sem.at[1], lax.rem(me + 1, n))
    edge_copy = remote(edge_out, edge_in, edge_sem.at[0], edge_sem.at[1], lax.rem(me + n - 1, n))

    @pl.when(me < n - 1)
    def _():
        halo_copy.start()

    for load in small_loads:
        load.wait()
    first = frame_len[0, 0]
    rows = e1_tab.shape[0]
    row_index = lax.broadcasted_iota(jnp.int32, (rows, count), 0)
    late = lax.broadcasted_iota(jnp.int32, (1, count), 1) >= first
    late_rows = lax.broadcasted_iota(jnp.int32, (rows, count), 1) >= first
    cum0 = jnp.zeros((rows, count), F32)
    cum1 = jnp.zeros((rows, count), F32)
    for h in range(heads):
        a = log_decay[0, 0, h]
        b = a + log_decay[0, 1, h]
        cum0 = jnp.where(row_index == h, a, cum0)
        cum1 = jnp.where(row_index == h, b, cum1)
    e1 = jnp.exp(cum1 - cum0)
    from0, from1 = scale * jnp.exp(cum0), scale * jnp.exp(cum1)
    e1_tab[...] = e1
    sc0_tab[...] = from0
    sc1_tab[...] = from1
    rs_tab[...] = jnp.where(late_rows, from1, from0)
    ie_tab[...] = jnp.where(late_rows, 1.0, e1)
    we_tab[...] = scale * jnp.where(late_rows, e1, 1.0)
    factors[octet] = jnp.exp(cum1)[:, :128]
    late_mask[...] = jnp.where(lax.broadcasted_iota(jnp.int32, (dim, count), 1) >= first, 1.0, 0.0).astype(BF16)

    def factor_copy(k, slot):
        peer = me - octet + lax.rem(octet + k, 8)
        return remote(factors.at[octet], factors.at[slot], f_send.at[k], f_recv.at[slot], peer)

    for k in range(1, 8):
        factor_copy(k, octet).start()

    level = timestep[0]
    gain = norm_gain[...][None, :]
    gain_row = gain * (1.0 + mod[pl.ds(level, 1), :])
    table = jnp.concatenate([conv_kernel[...], gain_row, jnp.zeros((8 - taps - 1, channels), F32)], axis=0)
    upper = table.astype(BF16).astype(F32)
    middle = (table - upper).astype(BF16).astype(F32)
    stack[:, 0:channels] = jnp.concatenate(
        [upper, middle, table - upper - middle, jnp.zeros((8, channels), F32)], axis=0).astype(BF16)
    stack[:, channels:] = jnp.zeros((32, padded - channels), BF16)
    row_of = lax.broadcasted_iota(jnp.int32, (32, (taps + 1) * 128), 0)
    tap_of = lax.broadcasted_iota(jnp.int32, (32, (taps + 1) * 128), 1) // 128
    spread = ((row_of % 8 == tap_of) & (row_of < 24)).astype(F32).astype(BF16)

    def spread_columns(k, c):
        at = pl.ds(pl.multiple_of(k * 128, 128), 128)
        columns[at, :] = mm(stack[:, at], spread, 0, 0)
        return c

    def spread_some(k, c):
        for j in range(6):
            spread_columns(k * 6 + j, c)
        return c

    lax.fori_loop(0, chunks // 6, spread_some, 0)
    for k in range(chunks // 6 * 6, chunks):
        spread_columns(k, 0)

    def column(strip, t):
        tile = columns[strip, t * 128 : (t + 1) * 128]
        return jnp.concatenate([tile] * (count // 128), axis=1)

    load_key.wait()
    load_query.wait()

    def lanes(h):
        return pl.ds(pl.multiple_of(h * dim, 16), dim)

    def weigh(product, h):
        rows_of = lax.broadcasted_iota(jnp.int32, (count, count), 0) >= first
        early = we_tab[pl.ds(h, 1), :]
        behind = jnp.where(late, scale, 0.0)
        return (product * jnp.where(rows_of, behind, early)).astype(BF16)

    def attn_work(h):
        c = lanes(h)
        attn[h] = weigh(mm(key[c, :], query[c, :], 0, 0), h)

    def pair(p, fn):
        fn(p * 2, 0)
        fn(p * 2 + 1, 1)

    def pairs(start, stop, fn):
        def go(p, c):
            pair(p, fn)
            return c

        lax.fori_loop(start, stop, go, 0)

    @pl.when(me > 0)
    def _():
        halo_copy.wait_recv()

    for k in range(1, 8):
        factor_copy(k, lax.rem(octet + k, 8)).wait_recv()
    before[...] = mm(halo_in[...], sel_last, 0, 0).astype(BF16)

    step = dim

    def strips(h):
        for r in range(0, dim, step):
            yield r, pl.ds(pl.multiple_of(h * dim + r, 16), step)

    def split_late(rows):
        second = rows * late_mask[...]
        return jnp.concatenate([rows - second, second], axis=0)

    def conv_work(g, i, h, j):
        c = lanes(h)
        for _, strip in strips(h):
            x = value[strip, :]
            joined = jnp.concatenate([before[strip, :], x], axis=1)
            total = column(strip, 0) * x.astype(F32)
            for t in range(1, taps):
                total = total + column(strip, t) * pltpu.roll(joined, t, 1)[:, 128:].astype(F32)
            conv[strip, :] = total.astype(BF16)
        outer = mm(split_late(conv[c, :]), key[c, :], 1, 1)
        local[0, g, 2 * i + j] = (e1_tab[pl.ds(h, 1), :][:, :dim] * outer[:dim] + outer[dim:]).astype(BF16)

    def part_work(h):
        c = lanes(h)
        part[c, :] = mm(conv[c, :], attn[h], 1, 0)

    def fold(t, strip, rows):
        total = sum(rows[:, k * 128 : (k + 1) * 128] for k in range(count // 128))
        upper = total.astype(BF16)
        folds[t, strip, 0:128] = upper
        folds[t, strip, 128:256] = (total - upper.astype(F32)).astype(BF16)

    def fold_sums(row, t):
        ones = (lax.broadcasted_iota(jnp.int32, (8, 256), 0) == row).astype(F32).astype(BF16)
        return mm(ones, folds[t], 1, 1)

    def norm_work(g, i, h, j):
        c = lanes(h)
        q = query[c, :]
        inter = mm(state[0, g, 2 * i + j], q, 1, 0)
        row_scale = rs_tab[pl.ds(h, 1), :]
        square = jnp.zeros((step, count), F32)
        cross = jnp.zeros((step, count), F32)
        for r, strip in strips(h):
            numerator = part[strip, :] + row_scale * inter[r : r + step]
            part[strip, :] = numerator
            square = square + numerator * numerator
            cross = cross + numerator * (up[strip, :].astype(F32) * column(strip, taps))
        square = jnp.sum(square, axis=0, keepdims=True) * (1.0 / dim)
        cross = jnp.sum(cross, axis=0, keepdims=True) * (1.0 / dim)
        inv_rms = lax.rsqrt(square + EPSILON)
        pull = inv_rms * (inv_rms * (inv_rms * cross))
        for _, strip in strips(h):
            numerator = part[strip, :]
            upstream = up[strip, :].astype(F32)
            terms = upstream * (numerator * inv_rms)
            fold(0, strip, terms)
            normed_grad = upstream * column(strip, taps)
            grad[strip, :] = (inv_rms * normed_grad - pull * numerator).astype(BF16)
        outer = mm(split_late(grad[c, :]), q, 1, 1)
        local[1, g, 2 * i + j] = (
            sc0_tab[pl.ds(h, 1), :][:, :dim] * outer[:dim] + sc1_tab[pl.ds(h, 1), :][:, :dim] * outer[dim:]
        ).astype(BF16)

    def back_work(g, i, h, j):
        c = lanes(h)
        q, k, gr = query[c, :], key[c, :], grad[c, :]
        score = weigh(mm(conv[c, :], gr, 0, 0), h)
        grad_query[c, :] = (
            mm(k, score, 1, 0) + rs_tab[pl.ds(h, 1), :] * mm(state[0, g, 2 * i + j], gr, 0, 0)
        ).astype(BF16)
        key_part[c, :] = mm(q, score, 1, 1)


    def carry_work(g, i, h, j):
        c = lanes(h)
        part[c, :] = mm(grad[c, :], attn[h], 1, 1)

    token = lax.broadcasted_iota(jnp.int32, (1, 128), 1)

    def value_work(g, i, h, j):
        c = lanes(h)
        inter = mm(state[1, g, 2 * i + j], key[c, :], 1, 0)
        into_end = ie_tab[pl.ds(h, 1), :]
        for r, strip in strips(h):
            own = part[strip, :] + into_end * inter[r : r + step]
            rounded = own.astype(BF16)
            opening[strip, :] = rounded[:, :128]
            x = value[strip, :].astype(F32)
            prior = before[strip, :]
            total = column(strip, 0) * own
            fold(0, strip, own * x)
            for t in range(1, taps):
                ahead = pltpu.roll(rounded, count - t, 1).astype(F32)
                ahead = jnp.concatenate(
                    [ahead[:, : count - 128], jnp.where(token < 128 - t, ahead[:, count - 128 :], 0.0)], axis=1)
                total = total + column(strip, t) * ahead
                edge = own[:, :128] * jnp.where(token < t, pltpu.roll(prior, t, 1).astype(F32), 0.0)
                product = ahead * x
                fold(t, strip, jnp.concatenate([product[:, :128] + edge, product[:, 128:]], axis=1))
            grad_value[strip, :] = total.astype(BF16)
            ending[strip, :] = total[:, count - 128 :]

    def key_work(g, i, h, j):
        c = lanes(h)
        grad_key[c, :] = (
            key_part[c, :] + ie_tab[pl.ds(h, 1), :] * mm(state[1, g, 2 * i + j], conv[c, :], 0, 0)
        ).astype(BF16)

    def group_work(g, fn):
        for i in range(2):
            for j in range(2):
                fn(g, i, 4 * g + 2 * i + j, j)

    def factor(slot, h):
        return factors[slot, pl.ds(h, 1), :][:, :dim]

    def scan_steps(rev):
        at = plane if rev == 0 else planes - 1 - plane
        odd = at % 2
        order = range(4) if rev == 0 else range(3, -1, -1)
        stride = 4 if rev == 0 else -4
        peer_of = lambda k: me - spot + lax.rem(spot + k, 4)
        slot_of = lambda k: lax.rem(spot + k, 4)

        def gather_copy(g, k, slot):
            return remote(
                local.at[rev, g, slot_of(k)], gathered.at[rev, g, slot],
                gather_send.at[rev, g, k], gather_recv.at[rev, g, slot], peer_of(k))

        def scatter_copy(g, k, slot):
            return remote(
                scattered.at[rev, g, slot_of(k)], state.at[rev, g, slot],
                scatter_send.at[rev, g, k], scatter_recv.at[rev, g, slot], peer_of(k))

        def reach(hops):
            return jnp.clip(me + hops * stride, 0, n - 1)

        def pair_copy(g):
            return remote(
                to_pair.at[rev, g], from_pair.at[rev, g], pair_send.at[rev, g], pair_recv.at[rev, g], reach(1))

        def next_copy(g, hops):
            return remote(
                to_next.at[rev, g], from_next.at[rev, g], next_send.at[rev, g, hops - 1], next_recv.at[rev, g],
                reach(hops))

        def plane_factor(first, h):
            return (factor(first, h) * factor(first + 1, h)) * (factor(first + 2, h) * factor(first + 3, h))

        def onward(g, value):
            to_next[rev, g] = value.astype(BF16)
            for hops in (1, 2):
                @pl.when(at + hops < planes)
                def _():
                    next_copy(g, hops).start()

        def h0(g):
            for k in (2, 3, 1):
                gather_copy(g, k, spot).start()

        def h1(g):
            gathered[rev, g, spot] = local[rev, g, spot]
            for k in range(1, 4):
                gather_copy(g, k, slot_of(k)).wait_recv()
            h = 4 * g + spot
            total = None
            for p in order:
                x = gathered[rev, g, p].astype(F32)
                total = x if total is None else factor(half_octet + p, h) * total + x
            plane_sum[rev, g] = total

            @pl.when(odd == 0)
            def _():
                to_pair[rev, g] = total.astype(BF16)
                pair_copy(g).start()

        def h2(g):
            @pl.when(odd == 1)
            def _():
                pair_copy(g).wait_recv()
                h = 4 * g + spot
                total = plane_factor(half_octet, h) * from_pair[rev, g].astype(F32) + plane_sum[rev, g]
                pair_sum[rev, g] = total

                @pl.when(at == 1)
                def _():
                    onward(g, total)

        def h3(g):
            @pl.when(at >= 2)
            def _():
                next_copy(g, 1).wait_recv()

            h = 4 * g + spot

            @pl.when(odd == 1)
            def _():
                mine, prior = plane_factor(half_octet, h), plane_factor(4 - half_octet, h)
                start = from_next[rev, g].astype(F32)

                @pl.when(at >= 3)
                def _():
                    onward(g, mine * prior * start + pair_sum[rev, g])

                entering[rev, g] = prior * start + from_pair[rev, g].astype(F32)

            @pl.when(odd == 0)
            def _():
                entering[rev, g] = from_next[rev, g].astype(F32)

            total = entering[rev, g]
            for i, p in enumerate(order):
                scattered[rev, g, p] = total.astype(BF16)
                if i < 3:
                    total = factor(half_octet + p, h) * total + gathered[rev, g, p].astype(F32)
            for k in (2, 3, 1):
                scatter_copy(g, k, spot).start()
            state[rev, g, spot] = scattered[rev, g, spot]

        def h5(g):
            for k in range(1, 4):
                scatter_copy(g, k, slot_of(k)).wait_recv()

        def finish(g):
            for k in range(1, 4):
                gather_copy(g, k, spot).wait_send()
                scatter_copy(g, k, spot).wait_send()

            @pl.when(odd == 0)
            def _():
                pair_copy(g).wait_send()

            @pl.when(odd == 1)
            def _():
                for hops in (1, 2):
                    @pl.when(at + hops < planes)
                    def _():
                        next_copy(g, hops).wait_send()

        wait = jnp.where(odd == 1, 2 + 3 * (at // 2), jnp.where(at == 0, 0, 3 * (at // 2) + 1))
        return 4 + wait, (h0, h1, h2, h3, h5), finish

    fore_at, fore, fore_finish = scan_steps(0)
    back_at, back, back_finish = scan_steps(1)

    half = heads // 2
    depth = 5 + 3 * (planes // 2 - 1)
    norm_base = max(depth + 6, 2 * groups)
    carry_base = norm_base + groups
    value_base = max(carry_base + groups, norm_base + depth + 5)
    ticks = value_base + groups

    def stage_back(p):
        pair(p, lambda h, j: back_work(p // 2, p % 2, h, j))

    def tick(i, carry):
        def at_tick(start, fn, stop=groups):
            g = i - start

            @pl.when((g >= 0) & (g < stop))
            def _():
                fn(g)

        at_tick(4, fore[1])
        at_tick(6, fore[2])
        at_tick(fore_at, fore[3])
        at_tick(norm_base, fore[4])
        at_tick(norm_base + 3, back[1])
        at_tick(norm_base + 5, back[2])
        at_tick(norm_base + back_at - 1, back[3])
        at_tick(value_base, back[4])

        def stage_conv(g):
            group_work(g, conv_work)
            fore[0](g)

        def stage_part(g):
            for i in range(4):
                attn_work(4 * g + i)
            for i in range(4):
                part_work(4 * g + i)

        def stage_norm(g):
            group_work(g, norm_work)
            back[0](g)

        def stage_carry(g):
            group_work(g, carry_work)
            stage_back(g)

        def stage_value(g):
            group_work(g, value_work)

        at_tick(0, stage_conv)
        at_tick(groups, stage_part)

        @pl.when(i == norm_base)
        def _():
            load_up.wait()

        at_tick(norm_base, stage_norm)

        @pl.when(i == value_base)
        def _():
            send_terms()

        at_tick(carry_base, stage_carry)
        at_tick(value_base, stage_value)
        return carry

    def term_copy(peer, slot):
        return remote(term_row, terms_all.at[slot], term_send.at[peer], term_recv.at[slot], peer)

    def send_terms():
        row = fold_sums(0, 0)[0:1, :]
        last = (chunks - 1) * 128
        term_row[:, :last] = row[:, :last]
        term_row[:, last:] = jnp.concatenate(
            [row[:, last:], jnp.full((1, padded - channels), level.astype(F32))], axis=1)
        terms_all[me] = term_row[...]
        others(lambda peer: term_copy(peer, me).start())

    lax.fori_loop(0, ticks, tick, 0)

    def t1_copy(peer, slot):
        return remote(tap_rows.at[peer], tap_in.at[slot], t1_send.at[peer], t1_recv.at[slot], peer)

    def t2_copy(peer, slot):
        return remote(tap_own, tap_all.at[slot], t2_send.at[peer], t2_recv.at[slot], peer)

    shares = tap_rows.shape[1]
    tap_rows[...] = jnp.zeros(tap_rows.shape, F32)
    tap_sums = sum(fold_sums(t, t) for t in range(taps))
    for k in range(chunks):
        width = min(128, channels - k * 128)
        tap_rows[k % n, k // n, :, :width] = tap_sums[:, k * 128 : k * 128 + width]
    tap_in[me] = tap_rows[me]
    others(lambda peer: t1_copy(peer, me).start())
    edge_out[...] = mm(sel_first, opening[...], 1, 1).astype(BF16)

    @pl.when(me > 0)
    def _():
        edge_copy.start()

    def key_groups(start, stop):
        def go(g, c):
            group_work(g, key_work)
            return c

        lax.fori_loop(start, stop, go, 0)

    middle_back = (groups + half + 1) // 2
    for p in range(groups, middle_back):
        stage_back(p)
    others(lambda peer: t1_copy(peer, peer).wait_recv())
    tap_own[...] = jnp.sum(tap_in[...], axis=0) * (1.0 / n)
    tap_all[me] = tap_own[...]
    others(lambda peer: t2_copy(peer, me).start())
    for p in range(middle_back, half):
        stage_back(p)
    outputs[0].start()
    key_groups(0, groups)
    outputs[1].start()

    others(lambda peer: term_copy(peer, peer).wait_recv())

    def gather_row(b, c):
        terms_rows[pl.ds(b, 1), :] = terms_all[b]
        return c

    lax.fori_loop(0, n, gather_row, 0)
    wanted = terms_rows[:, channels : channels + 1]
    level_lane = lax.broadcasted_iota(jnp.int32, (n, 64), 1).astype(F32)
    chosen = jnp.where(level_lane == wanted, 1.0, 0.0)
    sums = lax.dot_general(
        chosen, terms_rows[:, :channels], (((0,), (0,)), ((), ())), precision=lax.Precision.HIGHEST,
        preferred_element_type=F32)[:levels]
    gain_sum[...] = (jnp.sum(sums * (1.0 + mod[...]), axis=0, keepdims=True) * (1.0 / n))[0]
    table_sum[...] = sums * gain * (1.0 / n)
    outputs[4].start()
    outputs[5].start()

    @pl.when(me < n - 1)
    def _():
        edge_copy.wait_recv()

    fix_row = lax.broadcasted_iota(jnp.int32, (16, span * 128), 0)
    fix_lane = lax.broadcasted_iota(jnp.int32, (16, span * 128), 1)
    ahead_by = fix_lane // 128 + 1
    sel_fix = ((fix_lane % 128 == 128 - ahead_by + fix_row) & (fix_row < ahead_by)).astype(F32).astype(BF16)
    key_part[:, 0 : span * 128] = mm(edge_in[...], sel_fix, 0, 0)

    def fix_work(h, j):
        c = lanes(h)
        tile = ending[c, :]
        for t in range(1, taps):
            tile = tile + columns[c, t * 128 : (t + 1) * 128] * key_part[c, (t - 1) * 128 : t * 128]
        grad_value[c, count - 128 :] = tile.astype(BF16)

    pairs(0, half, fix_work)
    outputs[2].start()

    others(lambda peer: t2_copy(peer, peer).wait_recv())
    for k in range(chunks):
        width = min(128, channels - k * 128)
        kernel_sum[:, k * 128 : k * 128 + width] = tap_all[k % n, k // n][:taps, :width]
    outputs[3].start()

    @pl.when(me < n - 1)
    def _():
        halo_copy.wait_send()

    @pl.when(me > 0)
    def _():
        edge_copy.wait_send()

    for k in range(1, 8):
        factor_copy(k, octet).wait_send()

    def finish_scan(g, c):
        fore_finish(g)
        back_finish(g)
        return c

    lax.fori_loop(0, groups, finish_scan, 0)

    def finish_peer(peer):
        term_copy(peer, me).wait_send()
        t1_copy(peer, me).wait_send()
        t2_copy(peer, me).wait_send()

    others(finish_peer)
    for output in outputs:
        output.wait()


def write_kernel(parts, halves, *refs):
    sources, targets, held = refs[:parts], refs[parts : 2 * parts], refs[2 * parts : 3 * parts]
    into, out = refs[3 * parts :]
    pieces = []
    for i in range(parts):
        rows = sources[i].shape[0] // 2
        cuts = [pl.ds(0, rows), pl.ds(rows, rows)] if i < halves else [slice(None)]
        pieces += [(i, cut) for cut in cuts]
    view = lambda ref, cut: ref.at[cut] if not isinstance(cut, slice) else ref
    reads = [
        pltpu.make_async_copy(view(sources[i], cut), view(held[i], cut), into.at[k])
        for k, (i, cut) in enumerate(pieces)]
    writes = [
        pltpu.make_async_copy(view(held[i], cut), view(targets[i], cut), out.at[k])
        for k, (i, cut) in enumerate(pieces)]
    for read in reads:
        read.start()
    for read, write in zip(reads, writes):
        read.wait()
        write.start()
    for write in writes:
        write.wait()


def body(
    queries,
    key_rows,
    value_rows,
    frame_len,
    log_decay,
    timestep,
    conv_kernel,
    norm_gain,
    mod_table,
    out_grad,
):
    shape = jax.ShapeDtypeStruct
    count, channels = queries.shape
    heads = log_decay.shape[2]
    dim = channels // heads
    taps = conv_kernel.shape[0]
    levels = mod_table.shape[0]
    n = lax.axis_size("seq")
    groups = heads // 4
    padded = -(-channels // 128) * 128
    chunks = padded // 128
    shares = -(-chunks // n)
    head_rows = -(-heads // 8) * 8

    vmem = pl.BlockSpec(memory_space=pltpu.VMEM)
    hbm = pl.BlockSpec(memory_space=pltpu.HBM)
    whole = (channels, count)
    tile = (dim, dim)
    per = lambda *lead, dtype=BF16: pltpu.VMEM(tuple(lead) + tile, dtype)
    table = pltpu.VMEM((head_rows, count), F32)
    dma = lambda *dims: pltpu.SemaphoreType.DMA(dims)
    outs = (
        shape(whole, BF16), shape(whole, BF16), shape(whole, BF16),
        shape((taps, channels), F32), shape((channels,), F32), shape((levels, channels), F32))
    results = pl.pallas_call(
        functools.partial(fused_kernel, n, heads, dim, count, taps, levels),
        out_shape=outs,
        in_specs=[hbm] * 10,
        out_specs=(hbm,) * len(outs),
        scratch_shapes=[
            *(pltpu.VMEM(o.shape, o.dtype) for o in outs),
            pltpu.SMEM(frame_len.shape, jnp.int32), pltpu.SMEM(log_decay.shape, F32), pltpu.SMEM((1,), jnp.int32),
            pltpu.VMEM(conv_kernel.shape, F32), pltpu.VMEM((channels,), F32),
            pltpu.VMEM(whole, BF16), pltpu.VMEM(whole, BF16), pltpu.VMEM(whole, BF16), pltpu.VMEM(whole, BF16),
            pltpu.VMEM((levels, channels), F32),
            pltpu.VMEM(whole, BF16),
            pltpu.VMEM((heads, count, count), BF16),
            pltpu.VMEM(whole, F32), pltpu.VMEM(whole, F32),
            pltpu.VMEM(whole, BF16),
            per(2, groups, 4), per(2, groups, 4), pltpu.VMEM((dim, count), BF16),
            per(2, groups, 4), per(2, groups, 4), per(2, groups), per(2, groups), per(2, groups), per(2, groups),
            per(2, groups, dtype=F32), per(2, groups, dtype=F32), per(2, groups, dtype=F32),
            pltpu.VMEM((8, head_rows, 128), F32),
            table, table, table, table, table, table,
            pltpu.VMEM((32, padded), BF16), pltpu.VMEM((padded, (taps + 1) * 128), F32),
            pltpu.VMEM((channels, 128), BF16),
            pltpu.VMEM((16, channels), BF16), pltpu.VMEM((16, channels), BF16),
            pltpu.VMEM((16, channels), BF16), pltpu.VMEM((16, channels), BF16),
            pltpu.VMEM((channels, 128), BF16), pltpu.VMEM((channels, 128), F32),
            pltpu.VMEM((taps, channels, 256), BF16),
            pltpu.VMEM((1, padded), F32), pltpu.VMEM((n, 1, padded), F32), pltpu.VMEM((n, padded), F32),
            pltpu.VMEM((n, shares, 8, 128), F32), pltpu.VMEM((n, shares, 8, 128), F32),
            pltpu.VMEM((shares, 8, 128), F32), pltpu.VMEM((n, shares, 8, 128), F32),
            dma(10), dma(len(outs)), dma(2), dma(2), dma(8), dma(8), dma(2, groups, 4), dma(2, groups, 4),
            dma(2, groups, 4), dma(2, groups, 4), dma(2, groups), dma(2, groups), dma(2, groups, 2), dma(2, groups),
            dma(n), dma(n),
            dma(n), dma(n), dma(n), dma(n),
        ],
        compiler_params=pltpu.CompilerParams(
            collective_id=0, has_side_effects=True, vmem_limit_bytes=60 << 20),
        name="fused",
    )(
        frame_len, log_decay, timestep, queries.T, key_rows.T, value_rows.T, out_grad.T, mod_table,
        conv_kernel, norm_gain)
    grad_query, grad_key, grad_value, kernel_sum, gain_sum, table_sum = pl.pallas_call(
        functools.partial(write_kernel, len(outs), 3),
        out_shape=outs,
        in_specs=[hbm] * len(outs),
        out_specs=(hbm,) * len(outs),
        scratch_shapes=[*(pltpu.VMEM(o.shape, o.dtype) for o in outs), dma(len(outs) + 3), dma(len(outs) + 3)],
        compiler_params=pltpu.CompilerParams(vmem_limit_bytes=60 << 20),
        name="write",
    )(*results)
    return (grad_query.T, grad_key.T, grad_value.T, kernel_sum, gain_sum, table_sum)


def solution(mesh):
    in_specs = (
        P(("groups", "seq"), None),
        P(("groups", "seq"), None),
        P(("groups", "seq"), None),
        P(("groups", "seq"), None),
        P(("groups", "seq"), None, None),
        P(("groups", "seq")),
        P(),
        P(),
        P(),
        P(("groups", "seq"), None),
    )
    out_specs = (
        P(("groups", "seq"), None),
        P(("groups", "seq"), None),
        P(("groups", "seq"), None),
        P("groups", None),
        P("groups"),
        P("groups", None),
    )
    return jax.shard_map(body, mesh=mesh, in_specs=in_specs, out_specs=out_specs, check_vma=False)
```

```python
import functools

import jax
import jax.numpy as jnp
from jax import lax
from jax.experimental import pallas as pl
from jax.experimental.pallas import tpu as pltpu
from jax.sharding import PartitionSpec as P

EPSILON = 1e-06
MESH = pl.DeviceIdType.MESH
F32, BF16 = jnp.float32, jnp.bfloat16


def mm(a, b, ca, cb):
    return lax.dot_general(a, b, (((ca,), (cb,)), ((), ())), preferred_element_type=F32)


def fused_kernel(
    n, heads, dim, count, taps, levels,
    frame_hbm, decay_hbm, level_hbm, query_hbm, key_hbm, value_hbm, up_hbm, mod_hbm, taps_hbm, gain_hbm,
    query_out, key_out, value_out, kernel_out, gain_out, table_out,
    grad_query, grad_key, grad_value, kernel_sum, gain_sum, table_sum, frame_len, log_decay, timestep, conv_kernel, norm_gain, query, key, value, up, mod, conv, attn, part, key_part, grad, state, local, late_mask,
    gathered, scattered, to_pair, from_pair, to_next, from_next, plane_sum, pair_sum, entering,
    factors, e1_tab, rs_tab, ie_tab, we_tab, sc0_tab, sc1_tab, stack, columns, before,
    halo_out, halo_in, edge_out, edge_in, opening, ending, folds, term_row, terms_all, terms_rows,
    tap_rows, tap_in, tap_own, tap_all,
    load_sem, store_sem, halo_sem, edge_sem, f_send, f_recv, gather_send, gather_recv, scatter_send, scatter_recv,
    pair_send, pair_recv, next_send, next_recv, term_send, term_recv,
    t1_send, t1_recv, t2_send, t2_recv,
):
    groups = heads // 4
    planes = n // 4
    channels = heads * dim
    padded = stack.shape[1]
    chunks = padded // 128
    span = taps - 1
    scale = dim ** (-0.5)
    me = lax.axis_index("seq")
    video = lax.axis_index("groups")
    plane = me // 4
    spot, octet = me % 4, me % 8
    half_octet = octet - spot

    def dev(peer):
        return (video, peer)

    def remote(src, dst, send, recv, peer):
        return pltpu.make_async_remote_copy(
            src_ref=src, dst_ref=dst, send_sem=send, recv_sem=recv, device_id=dev(peer), device_id_type=MESH)

    def others(fn):
        def go(k, c):
            fn(lax.rem(me + k, n))
            return c

        lax.fori_loop(1, n, go, 0)

    barrier = pltpu.get_barrier_semaphore()
    others(lambda peer: pl.semaphore_signal(barrier, inc=1, device_id=dev(peer), device_id_type=MESH))
    loads = [
        pltpu.make_async_copy(src, dst, load_sem.at[i])
        for i, (src, dst) in enumerate(
            ((value_hbm, value), (frame_hbm, frame_len), (decay_hbm, log_decay), (level_hbm, timestep),
             (taps_hbm, conv_kernel), (gain_hbm, norm_gain), (mod_hbm, mod), (key_hbm, key), (query_hbm, query),
             (up_hbm, up)))
    ]
    for load in loads:
        load.start()
    load_value, load_key, load_query, load_up = loads[0], loads[7], loads[8], loads[9]
    small_loads = loads[1:7]
    outputs = [
        pltpu.make_async_copy(src, dst, store_sem.at[i])
        for i, (src, dst) in enumerate(
            ((grad_query, query_out), (grad_key, key_out), (grad_value, value_out), (kernel_sum, kernel_out),
             (gain_sum, gain_out), (table_sum, table_out)))
    ]

    sel_row = lax.broadcasted_iota(jnp.int32, (16, 128), 0)
    sel_lane = lax.broadcasted_iota(jnp.int32, (16, 128), 1)
    sel_last = ((sel_lane == sel_row + 128 - span) & (sel_row < span)).astype(F32).astype(BF16)
    sel_first = ((sel_lane == sel_row) & (sel_row < span)).astype(F32).astype(BF16)

    load_value.wait()
    halo_out[...] = mm(sel_last, value[:, count - 128 :], 1, 1).astype(BF16)

    @pl.when(me == 0)
    def _():
        halo_in[...] = jnp.zeros(halo_in.shape, BF16)

    @pl.when(me == n - 1)
    def _():
        edge_in[...] = jnp.zeros(edge_in.shape, BF16)

    @pl.when(plane < 2)
    def _():
        from_next[0] = jnp.zeros(from_next.shape[1:], BF16)

    @pl.when(plane >= planes - 2)
    def _():
        from_next[1] = jnp.zeros(from_next.shape[1:], BF16)

    pl.semaphore_wait(barrier, n - 1)

    halo_copy = remote(halo_out, halo_in, halo_sem.at[0], halo_sem.at[1], lax.rem(me + 1, n))
    edge_copy = remote(edge_out, edge_in, edge_sem.at[0], edge_sem.at[1], lax.rem(me + n - 1, n))

    @pl.when(me < n - 1)
    def _():
        halo_copy.start()

    for load in small_loads:
        load.wait()
    first = frame_len[0, 0]
    rows = e1_tab.shape[0]
    row_index = lax.broadcasted_iota(jnp.int32, (rows, count), 0)
    late = lax.broadcasted_iota(jnp.int32, (1, count), 1) >= first
    late_rows = lax.broadcasted_iota(jnp.int32, (rows, count), 1) >= first
    cum0 = jnp.zeros((rows, count), F32)
    cum1 = jnp.zeros((rows, count), F32)
    for h in range(heads):
        a = log_decay[0, 0, h]
        b = a + log_decay[0, 1, h]
        cum0 = jnp.where(row_index == h, a, cum0)
        cum1 = jnp.where(row_index == h, b, cum1)
    e1 = jnp.exp(cum1 - cum0)
    from0, from1 = scale * jnp.exp(cum0), scale * jnp.exp(cum1)
    e1_tab[...] = e1
    sc0_tab[...] = from0
    sc1_tab[...] = from1
    rs_tab[...] = jnp.where(late_rows, from1, from0)
    ie_tab[...] = jnp.where(late_rows, 1.0, e1)
    we_tab[...] = scale * jnp.where(late_rows, e1, 1.0)
    factors[octet] = jnp.exp(cum1)[:, :128]
    late_mask[...] = jnp.where(lax.broadcasted_iota(jnp.int32, (dim, count), 1) >= first, 1.0, 0.0).astype(BF16)

    def factor_copy(k, slot):
        peer = me - octet + lax.rem(octet + k, 8)
        return remote(factors.at[octet], factors.at[slot], f_send.at[k], f_recv.at[slot], peer)

    for k in range(1, 8):
        factor_copy(k, octet).start()

    level = timestep[0]
    gain = norm_gain[...][None, :]
    gain_row = gain * (1.0 + mod[pl.ds(level, 1), :])
    table = jnp.concatenate([conv_kernel[...], gain_row, jnp.zeros((8 - taps - 1, channels), F32)], axis=0)
    upper = table.astype(BF16).astype(F32)
    middle = (table - upper).astype(BF16).astype(F32)
    stack[:, 0:channels] = jnp.concatenate(
        [upper, middle, table - upper - middle, jnp.zeros((8, channels), F32)], axis=0).astype(BF16)
    stack[:, channels:] = jnp.zeros((32, padded - channels), BF16)
    row_of = lax.broadcasted_iota(jnp.int32, (32, (taps + 1) * 128), 0)
    tap_of = lax.broadcasted_iota(jnp.int32, (32, (taps + 1) * 128), 1) // 128
    spread = ((row_of % 8 == tap_of) & (row_of < 24)).astype(F32).astype(BF16)

    def spread_columns(k, c):
        at = pl.ds(pl.multiple_of(k * 128, 128), 128)
        columns[at, :] = mm(stack[:, at], spread, 0, 0)
        return c

    def spread_some(k, c):
        for j in range(6):
            spread_columns(k * 6 + j, c)
        return c

    lax.fori_loop(0, chunks // 6, spread_some, 0)
    for k in range(chunks // 6 * 6, chunks):
        spread_columns(k, 0)

    def column(strip, t):
        tile = columns[strip, t * 128 : (t + 1) * 128]
        return jnp.concatenate([tile] * (count // 128), axis=1)

    load_key.wait()
    load_query.wait()

    def lanes(h):
        return pl.ds(pl.multiple_of(h * dim, 16), dim)

    def weigh(product, h):
        rows_of = lax.broadcasted_iota(jnp.int32, (count, count), 0) >= first
        early = we_tab[pl.ds(h, 1), :]
        behind = jnp.where(late, scale, 0.0)
        return (product * jnp.where(rows_of, behind, early)).astype(BF16)

    def attn_work(h):
        c = lanes(h)
        attn[h] = weigh(mm(key[c, :], query[c, :], 0, 0), h)

    def pair(p, fn):
        fn(p * 2, 0)
        fn(p * 2 + 1, 1)

    def pairs(start, stop, fn):
        def go(p, c):
            pair(p, fn)
            return c

        lax.fori_loop(start, stop, go, 0)

    @pl.when(me > 0)
    def _():
        halo_copy.wait_recv()

    for k in range(1, 8):
        factor_copy(k, lax.rem(octet + k, 8)).wait_recv()
    before[...] = mm(halo_in[...], sel_last, 0, 0).astype(BF16)

    step = dim

    def strips(h):
        for r in range(0, dim, step):
            yield r, pl.ds(pl.multiple_of(h * dim + r, 16), step)

    def split_late(rows):
        second = rows * late_mask[...]
        return jnp.concatenate([rows - second, second], axis=0)

    def conv_work(g, i, h, j):
        c = lanes(h)
        for _, strip in strips(h):
            x = value[strip, :]
            joined = jnp.concatenate([before[strip, :], x], axis=1)
            total = column(strip, 0) * x.astype(F32)
            for t in range(1, taps):
                total = total + column(strip, t) * pltpu.roll(joined, t, 1)[:, 128:].astype(F32)
            conv[strip, :] = total.astype(BF16)
        outer = mm(split_late(conv[c, :]), key[c, :], 1, 1)
        local[0, g, 2 * i + j] = (e1_tab[pl.ds(h, 1), :][:, :dim] * outer[:dim] + outer[dim:]).astype(BF16)

    def part_work(h):
        c = lanes(h)
        part[c, :] = mm(conv[c, :], attn[h], 1, 0)

    def fold(t, strip, rows):
        total = sum(rows[:, k * 128 : (k + 1) * 128] for k in range(count // 128))
        upper = total.astype(BF16)
        folds[t, strip, 0:128] = upper
        folds[t, strip, 128:256] = (total - upper.astype(F32)).astype(BF16)

    def fold_sums(row, t):
        ones = (lax.broadcasted_iota(jnp.int32, (8, 256), 0) == row).astype(F32).astype(BF16)
        return mm(ones, folds[t], 1, 1)

    def norm_work(g, i, h, j):
        c = lanes(h)
        q = query[c, :]
        inter = mm(state[0, g, 2 * i + j], q, 1, 0)
        row_scale = rs_tab[pl.ds(h, 1), :]
        square = jnp.zeros((step, count), F32)
        cross = jnp.zeros((step, count), F32)
        for r, strip in strips(h):
            numerator = part[strip, :] + row_scale * inter[r : r + step]
            part[strip, :] = numerator
            square = square + numerator * numerator
            cross = cross + numerator * (up[strip, :].astype(F32) * column(strip, taps))
        square = jnp.sum(square, axis=0, keepdims=True) * (1.0 / dim)
        cross = jnp.sum(cross, axis=0, keepdims=True) * (1.0 / dim)
        inv_rms = lax.rsqrt(square + EPSILON)
        pull = inv_rms * (inv_rms * (inv_rms * cross))
        for _, strip in strips(h):
            numerator = part[strip, :]
            upstream = up[strip, :].astype(F32)
            terms = upstream * (numerator * inv_rms)
            fold(0, strip, terms)
            normed_grad = upstream * column(strip, taps)
            grad[strip, :] = (inv_rms * normed_grad - pull * numerator).astype(BF16)
        outer = mm(split_late(grad[c, :]), q, 1, 1)
        local[1, g, 2 * i + j] = (
            sc0_tab[pl.ds(h, 1), :][:, :dim] * outer[:dim] + sc1_tab[pl.ds(h, 1), :][:, :dim] * outer[dim:]
        ).astype(BF16)

    def back_work(g, i, h, j):
        c = lanes(h)
        q, k, gr = query[c, :], key[c, :], grad[c, :]
        score = weigh(mm(conv[c, :], gr, 0, 0), h)
        grad_query[c, :] = (
            mm(k, score, 1, 0) + rs_tab[pl.ds(h, 1), :] * mm(state[0, g, 2 * i + j], gr, 0, 0)
        ).astype(BF16)
        key_part[c, :] = mm(q, score, 1, 1)


    def carry_work(g, i, h, j):
        c = lanes(h)
        part[c, :] = mm(grad[c, :], attn[h], 1, 1)

    token = lax.broadcasted_iota(jnp.int32, (1, 128), 1)

    def value_work(g, i, h, j):
        c = lanes(h)
        inter = mm(state[1, g, 2 * i + j], key[c, :], 1, 0)
        into_end = ie_tab[pl.ds(h, 1), :]
        for r, strip in strips(h):
            own = part[strip, :] + into_end * inter[r : r + step]
            rounded = own.astype(BF16)
            opening[strip, :] = rounded[:, :128]
            x = value[strip, :].astype(F32)
            prior = before[strip, :]
            total = column(strip, 0) * own
            fold(0, strip, own * x)
            for t in range(1, taps):
                ahead = pltpu.roll(rounded, count - t, 1).astype(F32)
                ahead = jnp.concatenate(
                    [ahead[:, : count - 128], jnp.where(token < 128 - t, ahead[:, count - 128 :], 0.0)], axis=1)
                total = total + column(strip, t) * ahead
                edge = own[:, :128] * jnp.where(token < t, pltpu.roll(prior, t, 1).astype(F32), 0.0)
                product = ahead * x
                fold(t, strip, jnp.concatenate([product[:, :128] + edge, product[:, 128:]], axis=1))
            grad_value[strip, :] = total.astype(BF16)
            ending[strip, :] = total[:, count - 128 :]

    def key_work(g, i, h, j):
        c = lanes(h)
        grad_key[c, :] = (
            key_part[c, :] + ie_tab[pl.ds(h, 1), :] * mm(state[1, g, 2 * i + j], conv[c, :], 0, 0)
        ).astype(BF16)

    def group_work(g, fn):
        for i in range(2):
            for j in range(2):
                fn(g, i, 4 * g + 2 * i + j, j)

    def factor(slot, h):
        return factors[slot, pl.ds(h, 1), :][:, :dim]

    def scan_steps(rev):
        at = plane if rev == 0 else planes - 1 - plane
        odd = at % 2
        order = range(4) if rev == 0 else range(3, -1, -1)
        stride = 4 if rev == 0 else -4
        peer_of = lambda k: me - spot + lax.rem(spot + k, 4)
        slot_of = lambda k: lax.rem(spot + k, 4)

        def gather_copy(g, k, slot):
            return remote(
                local.at[rev, g, slot_of(k)], gathered.at[rev, g, slot],
                gather_send.at[rev, g, k], gather_recv.at[rev, g, slot], peer_of(k))

        def scatter_copy(g, k, slot):
            return remote(
                scattered.at[rev, g, slot_of(k)], state.at[rev, g, slot],
                scatter_send.at[rev, g, k], scatter_recv.at[rev, g, slot], peer_of(k))

        def reach(hops):
            return jnp.clip(me + hops * stride, 0, n - 1)

        def pair_copy(g):
            return remote(
                to_pair.at[rev, g], from_pair.at[rev, g], pair_send.at[rev, g], pair_recv.at[rev, g], reach(1))

        def next_copy(g, hops):
            return remote(
                to_next.at[rev, g], from_next.at[rev, g], next_send.at[rev, g, hops - 1], next_recv.at[rev, g],
                reach(hops))

        def plane_factor(first, h):
            return (factor(first, h) * factor(first + 1, h)) * (factor(first + 2, h) * factor(first + 3, h))

        def onward(g, value):
            to_next[rev, g] = value.astype(BF16)
            for hops in (1, 2):
                @pl.when(at + hops < planes)
                def _():
                    next_copy(g, hops).start()

        def h0(g):
            for k in (2, 3, 1):
                gather_copy(g, k, spot).start()

        def h1(g):
            gathered[rev, g, spot] = local[rev, g, spot]
            for k in range(1, 4):
                gather_copy(g, k, slot_of(k)).wait_recv()
            h = 4 * g + spot
            total = None
            for p in order:
                x = gathered[rev, g, p].astype(F32)
                total = x if total is None else factor(half_octet + p, h) * total + x
            plane_sum[rev, g] = total

            @pl.when(odd == 0)
            def _():
                to_pair[rev, g] = total.astype(BF16)
                pair_copy(g).start()

        def h2(g):
            @pl.when(odd == 1)
            def _():
                pair_copy(g).wait_recv()
                h = 4 * g + spot
                total = plane_factor(half_octet, h) * from_pair[rev, g].astype(F32) + plane_sum[rev, g]
                pair_sum[rev, g] = total

                @pl.when(at == 1)
                def _():
                    onward(g, total)

        def h3(g):
            @pl.when(at >= 2)
            def _():
                next_copy(g, 1).wait_recv()

            h = 4 * g + spot

            @pl.when(odd == 1)
            def _():
                mine, prior = plane_factor(half_octet, h), plane_factor(4 - half_octet, h)
                start = from_next[rev, g].astype(F32)

                @pl.when(at >= 3)
                def _():
                    onward(g, mine * prior * start + pair_sum[rev, g])

                entering[rev, g] = prior * start + from_pair[rev, g].astype(F32)

            @pl.when(odd == 0)
            def _():
                entering[rev, g] = from_next[rev, g].astype(F32)

            total = entering[rev, g]
            for i, p in enumerate(order):
                scattered[rev, g, p] = total.astype(BF16)
                if i < 3:
                    total = factor(half_octet + p, h) * total + gathered[rev, g, p].astype(F32)
            for k in (2, 3, 1):
                scatter_copy(g, k, spot).start()
            state[rev, g, spot] = scattered[rev, g, spot]

        def h5(g):
            for k in range(1, 4):
                scatter_copy(g, k, slot_of(k)).wait_recv()

        def finish(g):
            for k in range(1, 4):
                gather_copy(g, k, spot).wait_send()
                scatter_copy(g, k, spot).wait_send()

            @pl.when(odd == 0)
            def _():
                pair_copy(g).wait_send()

            @pl.when(odd == 1)
            def _():
                for hops in (1, 2):
                    @pl.when(at + hops < planes)
                    def _():
                        next_copy(g, hops).wait_send()

        wait = jnp.where(odd == 1, 2 + 3 * (at // 2), jnp.where(at == 0, 0, 3 * (at // 2) + 1))
        return 4 + wait, (h0, h1, h2, h3, h5), finish

    fore_at, fore, fore_finish = scan_steps(0)
    back_at, back, back_finish = scan_steps(1)

    half = heads // 2
    depth = 5 + 3 * (planes // 2 - 1)
    norm_base = max(depth + 7, 2 * groups + 1)
    carry_base = norm_base + groups
    value_base = max(carry_base + groups, norm_base + depth + 5)
    ticks = value_base + groups

    def stage_back(p):
        pair(p, lambda h, j: back_work(p // 2, p % 2, h, j))

    def tick(i, carry):
        def at_tick(start, fn, stop=groups):
            g = i - start

            @pl.when((g >= 0) & (g < stop))
            def _():
                fn(g)

        at_tick(5, fore[1])
        at_tick(7, fore[2])
        at_tick(fore_at + 1, fore[3])
        at_tick(norm_base, fore[4])
        at_tick(norm_base + 3, back[1])
        at_tick(norm_base + 5, back[2])
        at_tick(norm_base + back_at - 1, back[3])
        at_tick(value_base, back[4])

        def stage_conv(g):
            group_work(g, conv_work)
            fore[0](g)

        def stage_part(g):
            for i in range(4):
                attn_work(4 * g + i)
            for i in range(4):
                part_work(4 * g + i)

        def stage_norm(g):
            group_work(g, norm_work)
            back[0](g)

        def stage_carry(g):
            group_work(g, carry_work)
            stage_back(g)

        def stage_value(g):
            group_work(g, value_work)

        at_tick(0, stage_conv)
        at_tick(groups, stage_part)

        @pl.when(i == norm_base)
        def _():
            load_up.wait()

        at_tick(norm_base, stage_norm)

        @pl.when(i == value_base)
        def _():
            send_terms()

        at_tick(carry_base, stage_carry)
        at_tick(value_base, stage_value)
        return carry

    def term_copy(peer, slot):
        return remote(term_row, terms_all.at[slot], term_send.at[peer], term_recv.at[slot], peer)

    def send_terms():
        row = fold_sums(0, 0)[0:1, :]
        last = (chunks - 1) * 128
        term_row[:, :last] = row[:, :last]
        term_row[:, last:] = jnp.concatenate(
            [row[:, last:], jnp.full((1, padded - channels), level.astype(F32))], axis=1)
        terms_all[me] = term_row[...]
        others(lambda peer: term_copy(peer, me).start())

    lax.fori_loop(0, ticks, tick, 0)

    def t1_copy(peer, slot):
        return remote(tap_rows.at[peer], tap_in.at[slot], t1_send.at[peer], t1_recv.at[slot], peer)

    def t2_copy(peer, slot):
        return remote(tap_own, tap_all.at[slot], t2_send.at[peer], t2_recv.at[slot], peer)

    shares = tap_rows.shape[1]
    tap_rows[...] = jnp.zeros(tap_rows.shape, F32)
    tap_sums = sum(fold_sums(t, t) for t in range(taps))
    for k in range(chunks):
        width = min(128, channels - k * 128)
        tap_rows[k % n, k // n, :, :width] = tap_sums[:, k * 128 : k * 128 + width]
    tap_in[me] = tap_rows[me]
    others(lambda peer: t1_copy(peer, me).start())
    edge_out[...] = mm(sel_first, opening[...], 1, 1).astype(BF16)

    @pl.when(me > 0)
    def _():
        edge_copy.start()

    def key_groups(start, stop):
        def go(g, c):
            group_work(g, key_work)
            return c

        lax.fori_loop(start, stop, go, 0)

    middle_back = (groups + half + 1) // 2
    for p in range(groups, middle_back):
        stage_back(p)
    others(lambda peer: t1_copy(peer, peer).wait_recv())
    tap_own[...] = jnp.sum(tap_in[...], axis=0) * (1.0 / n)
    tap_all[me] = tap_own[...]
    others(lambda peer: t2_copy(peer, me).start())
    for p in range(middle_back, half):
        stage_back(p)
    outputs[0].start()
    key_groups(0, groups)
    outputs[1].start()

    others(lambda peer: term_copy(peer, peer).wait_recv())

    def gather_row(b, c):
        terms_rows[pl.ds(b, 1), :] = terms_all[b]
        return c

    lax.fori_loop(0, n, gather_row, 0)
    wanted = terms_rows[:, channels : channels + 1]
    level_lane = lax.broadcasted_iota(jnp.int32, (n, 64), 1).astype(F32)
    chosen = jnp.where(level_lane == wanted, 1.0, 0.0)
    sums = lax.dot_general(
        chosen, terms_rows[:, :channels], (((0,), (0,)), ((), ())), precision=lax.Precision.HIGHEST,
        preferred_element_type=F32)[:levels]
    gain_sum[...] = (jnp.sum(sums * (1.0 + mod[...]), axis=0, keepdims=True) * (1.0 / n))[0]
    table_sum[...] = sums * gain * (1.0 / n)
    outputs[4].start()
    outputs[5].start()

    @pl.when(me < n - 1)
    def _():
        edge_copy.wait_recv()

    fix_row = lax.broadcasted_iota(jnp.int32, (16, span * 128), 0)
    fix_lane = lax.broadcasted_iota(jnp.int32, (16, span * 128), 1)
    ahead_by = fix_lane // 128 + 1
    sel_fix = ((fix_lane % 128 == 128 - ahead_by + fix_row) & (fix_row < ahead_by)).astype(F32).astype(BF16)
    key_part[:, 0 : span * 128] = mm(edge_in[...], sel_fix, 0, 0)

    def fix_work(h, j):
        c = lanes(h)
        tile = ending[c, :]
        for t in range(1, taps):
            tile = tile + columns[c, t * 128 : (t + 1) * 128] * key_part[c, (t - 1) * 128 : t * 128]
        grad_value[c, count - 128 :] = tile.astype(BF16)

    pairs(0, half, fix_work)
    outputs[2].start()

    others(lambda peer: t2_copy(peer, peer).wait_recv())
    for k in range(chunks):
        width = min(128, channels - k * 128)
        kernel_sum[:, k * 128 : k * 128 + width] = tap_all[k % n, k // n][:taps, :width]
    outputs[3].start()

    @pl.when(me < n - 1)
    def _():
        halo_copy.wait_send()

    @pl.when(me > 0)
    def _():
        edge_copy.wait_send()

    for k in range(1, 8):
        factor_copy(k, octet).wait_send()

    def finish_scan(g, c):
        fore_finish(g)
        back_finish(g)
        return c

    lax.fori_loop(0, groups, finish_scan, 0)

    def finish_peer(peer):
        term_copy(peer, me).wait_send()
        t1_copy(peer, me).wait_send()
        t2_copy(peer, me).wait_send()

    others(finish_peer)
    for output in outputs:
        output.wait()


def write_kernel(parts, quartered, *refs):
    sources, targets, held = refs[:parts], refs[parts : 2 * parts], refs[2 * parts : 3 * parts]
    into, out = refs[3 * parts :]
    pieces = []
    for i in range(parts):
        rows = sources[i].shape[0] // 4
        cuts = [pl.ds(k * rows, rows) for k in range(4)] if i < quartered else [slice(None)]
        pieces += [(i, cut) for cut in cuts]
    view = lambda ref, cut: ref.at[cut] if not isinstance(cut, slice) else ref
    reads = [
        pltpu.make_async_copy(view(sources[i], cut), view(held[i], cut), into.at[k])
        for k, (i, cut) in enumerate(pieces)]
    writes = [
        pltpu.make_async_copy(view(held[i], cut), view(targets[i], cut), out.at[k])
        for k, (i, cut) in enumerate(pieces)]
    ahead = 5
    for read in reads[:ahead]:
        read.start()
    for k, (read, write) in enumerate(zip(reads, writes)):
        read.wait()
        write.start()
        if k + ahead < len(reads):
            reads[k + ahead].start()
    for write in writes:
        write.wait()


def body(
    queries,
    key_rows,
    value_rows,
    frame_len,
    log_decay,
    timestep,
    conv_kernel,
    norm_gain,
    mod_table,
    out_grad,
):
    shape = jax.ShapeDtypeStruct
    count, channels = queries.shape
    heads = log_decay.shape[2]
    dim = channels // heads
    taps = conv_kernel.shape[0]
    levels = mod_table.shape[0]
    n = lax.axis_size("seq")
    groups = heads // 4
    padded = -(-channels // 128) * 128
    chunks = padded // 128
    shares = -(-chunks // n)
    head_rows = -(-heads // 8) * 8

    vmem = pl.BlockSpec(memory_space=pltpu.VMEM)
    hbm = pl.BlockSpec(memory_space=pltpu.HBM)
    whole = (channels, count)
    tile = (dim, dim)
    per = lambda *lead, dtype=BF16: pltpu.VMEM(tuple(lead) + tile, dtype)
    table = pltpu.VMEM((head_rows, count), F32)
    dma = lambda *dims: pltpu.SemaphoreType.DMA(dims)
    outs = (
        shape(whole, BF16), shape(whole, BF16), shape(whole, BF16),
        shape((taps, channels), F32), shape((channels,), F32), shape((levels, channels), F32))
    results = pl.pallas_call(
        functools.partial(fused_kernel, n, heads, dim, count, taps, levels),
        out_shape=outs,
        in_specs=[hbm] * 10,
        out_specs=(hbm,) * len(outs),
        scratch_shapes=[
            *(pltpu.VMEM(o.shape, o.dtype) for o in outs),
            pltpu.SMEM(frame_len.shape, jnp.int32), pltpu.SMEM(log_decay.shape, F32), pltpu.SMEM((1,), jnp.int32),
            pltpu.VMEM(conv_kernel.shape, F32), pltpu.VMEM((channels,), F32),
            pltpu.VMEM(whole, BF16), pltpu.VMEM(whole, BF16), pltpu.VMEM(whole, BF16), pltpu.VMEM(whole, BF16),
            pltpu.VMEM((levels, channels), F32),
            pltpu.VMEM(whole, BF16),
            pltpu.VMEM((heads, count, count), BF16),
            pltpu.VMEM(whole, F32), pltpu.VMEM(whole, F32),
            pltpu.VMEM(whole, BF16),
            per(2, groups, 4), per(2, groups, 4), pltpu.VMEM((dim, count), BF16),
            per(2, groups, 4), per(2, groups, 4), per(2, groups), per(2, groups), per(2, groups), per(2, groups),
            per(2, groups, dtype=F32), per(2, groups, dtype=F32), per(2, groups, dtype=F32),
            pltpu.VMEM((8, head_rows, 128), F32),
            table, table, table, table, table, table,
            pltpu.VMEM((32, padded), BF16), pltpu.VMEM((padded, (taps + 1) * 128), F32),
            pltpu.VMEM((channels, 128), BF16),
            pltpu.VMEM((16, channels), BF16), pltpu.VMEM((16, channels), BF16),
            pltpu.VMEM((16, channels), BF16), pltpu.VMEM((16, channels), BF16),
            pltpu.VMEM((channels, 128), BF16), pltpu.VMEM((channels, 128), F32),
            pltpu.VMEM((taps, channels, 256), BF16),
            pltpu.VMEM((1, padded), F32), pltpu.VMEM((n, 1, padded), F32), pltpu.VMEM((n, padded), F32),
            pltpu.VMEM((n, shares, 8, 128), F32), pltpu.VMEM((n, shares, 8, 128), F32),
            pltpu.VMEM((shares, 8, 128), F32), pltpu.VMEM((n, shares, 8, 128), F32),
            dma(10), dma(len(outs)), dma(2), dma(2), dma(8), dma(8), dma(2, groups, 4), dma(2, groups, 4),
            dma(2, groups, 4), dma(2, groups, 4), dma(2, groups), dma(2, groups), dma(2, groups, 2), dma(2, groups),
            dma(n), dma(n),
            dma(n), dma(n), dma(n), dma(n),
        ],
        compiler_params=pltpu.CompilerParams(
            collective_id=0, has_side_effects=True, vmem_limit_bytes=60 << 20),
        name="fused",
    )(
        frame_len, log_decay, timestep, queries.T, key_rows.T, value_rows.T, out_grad.T, mod_table,
        conv_kernel, norm_gain)
    grad_query, grad_key, grad_value, kernel_sum, gain_sum, table_sum = pl.pallas_call(
        functools.partial(write_kernel, len(outs), 3),
        out_shape=outs,
        in_specs=[hbm] * len(outs),
        out_specs=(hbm,) * len(outs),
        scratch_shapes=[*(pltpu.VMEM(o.shape, o.dtype) for o in outs), dma(len(outs) + 9), dma(len(outs) + 9)],
        compiler_params=pltpu.CompilerParams(vmem_limit_bytes=60 << 20),
        name="write",
    )(*results)
    return (grad_query.T, grad_key.T, grad_value.T, kernel_sum, gain_sum, table_sum)


def solution(mesh):
    in_specs = (
        P(("groups", "seq"), None),
        P(("groups", "seq"), None),
        P(("groups", "seq"), None),
        P(("groups", "seq"), None),
        P(("groups", "seq"), None, None),
        P(("groups", "seq")),
        P(),
        P(),
        P(),
        P(("groups", "seq"), None),
    )
    out_specs = (
        P(("groups", "seq"), None),
        P(("groups", "seq"), None),
        P(("groups", "seq"), None),
        P("groups", None),
        P("groups"),
        P("groups", None),
    )
    return jax.shard_map(body, mesh=mesh, in_specs=in_specs, out_specs=out_specs, check_vma=False)
```

```python
import functools

import jax
import jax.numpy as jnp
from jax import lax
from jax.experimental import pallas as pl
from jax.experimental.pallas import tpu as pltpu
from jax.sharding import PartitionSpec as P

EPSILON = 1e-06
MESH = pl.DeviceIdType.MESH
F32, BF16 = jnp.float32, jnp.bfloat16


def mm(a, b, ca, cb):
    return lax.dot_general(a, b, (((ca,), (cb,)), ((), ())), preferred_element_type=F32)


def fused_kernel(
    n, heads, dim, count, taps, levels,
    frame_hbm, decay_hbm, level_hbm, query_hbm, key_hbm, value_hbm, up_hbm, mod_hbm, taps_hbm, gain_hbm,
    query_out, key_out, value_out, kernel_out, gain_out, table_out,
    grad_query, grad_key, grad_value, kernel_sum, gain_sum, table_sum, frame_len, log_decay, timestep, conv_kernel, norm_gain, query, key, value, up, mod, conv, attn, part, key_part, grad, state, local, late_mask,
    gathered, scattered, to_pair, from_pair, to_next, from_next, plane_sum, pair_sum, entering,
    factors, e1_tab, rs_tab, ie_tab, we_tab, sc0_tab, sc1_tab, stack, columns, before,
    halo_out, halo_in, edge_out, edge_in, opening, ending, folds, term_row, terms_all, terms_rows,
    tap_rows, tap_in, tap_own, tap_all,
    load_sem, store_sem, halo_sem, edge_sem, f_send, f_recv, gather_send, gather_recv, scatter_send, scatter_recv,
    pair_send, pair_recv, next_send, next_recv, term_send, term_recv,
    t1_send, t1_recv, t2_send, t2_recv,
):
    groups = heads // 4
    planes = n // 4
    channels = heads * dim
    padded = stack.shape[1]
    chunks = padded // 128
    span = taps - 1
    scale = dim ** (-0.5)
    me = lax.axis_index("seq")
    video = lax.axis_index("groups")
    plane = me // 4
    spot, octet = me % 4, me % 8
    half_octet = octet - spot

    def dev(peer):
        return (video, peer)

    def remote(src, dst, send, recv, peer):
        return pltpu.make_async_remote_copy(
            src_ref=src, dst_ref=dst, send_sem=send, recv_sem=recv, device_id=dev(peer), device_id_type=MESH)

    def others(fn):
        def go(k, c):
            fn(lax.rem(me + k, n))
            return c

        lax.fori_loop(1, n, go, 0)

    barrier = pltpu.get_barrier_semaphore()
    others(lambda peer: pl.semaphore_signal(barrier, inc=1, device_id=dev(peer), device_id_type=MESH))
    loads = [
        pltpu.make_async_copy(src, dst, load_sem.at[i])
        for i, (src, dst) in enumerate(
            ((value_hbm, value), (frame_hbm, frame_len), (decay_hbm, log_decay), (level_hbm, timestep),
             (taps_hbm, conv_kernel), (gain_hbm, norm_gain), (mod_hbm, mod), (key_hbm, key), (query_hbm, query),
             (up_hbm, up)))
    ]
    for load in loads:
        load.start()
    load_value, load_key, load_query, load_up = loads[0], loads[7], loads[8], loads[9]
    small_loads = loads[1:7]
    outputs = [
        pltpu.make_async_copy(src, dst, store_sem.at[i])
        for i, (src, dst) in enumerate(
            ((grad_query, query_out), (grad_key, key_out), (grad_value, value_out), (kernel_sum, kernel_out),
             (gain_sum, gain_out), (table_sum, table_out)))
    ]

    sel_row = lax.broadcasted_iota(jnp.int32, (16, 128), 0)
    sel_lane = lax.broadcasted_iota(jnp.int32, (16, 128), 1)
    sel_last = ((sel_lane == sel_row + 128 - span) & (sel_row < span)).astype(F32).astype(BF16)
    sel_first = ((sel_lane == sel_row) & (sel_row < span)).astype(F32).astype(BF16)

    load_value.wait()
    halo_out[...] = mm(sel_last, value[:, count - 128 :], 1, 1).astype(BF16)

    @pl.when(me == 0)
    def _():
        halo_in[...] = jnp.zeros(halo_in.shape, BF16)

    @pl.when(me == n - 1)
    def _():
        edge_in[...] = jnp.zeros(edge_in.shape, BF16)

    @pl.when(plane < 2)
    def _():
        from_next[0] = jnp.zeros(from_next.shape[1:], BF16)

    @pl.when(plane >= planes - 2)
    def _():
        from_next[1] = jnp.zeros(from_next.shape[1:], BF16)

    pl.semaphore_wait(barrier, n - 1)

    halo_copy = remote(halo_out, halo_in, halo_sem.at[0], halo_sem.at[1], lax.rem(me + 1, n))
    edge_copy = remote(edge_out, edge_in, edge_sem.at[0], edge_sem.at[1], lax.rem(me + n - 1, n))

    @pl.when(me < n - 1)
    def _():
        halo_copy.start()

    for load in small_loads:
        load.wait()
    first = frame_len[0, 0]
    rows = e1_tab.shape[0]
    row_index = lax.broadcasted_iota(jnp.int32, (rows, count), 0)
    late = lax.broadcasted_iota(jnp.int32, (1, count), 1) >= first
    late_rows = lax.broadcasted_iota(jnp.int32, (rows, count), 1) >= first
    cum0 = jnp.zeros((rows, count), F32)
    cum1 = jnp.zeros((rows, count), F32)
    for h in range(heads):
        a = log_decay[0, 0, h]
        b = a + log_decay[0, 1, h]
        cum0 = jnp.where(row_index == h, a, cum0)
        cum1 = jnp.where(row_index == h, b, cum1)
    e1 = jnp.exp(cum1 - cum0)
    from0, from1 = scale * jnp.exp(cum0), scale * jnp.exp(cum1)
    e1_tab[...] = e1
    sc0_tab[...] = from0
    sc1_tab[...] = from1
    rs_tab[...] = jnp.where(late_rows, from1, from0)
    ie_tab[...] = jnp.where(late_rows, 1.0, e1)
    we_tab[...] = scale * jnp.where(late_rows, e1, 1.0)
    factors[octet] = jnp.exp(cum1)[:, :128]
    late_mask[...] = jnp.where(lax.broadcasted_iota(jnp.int32, (dim, count), 1) >= first, 1.0, 0.0).astype(BF16)

    def factor_copy(k, slot):
        peer = me - octet + lax.rem(octet + k, 8)
        return remote(factors.at[octet], factors.at[slot], f_send.at[k], f_recv.at[slot], peer)

    for k in range(1, 8):
        factor_copy(k, octet).start()

    level = timestep[0]
    gain = norm_gain[...][None, :]
    gain_row = gain * (1.0 + mod[pl.ds(level, 1), :])
    table = jnp.concatenate([conv_kernel[...], gain_row, jnp.zeros((8 - taps - 1, channels), F32)], axis=0)
    upper = table.astype(BF16).astype(F32)
    middle = (table - upper).astype(BF16).astype(F32)
    stack[:, 0:channels] = jnp.concatenate(
        [upper, middle, table - upper - middle, jnp.zeros((8, channels), F32)], axis=0).astype(BF16)
    stack[:, channels:] = jnp.zeros((32, padded - channels), BF16)
    row_of = lax.broadcasted_iota(jnp.int32, (32, (taps + 1) * 128), 0)
    tap_of = lax.broadcasted_iota(jnp.int32, (32, (taps + 1) * 128), 1) // 128
    spread = ((row_of % 8 == tap_of) & (row_of < 24)).astype(F32).astype(BF16)

    def spread_columns(k, c):
        at = pl.ds(pl.multiple_of(k * 128, 128), 128)
        columns[at, :] = mm(stack[:, at], spread, 0, 0)
        return c

    def spread_some(k, c):
        for j in range(6):
            spread_columns(k * 6 + j, c)
        return c

    lax.fori_loop(0, chunks // 6, spread_some, 0)
    for k in range(chunks // 6 * 6, chunks):
        spread_columns(k, 0)

    def column(strip, t):
        tile = columns[strip, t * 128 : (t + 1) * 128]
        return jnp.concatenate([tile] * (count // 128), axis=1)

    load_key.wait()
    load_query.wait()

    def lanes(h):
        return pl.ds(pl.multiple_of(h * dim, 16), dim)

    def weigh(product, h):
        rows_of = lax.broadcasted_iota(jnp.int32, (count, count), 0) >= first
        early = we_tab[pl.ds(h, 1), :]
        behind = jnp.where(late, scale, 0.0)
        return (product * jnp.where(rows_of, behind, early)).astype(BF16)

    def attn_work(h):
        c = lanes(h)
        attn[h] = weigh(mm(key[c, :], query[c, :], 0, 0), h)

    def pair(p, fn):
        fn(p * 2, 0)
        fn(p * 2 + 1, 1)

    def pairs(start, stop, fn):
        def go(p, c):
            pair(p, fn)
            return c

        lax.fori_loop(start, stop, go, 0)

    @pl.when(me > 0)
    def _():
        halo_copy.wait_recv()

    for k in range(1, 8):
        factor_copy(k, lax.rem(octet + k, 8)).wait_recv()
    before[...] = mm(halo_in[...], sel_last, 0, 0).astype(BF16)

    step = dim

    def strips(h):
        for r in range(0, dim, step):
            yield r, pl.ds(pl.multiple_of(h * dim + r, 16), step)

    def split_late(rows):
        second = rows * late_mask[...]
        return jnp.concatenate([rows - second, second], axis=0)

    def conv_work(g, i, h, j):
        c = lanes(h)
        for _, strip in strips(h):
            x = value[strip, :]
            joined = jnp.concatenate([before[strip, :], x], axis=1)
            total = column(strip, 0) * x.astype(F32)
            for t in range(1, taps):
                total = total + column(strip, t) * pltpu.roll(joined, t, 1)[:, 128:].astype(F32)
            conv[strip, :] = total.astype(BF16)
        outer = mm(split_late(conv[c, :]), key[c, :], 1, 1)
        local[0, g, 2 * i + j] = (e1_tab[pl.ds(h, 1), :][:, :dim] * outer[:dim] + outer[dim:]).astype(BF16)

    def part_work(h):
        c = lanes(h)
        part[c, :] = mm(conv[c, :], attn[h], 1, 0)

    def fold(t, strip, rows):
        total = sum(rows[:, k * 128 : (k + 1) * 128] for k in range(count // 128))
        upper = total.astype(BF16)
        folds[t, strip, 0:128] = upper
        folds[t, strip, 128:256] = (total - upper.astype(F32)).astype(BF16)

    def fold_sums(row, t):
        ones = (lax.broadcasted_iota(jnp.int32, (8, 256), 0) == row).astype(F32).astype(BF16)
        return mm(ones, folds[t], 1, 1)

    def norm_work(g, i, h, j):
        c = lanes(h)
        q = query[c, :]
        inter = mm(state[0, g, 2 * i + j], q, 1, 0)
        row_scale = rs_tab[pl.ds(h, 1), :]
        square = jnp.zeros((step, count), F32)
        cross = jnp.zeros((step, count), F32)
        for r, strip in strips(h):
            numerator = part[strip, :] + row_scale * inter[r : r + step]
            part[strip, :] = numerator
            square = square + numerator * numerator
            cross = cross + numerator * (up[strip, :].astype(F32) * column(strip, taps))
        square = jnp.sum(square, axis=0, keepdims=True) * (1.0 / dim)
        cross = jnp.sum(cross, axis=0, keepdims=True) * (1.0 / dim)
        inv_rms = lax.rsqrt(square + EPSILON)
        pull = inv_rms * (inv_rms * (inv_rms * cross))
        for _, strip in strips(h):
            numerator = part[strip, :]
            upstream = up[strip, :].astype(F32)
            terms = upstream * (numerator * inv_rms)
            fold(0, strip, terms)
            normed_grad = upstream * column(strip, taps)
            grad[strip, :] = (inv_rms * normed_grad - pull * numerator).astype(BF16)
        outer = mm(split_late(grad[c, :]), q, 1, 1)
        local[1, g, 2 * i + j] = (
            sc0_tab[pl.ds(h, 1), :][:, :dim] * outer[:dim] + sc1_tab[pl.ds(h, 1), :][:, :dim] * outer[dim:]
        ).astype(BF16)

    def back_work(g, i, h, j):
        c = lanes(h)
        q, k, gr = query[c, :], key[c, :], grad[c, :]
        score = weigh(mm(conv[c, :], gr, 0, 0), h)
        grad_query[c, :] = (
            mm(k, score, 1, 0) + rs_tab[pl.ds(h, 1), :] * mm(state[0, g, 2 * i + j], gr, 0, 0)
        ).astype(BF16)
        key_part[c, :] = mm(q, score, 1, 1)


    def carry_work(g, i, h, j):
        c = lanes(h)
        part[c, :] = mm(grad[c, :], attn[h], 1, 1)

    token = lax.broadcasted_iota(jnp.int32, (1, 128), 1)

    def value_work(g, i, h, j):
        c = lanes(h)
        inter = mm(state[1, g, 2 * i + j], key[c, :], 1, 0)
        into_end = ie_tab[pl.ds(h, 1), :]
        for r, strip in strips(h):
            own = part[strip, :] + into_end * inter[r : r + step]
            rounded = own.astype(BF16)
            opening[strip, :] = rounded[:, :128]
            x = value[strip, :].astype(F32)
            prior = before[strip, :]
            total = column(strip, 0) * own
            fold(0, strip, own * x)
            for t in range(1, taps):
                ahead = pltpu.roll(rounded, count - t, 1).astype(F32)
                ahead = jnp.concatenate(
                    [ahead[:, : count - 128], jnp.where(token < 128 - t, ahead[:, count - 128 :], 0.0)], axis=1)
                total = total + column(strip, t) * ahead
                edge = own[:, :128] * jnp.where(token < t, pltpu.roll(prior, t, 1).astype(F32), 0.0)
                product = ahead * x
                fold(t, strip, jnp.concatenate([product[:, :128] + edge, product[:, 128:]], axis=1))
            grad_value[strip, :] = total.astype(BF16)
            ending[strip, :] = total[:, count - 128 :]

    def key_work(g, i, h, j):
        c = lanes(h)
        grad_key[c, :] = (
            key_part[c, :] + ie_tab[pl.ds(h, 1), :] * mm(state[1, g, 2 * i + j], conv[c, :], 0, 0)
        ).astype(BF16)

    def group_work(g, fn):
        for i in range(2):
            for j in range(2):
                fn(g, i, 4 * g + 2 * i + j, j)

    def factor(slot, h):
        return factors[slot, pl.ds(h, 1), :][:, :dim]

    def scan_steps(rev):
        at = plane if rev == 0 else planes - 1 - plane
        odd = at % 2
        order = range(4) if rev == 0 else range(3, -1, -1)
        stride = 4 if rev == 0 else -4
        peer_of = lambda k: me - spot + lax.rem(spot + k, 4)
        slot_of = lambda k: lax.rem(spot + k, 4)

        def gather_copy(g, k, slot):
            return remote(
                local.at[rev, g, slot_of(k)], gathered.at[rev, g, slot],
                gather_send.at[rev, g, k], gather_recv.at[rev, g, slot], peer_of(k))

        def scatter_copy(g, k, slot):
            return remote(
                scattered.at[rev, g, slot_of(k)], state.at[rev, g, slot],
                scatter_send.at[rev, g, k], scatter_recv.at[rev, g, slot], peer_of(k))

        def reach(hops):
            return jnp.clip(me + hops * stride, 0, n - 1)

        def pair_copy(g):
            return remote(
                to_pair.at[rev, g], from_pair.at[rev, g], pair_send.at[rev, g], pair_recv.at[rev, g], reach(1))

        def next_copy(g, hops):
            return remote(
                to_next.at[rev, g], from_next.at[rev, g], next_send.at[rev, g, hops - 1], next_recv.at[rev, g],
                reach(hops))

        def plane_factor(first, h):
            return (factor(first, h) * factor(first + 1, h)) * (factor(first + 2, h) * factor(first + 3, h))

        def onward(g, value):
            to_next[rev, g] = value.astype(BF16)
            for hops in (1, 2):
                @pl.when(at + hops < planes)
                def _():
                    next_copy(g, hops).start()

        def h0(g):
            for k in (2, 3, 1):
                gather_copy(g, k, spot).start()

        def h1(g):
            gathered[rev, g, spot] = local[rev, g, spot]
            for k in range(1, 4):
                gather_copy(g, k, slot_of(k)).wait_recv()
            h = 4 * g + spot
            total = None
            for p in order:
                x = gathered[rev, g, p].astype(F32)
                total = x if total is None else factor(half_octet + p, h) * total + x
            plane_sum[rev, g] = total

            @pl.when(odd == 0)
            def _():
                to_pair[rev, g] = total.astype(BF16)
                pair_copy(g).start()

        def h2(g):
            @pl.when(odd == 1)
            def _():
                pair_copy(g).wait_recv()
                h = 4 * g + spot
                total = plane_factor(half_octet, h) * from_pair[rev, g].astype(F32) + plane_sum[rev, g]
                pair_sum[rev, g] = total

                @pl.when(at == 1)
                def _():
                    onward(g, total)

        def h3(g):
            @pl.when(at >= 2)
            def _():
                next_copy(g, 1).wait_recv()

            h = 4 * g + spot

            @pl.when(odd == 1)
            def _():
                mine, prior = plane_factor(half_octet, h), plane_factor(4 - half_octet, h)
                start = from_next[rev, g].astype(F32)

                @pl.when(at >= 3)
                def _():
                    onward(g, mine * prior * start + pair_sum[rev, g])

                entering[rev, g] = prior * start + from_pair[rev, g].astype(F32)

            @pl.when(odd == 0)
            def _():
                entering[rev, g] = from_next[rev, g].astype(F32)

            total = entering[rev, g]
            for i, p in enumerate(order):
                scattered[rev, g, p] = total.astype(BF16)
                if i < 3:
                    total = factor(half_octet + p, h) * total + gathered[rev, g, p].astype(F32)
            for k in (2, 3, 1):
                scatter_copy(g, k, spot).start()
            state[rev, g, spot] = scattered[rev, g, spot]

        def h5(g):
            for k in range(1, 4):
                scatter_copy(g, k, slot_of(k)).wait_recv()

        def finish(g):
            for k in range(1, 4):
                gather_copy(g, k, spot).wait_send()
                scatter_copy(g, k, spot).wait_send()

            @pl.when(odd == 0)
            def _():
                pair_copy(g).wait_send()

            @pl.when(odd == 1)
            def _():
                for hops in (1, 2):
                    @pl.when(at + hops < planes)
                    def _():
                        next_copy(g, hops).wait_send()

        wait = jnp.where(odd == 1, 2 + 3 * (at // 2), jnp.where(at == 0, 0, 3 * (at // 2) + 1))
        return 4 + wait, (h0, h1, h2, h3, h5), finish

    fore_at, fore, fore_finish = scan_steps(0)
    back_at, back, back_finish = scan_steps(1)

    half = heads // 2
    depth = 5 + 3 * (planes // 2 - 1)
    norm_base = max(depth + 7, 2 * groups + 1)
    carry_base = norm_base + groups
    value_base = max(carry_base + groups, norm_base + depth + 5)
    ticks = value_base + groups

    def stage_back(p):
        pair(p, lambda h, j: back_work(p // 2, p % 2, h, j))

    def tick(i, carry):
        def at_tick(start, fn, stop=groups):
            g = i - start

            @pl.when((g >= 0) & (g < stop))
            def _():
                fn(g)

        at_tick(5, fore[1])
        at_tick(7, fore[2])
        at_tick(fore_at + 1, fore[3])
        at_tick(norm_base, fore[4])
        at_tick(norm_base + 3, back[1])
        at_tick(norm_base + 5, back[2])
        at_tick(norm_base + back_at - 1, back[3])
        at_tick(value_base, back[4])

        def stage_conv(g):
            group_work(g, conv_work)
            fore[0](g)

        def stage_part(g):
            for i in range(4):
                attn_work(4 * g + i)
            for i in range(4):
                part_work(4 * g + i)

        def stage_norm(g):
            group_work(g, norm_work)
            back[0](g)

        def stage_carry(g):
            group_work(g, carry_work)
            stage_back(g)

        def stage_value(g):
            group_work(g, value_work)

        at_tick(0, stage_conv)
        at_tick(groups, stage_part)

        @pl.when(i == norm_base)
        def _():
            load_up.wait()

        at_tick(norm_base, stage_norm)

        @pl.when(i == value_base)
        def _():
            send_terms()

        at_tick(carry_base, stage_carry)
        at_tick(value_base, stage_value)
        return carry

    def term_copy(peer, slot):
        return remote(term_row, terms_all.at[slot], term_send.at[peer], term_recv.at[slot], peer)

    def send_terms():
        row = fold_sums(0, 0)[0:1, :]
        last = (chunks - 1) * 128
        term_row[:, :last] = row[:, :last]
        term_row[:, last:] = jnp.concatenate(
            [row[:, last:], jnp.full((1, padded - channels), level.astype(F32))], axis=1)
        terms_all[me] = term_row[...]
        others(lambda peer: term_copy(peer, me).start())

    lax.fori_loop(0, ticks, tick, 0)

    def t1_copy(peer, slot):
        return remote(tap_rows.at[peer], tap_in.at[slot], t1_send.at[peer], t1_recv.at[slot], peer)

    def t2_copy(peer, slot):
        return remote(tap_own, tap_all.at[slot], t2_send.at[peer], t2_recv.at[slot], peer)

    shares = tap_rows.shape[1]
    tap_rows[...] = jnp.zeros(tap_rows.shape, F32)
    tap_sums = sum(fold_sums(t, t) for t in range(taps))
    for k in range(chunks):
        width = min(128, channels - k * 128)
        tap_rows[k % n, k // n, :, :width] = tap_sums[:, k * 128 : k * 128 + width]
    tap_in[me] = tap_rows[me]
    others(lambda peer: t1_copy(peer, me).start())
    edge_out[...] = mm(sel_first, opening[...], 1, 1).astype(BF16)

    @pl.when(me > 0)
    def _():
        edge_copy.start()

    def key_groups(start, stop):
        def go(g, c):
            group_work(g, key_work)
            return c

        lax.fori_loop(start, stop, go, 0)

    middle_back = (groups + half + 1) // 2
    for p in range(groups, middle_back):
        stage_back(p)
    others(lambda peer: t1_copy(peer, peer).wait_recv())
    tap_own[...] = jnp.sum(tap_in[...], axis=0) * (1.0 / n)
    tap_all[me] = tap_own[...]
    others(lambda peer: t2_copy(peer, me).start())
    for p in range(middle_back, half):
        stage_back(p)
    outputs[0].start()
    key_groups(0, groups)
    outputs[1].start()

    others(lambda peer: term_copy(peer, peer).wait_recv())

    def gather_row(b, c):
        terms_rows[pl.ds(b, 1), :] = terms_all[b]
        return c

    lax.fori_loop(0, n, gather_row, 0)
    wanted = terms_rows[:, channels : channels + 1]
    level_lane = lax.broadcasted_iota(jnp.int32, (n, 64), 1).astype(F32)
    chosen = jnp.where(level_lane == wanted, 1.0, 0.0)
    sums = lax.dot_general(
        chosen, terms_rows[:, :channels], (((0,), (0,)), ((), ())), precision=lax.Precision.HIGHEST,
        preferred_element_type=F32)[:levels]
    gain_sum[...] = (jnp.sum(sums * (1.0 + mod[...]), axis=0, keepdims=True) * (1.0 / n))[0]
    table_sum[...] = sums * gain * (1.0 / n)
    outputs[4].start()
    outputs[5].start()

    @pl.when(me < n - 1)
    def _():
        edge_copy.wait_recv()

    fix_row = lax.broadcasted_iota(jnp.int32, (16, span * 128), 0)
    fix_lane = lax.broadcasted_iota(jnp.int32, (16, span * 128), 1)
    ahead_by = fix_lane // 128 + 1
    sel_fix = ((fix_lane % 128 == 128 - ahead_by + fix_row) & (fix_row < ahead_by)).astype(F32).astype(BF16)
    key_part[:, 0 : span * 128] = mm(edge_in[...], sel_fix, 0, 0)

    def fix_work(h, j):
        c = lanes(h)
        tile = ending[c, :]
        for t in range(1, taps):
            tile = tile + columns[c, t * 128 : (t + 1) * 128] * key_part[c, (t - 1) * 128 : t * 128]
        grad_value[c, count - 128 :] = tile.astype(BF16)

    pairs(0, half, fix_work)
    outputs[2].start()

    others(lambda peer: t2_copy(peer, peer).wait_recv())
    for k in range(chunks):
        width = min(128, channels - k * 128)
        kernel_sum[:, k * 128 : k * 128 + width] = tap_all[k % n, k // n][:taps, :width]
    outputs[3].start()

    @pl.when(me < n - 1)
    def _():
        halo_copy.wait_send()

    @pl.when(me > 0)
    def _():
        edge_copy.wait_send()

    for k in range(1, 8):
        factor_copy(k, octet).wait_send()

    def finish_scan(g, c):
        fore_finish(g)
        back_finish(g)
        return c

    lax.fori_loop(0, groups, finish_scan, 0)

    def finish_peer(peer):
        term_copy(peer, me).wait_send()
        t1_copy(peer, me).wait_send()
        t2_copy(peer, me).wait_send()

    others(finish_peer)
    for output in outputs:
        output.wait()


def write_kernel(parts, halves, *refs):
    sources, targets, held = refs[:parts], refs[parts : 2 * parts], refs[2 * parts : 3 * parts]
    into, out = refs[3 * parts :]
    pieces = []
    for i in range(parts):
        rows = sources[i].shape[0] // 2
        cuts = [pl.ds(0, rows), pl.ds(rows, rows)] if i < halves else [slice(None)]
        pieces += [(i, cut) for cut in cuts]
    view = lambda ref, cut: ref.at[cut] if not isinstance(cut, slice) else ref
    reads = [
        pltpu.make_async_copy(view(sources[i], cut), view(held[i], cut), into.at[k])
        for k, (i, cut) in enumerate(pieces)]
    writes = [
        pltpu.make_async_copy(view(held[i], cut), view(targets[i], cut), out.at[k])
        for k, (i, cut) in enumerate(pieces)]
    for read in reads:
        read.start()
    for read, write in zip(reads, writes):
        read.wait()
        write.start()
    for write in writes:
        write.wait()


def body(
    queries,
    key_rows,
    value_rows,
    frame_len,
    log_decay,
    timestep,
    conv_kernel,
    norm_gain,
    mod_table,
    out_grad,
):
    shape = jax.ShapeDtypeStruct
    count, channels = queries.shape
    heads = log_decay.shape[2]
    dim = channels // heads
    taps = conv_kernel.shape[0]
    levels = mod_table.shape[0]
    n = lax.axis_size("seq")
    groups = heads // 4
    padded = -(-channels // 128) * 128
    chunks = padded // 128
    shares = -(-chunks // n)
    head_rows = -(-heads // 8) * 8

    vmem = pl.BlockSpec(memory_space=pltpu.VMEM)
    hbm = pl.BlockSpec(memory_space=pltpu.HBM)
    whole = (channels, count)
    tile = (dim, dim)
    per = lambda *lead, dtype=BF16: pltpu.VMEM(tuple(lead) + tile, dtype)
    table = pltpu.VMEM((head_rows, count), F32)
    dma = lambda *dims: pltpu.SemaphoreType.DMA(dims)
    outs = (
        shape(whole, BF16), shape(whole, BF16), shape(whole, BF16),
        shape((taps, channels), F32), shape((channels,), F32), shape((levels, channels), F32))
    results = pl.pallas_call(
        functools.partial(fused_kernel, n, heads, dim, count, taps, levels),
        out_shape=outs,
        in_specs=[hbm] * 10,
        out_specs=(hbm,) * len(outs),
        scratch_shapes=[
            *(pltpu.VMEM(o.shape, o.dtype) for o in outs),
            pltpu.SMEM(frame_len.shape, jnp.int32), pltpu.SMEM(log_decay.shape, F32), pltpu.SMEM((1,), jnp.int32),
            pltpu.VMEM(conv_kernel.shape, F32), pltpu.VMEM((channels,), F32),
            pltpu.VMEM(whole, BF16), pltpu.VMEM(whole, BF16), pltpu.VMEM(whole, BF16), pltpu.VMEM(whole, BF16),
            pltpu.VMEM((levels, channels), F32),
            pltpu.VMEM(whole, BF16),
            pltpu.VMEM((heads, count, count), BF16),
            pltpu.VMEM(whole, F32), pltpu.VMEM(whole, F32),
            pltpu.VMEM(whole, BF16),
            per(2, groups, 4), per(2, groups, 4), pltpu.VMEM((dim, count), BF16),
            per(2, groups, 4), per(2, groups, 4), per(2, groups), per(2, groups), per(2, groups), per(2, groups),
            per(2, groups, dtype=F32), per(2, groups, dtype=F32), per(2, groups, dtype=F32),
            pltpu.VMEM((8, head_rows, 128), F32),
            table, table, table, table, table, table,
            pltpu.VMEM((32, padded), BF16), pltpu.VMEM((padded, (taps + 1) * 128), F32),
            pltpu.VMEM((channels, 128), BF16),
            pltpu.VMEM((16, channels), BF16), pltpu.VMEM((16, channels), BF16),
            pltpu.VMEM((16, channels), BF16), pltpu.VMEM((16, channels), BF16),
            pltpu.VMEM((channels, 128), BF16), pltpu.VMEM((channels, 128), F32),
            pltpu.VMEM((taps, channels, 256), BF16),
            pltpu.VMEM((1, padded), F32), pltpu.VMEM((n, 1, padded), F32), pltpu.VMEM((n, padded), F32),
            pltpu.VMEM((n, shares, 8, 128), F32), pltpu.VMEM((n, shares, 8, 128), F32),
            pltpu.VMEM((shares, 8, 128), F32), pltpu.VMEM((n, shares, 8, 128), F32),
            dma(10), dma(len(outs)), dma(2), dma(2), dma(8), dma(8), dma(2, groups, 4), dma(2, groups, 4),
            dma(2, groups, 4), dma(2, groups, 4), dma(2, groups), dma(2, groups), dma(2, groups, 2), dma(2, groups),
            dma(n), dma(n),
            dma(n), dma(n), dma(n), dma(n),
        ],
        compiler_params=pltpu.CompilerParams(
            collective_id=0, has_side_effects=True, vmem_limit_bytes=60 << 20),
        name="fused",
    )(
        frame_len, log_decay, timestep, queries.T, key_rows.T, value_rows.T, out_grad.T, mod_table,
        conv_kernel, norm_gain)
    grad_query, grad_key, grad_value, kernel_sum, gain_sum, table_sum = pl.pallas_call(
        functools.partial(write_kernel, len(outs), 3),
        out_shape=outs,
        in_specs=[hbm] * len(outs),
        out_specs=(hbm,) * len(outs),
        scratch_shapes=[*(pltpu.VMEM(o.shape, o.dtype) for o in outs), dma(len(outs) + 3), dma(len(outs) + 3)],
        compiler_params=pltpu.CompilerParams(vmem_limit_bytes=60 << 20),
        name="write",
    )(*results)
    return (grad_query.T, grad_key.T, grad_value.T, kernel_sum, gain_sum, table_sum)


def solution(mesh):
    in_specs = (
        P(("groups", "seq"), None),
        P(("groups", "seq"), None),
        P(("groups", "seq"), None),
        P(("groups", "seq"), None),
        P(("groups", "seq"), None, None),
        P(("groups", "seq")),
        P(),
        P(),
        P(),
        P(("groups", "seq"), None),
    )
    out_specs = (
        P(("groups", "seq"), None),
        P(("groups", "seq"), None),
        P(("groups", "seq"), None),
        P("groups", None),
        P("groups"),
        P("groups", None),
    )
    return jax.shard_map(body, mesh=mesh, in_specs=in_specs, out_specs=out_specs, check_vma=False)
```
